512 devices in a mesh: slab: 128 (over y, z, core), sub: 4 (over x).
Axes of the slice: x: 4, y: 4, z: 16, core: 2. Of those that a mesh axis runs over, the one named last changes fastest.
Arguments:
- right_side: float32 [4, 524288], P(None, ('slab', 'sub')), may hold values from -6 to 6
- warm_start: float32 [4, 524288], P(None, ('slab', 'sub')), may hold values from -6 to 6
- fine_blocks: float32 [8192, 3, 4096], P(('slab', 'sub')), may hold values from -0.6 to 1.25, as said below
- fine_columns: int32 [8192, 3], P(('slab', 'sub')), may hold values from 0 to 8191, as said below
- fine_prolong: float32 [8192, 2, 4096], P(('slab', 'sub')), may hold values from -0.1875 to 0.1875
- owner_rows: int32 [8192, 2], P(('slab', 'sub')), may hold values from 0 to 1023, as said below
- send_slots: int32 [8192, 2], P(('slab', 'sub')), may hold values from 0 to 1, as said below
- receive_rows: int32 [128, 4, 128, 2], P('slab', 'sub'), may hold values from -1 to 7, as said below
- middle_blocks: float32 [1024, 3, 4096], P('slab'), may hold values from -0.6 to 1.25, as said below
- middle_columns: int32 [1024, 3], P('slab'), may hold values from 0 to 1023, as said below
- middle_prolong: float32 [1024, 4096], P('slab'), may hold values from -0.375 to 0.375
- coarse_blocks: float32 [256, 3, 4096], P('slab'), may hold values from -0.6 to 1.25, as said below
- coarse_columns: int32 [256, 3], P('slab'), may hold values from 0 to 255, as said below
Outputs:
- solution: float32 [4, 524288], P(None, ('slab', 'sub'))
- residual: float32 [4, 524288], P(None, ('slab', 'sub'))
The draws below stay inside these ranges and needn't reach their ends.
Inputs may be any that keep to these rules, and one draw needn't show every extreme that they name: `fine_columns`: column 0 of each row is the row itself; every other column lies within 8 rows of it, inside the level. `middle_columns`: column 0 of each row is the row itself; every other column lies within 2 rows of it, inside the level. `coarse_columns`: column 0 of each row is the row itself; every other column lies within 1 row of it, inside the level. The owner of a block is owner_rows // 8; receive_rows[o, u, s, c] equals owner_rows % 8 of the block of device s * 4 + u that sits in slot c for owner o. `send_slots`: the blocks of one device occupy distinct pairs (owner, slot); one owner gets all 2 slots from every device. `receive_rows`: -1 marks a slot that no block of that device fills. `fine_blocks`: the diagonal entries of slot 0's block lie in 0.8 to 1.25. `middle_blocks`: the diagonal entries of slot 0's block lie in 0.8 to 1.25. `coarse_blocks`: the diagonal entries of slot 0's block lie in 0.8 to 1.25.
All inputs are finite; a program needn't handle non-finite values.
Results may differ from the reference program's by a relative error of at most 0.0003.
Values sent between devices are 32-bit elements; how exact they have to be, the bound alone decides.
No kernel may reach another device: no remote copies, remote signals or barrier semaphores. Data moves between devices by JAX's collectives and lax.ppermute only.
A program may use at most 64 MiB of HBM per device.

```python
import jax
import jax.numpy as jnp
from jax import lax

BS = 64
R0 = 16
R1 = 8
R2 = 2
K0 = 3
K1 = 3
K2 = 3
H0 = 8
H1 = 2
H2 = 1
NRHS = 4
DEG0 = 3
DEG1 = 3
DEG2 = 4
CAP = 2
N0 = 8192
N1 = 1024
N2 = 256
N_SLAB = 128
N_SUB = 4
DEVICES = 512


def block_values(key, row_count, slot_count):
    noise_key, diagonal_key, couple_key = jax.random.split(key, 3)
    noise_part = jax.random.truncated_normal(noise_key, -4.0, 4.0, (row_count, slot_count, BS, BS), jnp.float32) * 0.025
    diagonal = jax.random.uniform(diagonal_key, (row_count, 1, BS), jnp.float32, 0.8, 1.25)
    coupling = jax.random.uniform(couple_key, (row_count, slot_count, 1, 1), jnp.float32, 0.2, 0.45)
    identity = jnp.eye(BS, dtype=jnp.float32)
    first_slot = (jnp.arange(slot_count) == 0)[None, :, None, None]
    diagonal_block = noise_part * (1.0 - identity) + identity * diagonal[:, :, :, None]
    other_block = noise_part - coupling * identity
    blocks = jnp.where(first_slot, diagonal_block, other_block)
    return blocks.reshape(row_count, slot_count, BS * BS)


def band_columns(key, row_count, slot_count, rim_rows):
    sign_key, step_key = jax.random.split(key)
    step_sizes = jax.random.randint(step_key, (row_count, slot_count), 1, rim_rows + 1)
    sign_values = jnp.where(jax.random.randint(sign_key, (row_count, slot_count), 0, 2) == 0, -1, 1)
    row_index = jnp.arange(row_count, dtype=jnp.int32)[:, None]
    forward = row_index + sign_values * step_sizes
    reflected = row_index - sign_values * step_sizes
    inside = (forward >= 0) & (forward < row_count)
    picked = jnp.where(inside, forward, reflected)
    first_slot = jnp.arange(slot_count)[None, :] == 0
    return jnp.where(first_slot, row_index, picked).astype(jnp.int32)


def routing(key):
    slot_total = N_SLAB * CAP
    piece_count = 2 * R0
    full_owner = jax.random.randint(jax.random.fold_in(key, 101), (), 0, N_SLAB)
    device_keys = jax.random.split(jax.random.fold_in(key, 202), DEVICES)

    def one_device(device_key):
        order_key, shuffle_key, row_key = jax.random.split(device_key, 3)
        priority = jax.random.permutation(order_key, slot_total).astype(jnp.int32)
        owner_index = jnp.arange(slot_total, dtype=jnp.int32) // CAP
        priority = jnp.where(owner_index == full_owner, priority - slot_total, priority)
        chosen = jnp.argsort(priority)[:piece_count].astype(jnp.int32)
        chosen = jax.random.permutation(shuffle_key, chosen)
        local_rows = jax.random.randint(row_key, (piece_count,), 0, R1).astype(jnp.int32)
        return (chosen, local_rows)
    chosen, local_rows = jax.vmap(one_device)(device_keys)
    owner_rows = chosen // CAP * R1 + local_rows
    slot_values = chosen % CAP
    slot_table = jnp.full((DEVICES, slot_total), -1, jnp.int32)
    slot_table = slot_table.at[jnp.arange(DEVICES, dtype=jnp.int32)[:, None], chosen].set(local_rows)
    slot_table = slot_table.reshape(N_SLAB, N_SUB, N_SLAB, CAP).transpose(2, 1, 0, 3)
    return (owner_rows.reshape(N0, 2).astype(jnp.int32), slot_values.reshape(N0, 2).astype(jnp.int32), slot_table)


def draw_fine_blocks(key, part):
    return block_values(key, N0, K0)


def draw_middle_blocks(key, part):
    return block_values(key, N1, K1)


def draw_coarse_blocks(key, part):
    return block_values(key, N2, K2)


def draw_fine_columns(key, part):
    return band_columns(key, N0, K0, H0)


def draw_middle_columns(key, part):
    return band_columns(key, N1, K1, H1)


def draw_coarse_columns(key, part):
    return band_columns(key, N2, K2, H2)


def draw_owner_rows(key, part):
    return routing(key)[0]


def draw_send_slots(key, part):
    return routing(key)[1]


def draw_receive_rows(key, part):
    return routing(key)[2]


def steps_of(key, dims, cuts, low, top_value):
    gain, own = 1.0, jax.random.fold_in(key, 6)
    for axis_at, shards_of in cuts:
        steps = jnp.exp(jax.random.uniform(jax.random.fold_in(own, axis_at), (shards_of,), jnp.float32, low / len(cuts), top_value / len(cuts)))
        gain = gain * jnp.repeat(steps, dims[axis_at] // shards_of).reshape([-1 if axis == axis_at else 1 for axis in range(len(dims))])
    return gain


def gaussian(rng, shape, deviation, limit, cuts=(), kind=jnp.bfloat16):
    entries = deviation * jax.random.normal(rng, shape, jnp.float32)
    if cuts:
        entries = entries * steps_of(rng, shape, cuts, -0.22, 0.18)
    return jnp.clip(entries, -limit, limit).astype(kind)


def setup_inputs(seed: int = 0) -> dict:
    keys = jax.random.split(jax.random.key(seed), 14)
    return {
        "right_side": gaussian(keys[0], (NRHS, N0 * BS), 1.0, 6.0, ((1, 512),), jnp.float32),
        "warm_start": gaussian(keys[1], (NRHS, N0 * BS), 1.0, 6.0, ((1, 512),), jnp.float32),
        "fine_blocks": draw_fine_blocks(jax.random.fold_in(keys[13], 71), 0),
        "fine_columns": draw_fine_columns(jax.random.fold_in(keys[13], 71), 0),
        "fine_prolong": gaussian(keys[4], (N0, 2, BS * BS), (BS * (2 * R0 * N_SUB // R1)) ** -0.5, 0.1875, ((0, 512),), jnp.float32),
        "owner_rows": draw_owner_rows(jax.random.fold_in(keys[13], 71), 0),
        "send_slots": draw_send_slots(jax.random.fold_in(keys[13], 71), 0),
        "receive_rows": draw_receive_rows(jax.random.fold_in(keys[13], 71), 0),
        "middle_blocks": draw_middle_blocks(jax.random.fold_in(keys[13], 71), 0),
        "middle_columns": draw_middle_columns(jax.random.fold_in(keys[13], 71), 0),
        "middle_prolong": gaussian(keys[10], (N1, BS * BS), (BS * (R1 // R2)) ** -0.5, 0.375, ((0, 128),), jnp.float32),
        "coarse_blocks": draw_coarse_blocks(jax.random.fold_in(keys[13], 71), 0),
        "coarse_columns": draw_coarse_columns(jax.random.fold_in(keys[13], 71), 0),
    }


LOWER_EDGE = 0.3
UPPER_EDGE = 2.2


def apply_blocks(blocks, columns, values):
    row_count, slot_count = columns.shape
    matrices = blocks.reshape(row_count, slot_count, BS, BS)
    picked = values[:, columns]
    return jnp.einsum("ikab,rikb->ria", matrices, picked, precision=lax.Precision.HIGHEST)


def inverse_diagonal(blocks, columns):
    row_count, slot_count = columns.shape
    matrices = blocks.reshape(row_count, slot_count, BS, BS)
    return 1.0 / jnp.diagonal(matrices[:, 0], axis1=1, axis2=2)


def chebyshev(operate, inverse, solution, residual, degree, need_residual):
    center = 0.5 * (UPPER_EDGE + LOWER_EDGE)
    half_width = 0.5 * (UPPER_EDGE - LOWER_EDGE)
    scaled = center / half_width
    factor = 1.0 / scaled
    direction = inverse * residual / center
    for iteration in range(degree):
        solution = solution + direction
        if iteration < degree - 1 or need_residual:
            residual = residual - operate(direction)
        if iteration < degree - 1:
            factor_next = 1.0 / (2.0 * scaled - factor)
            direction = (factor_next * factor) * direction + (2.0 * factor_next / half_width) * (inverse * residual)
            factor = factor_next
    return solution, residual


def reference(right_side, warm_start, fine_blocks, fine_columns, fine_prolong, owner_rows, send_slots, receive_rows, middle_blocks, middle_columns, middle_prolong, coarse_blocks, coarse_columns):
    count_fine = fine_columns.shape[0]
    count_middle = middle_columns.shape[0]
    ratio_rows = R1 // R2
    target = right_side.reshape(NRHS, count_fine, BS)
    solution = warm_start.reshape(NRHS, count_fine, BS)

    def fine_apply(values):
        return apply_blocks(fine_blocks, fine_columns, values)

    def middle_apply(values):
        return apply_blocks(middle_blocks, middle_columns, values)

    def coarse_apply(values):
        return apply_blocks(coarse_blocks, coarse_columns, values)

    fine_inverse = inverse_diagonal(fine_blocks, fine_columns)
    middle_inverse = inverse_diagonal(middle_blocks, middle_columns)
    coarse_inverse = inverse_diagonal(coarse_blocks, coarse_columns)

    residual = target - fine_apply(solution)
    solution, residual = chebyshev(fine_apply, fine_inverse, solution, residual, DEG0, True)

    device_index = (jnp.arange(count_fine) // R0).astype(jnp.int32)
    slab_index = (device_index // N_SUB)[:, None]
    sub_index = (device_index % N_SUB)[:, None]
    owner_index = owner_rows // R1
    row_index = owner_index * R1 + receive_rows[owner_index, sub_index, slab_index, send_slots]

    prolong = fine_prolong.reshape(count_fine, 2, BS, BS)
    pieces = jnp.einsum("ieab,ria->rieb", prolong, residual, precision=lax.Precision.HIGHEST)
    middle_rhs = jnp.zeros((NRHS, count_middle, BS), jnp.float32).at[:, row_index].add(pieces)

    middle_zero = jnp.zeros((NRHS, count_middle, BS), jnp.float32)
    middle_solution, middle_residual = chebyshev(middle_apply, middle_inverse, middle_zero, middle_rhs, DEG1, True)
    middle_mats = middle_prolong.reshape(count_middle, BS, BS)
    lifted = jnp.einsum("iab,ria->rib", middle_mats, middle_residual, precision=lax.Precision.HIGHEST)
    coarse_rhs = lifted.reshape(NRHS, count_middle // ratio_rows, ratio_rows, BS).sum(axis=2)
    coarse_zero = jnp.zeros_like(coarse_rhs)
    coarse_solution, unused = chebyshev(coarse_apply, coarse_inverse, coarse_zero, coarse_rhs, DEG2, False)

    spread = jnp.repeat(coarse_solution, ratio_rows, axis=1)
    middle_solution = middle_solution + jnp.einsum("iab,rib->ria", middle_mats, spread, precision=lax.Precision.HIGHEST)
    middle_residual = middle_rhs - middle_apply(middle_solution)
    middle_solution, unused = chebyshev(middle_apply, middle_inverse, middle_solution, middle_residual, DEG1, False)

    gathered = middle_solution[:, row_index]
    solution = solution + jnp.einsum("ieab,rieb->ria", prolong, gathered, precision=lax.Precision.HIGHEST)
    residual = target - fine_apply(solution)
    solution, residual = chebyshev(fine_apply, fine_inverse, solution, residual, DEG0, True)
    return solution.reshape(NRHS, count_fine * BS), residual.reshape(NRHS, count_fine * BS)
```

```python
import jax
import jax.numpy as jnp
import numpy as np
from jax import lax
from jax.experimental import pallas as pl
from jax.experimental.pallas import tpu as pltpu
from jax.sharding import PartitionSpec as P

F32 = jnp.float32
BF16 = jnp.bfloat16
I32 = jnp.int32
BS = 64
NRHS = 4
R0 = 16
R1 = 8
R2 = 2
XN = 4
YN = 4
TN_ = 32

CENTER = 0.5 * (2.2 + 0.3)
HALF = 0.5 * (2.2 - 0.3)
SCALED = CENTER / HALF
FACTORS = [1.0 / SCALED]
for _ in range(3):
    FACTORS.append(1.0 / (2.0 * SCALED - FACTORS[-1]))
KEEP = [FACTORS[t + 1] * FACTORS[t] for t in range(3)]
GAIN = [2.0 * FACTORS[t + 1] / HALF for t in range(3)]

NN = ((1,), (0,))
NT = ((1,), (1,))
TN = ((0,), (0,))

FINE_ORDER = [(i % 2) * 8 + i // 2 for i in range(R0)]
RIM_ORDER = FINE_ORDER[8:] + FINE_ORDER[:8]
PLAIN_ORDER = list(range(16))


def kern(body, outs, args, smem=()):
    count = len(args)

    def kernel(*refs):
        ins = [r if i in smem else r[...] for i, r in enumerate(refs[:count])]
        for ref, value in zip(refs[count:], body(*ins)):
            ref[...] = value

    specs = [
        pl.BlockSpec(memory_space=pltpu.SMEM if i in smem else pltpu.VMEM) for i in range(count)
    ]
    return pl.pallas_call(
        kernel,
        in_specs=specs,
        out_specs=[pl.BlockSpec(memory_space=pltpu.VMEM) for _ in outs],
        out_shape=[jax.ShapeDtypeStruct(s, d) for s, d in outs],
        compiler_params=pltpu.CompilerParams(vmem_limit_bytes=48 << 20),
        name=body.__name__,
    )(*args)


def mm(a, b, dims):
    return lax.dot_general(a, b, (dims, ((), ())), preferred_element_type=F32)


def iota(shape, dim):
    return lax.broadcasted_iota(I32, shape, dim)


def split(v):
    hi = v.astype(BF16)
    return hi, (v - hi.astype(F32)).astype(BF16)


def stacked(v):
    hi, lo = split(v)
    return jnp.concatenate([hi, lo], axis=0)


def one_hot(size, idx):
    return (iota((size, idx.shape[1]), 0) == idx).astype(F32).astype(BF16)


def lanes_in(x):
    lane = iota(x.shape, 1)
    place = lane & 63
    return jnp.take_along_axis(x, (lane & 64) + 2 * (place & 31) + (place >> 5), axis=1)


def lanes_out(x):
    lane = iota(x.shape, 1)
    b = lane & 63
    return jnp.take_along_axis(x, (lane & 64) + (b & 1) * 32 + (b >> 1), axis=1)


def tiles(raw):
    return lanes_in(raw.reshape(raw.shape[0] * 32, 128))


def double(g):
    return jnp.concatenate([g, g], axis=1)


def spread(hi, lo):
    low = iota(hi.shape, 1) < 64
    zero = jnp.zeros_like(hi)
    top = jnp.concatenate([jnp.where(low, hi, zero), jnp.where(low, lo, zero)], axis=1)
    bottom = jnp.concatenate([jnp.where(low, zero, hi), jnp.where(low, zero, lo)], axis=1)
    return jnp.concatenate([top, bottom], axis=0).astype(BF16)


def gathered(x, table):
    g = mm(x, table, NN)
    return spread(g[:64], g[64:])


def pick(t, order):
    lane = iota((32, 128), 1)
    place = (lane & 63) >> 2
    y = jnp.zeros((32, 128), F32)
    for i in range(16):
        y = y + jnp.where(place == order[i], t[i * 32 : i * 32 + 32], 0.0)
    return jnp.concatenate([y[:, :64], y[:, 64:]], axis=0)


def forward(his, los, rights, order):
    hi = jnp.concatenate(his, axis=1) if len(his) > 1 else his[0]
    lo = jnp.concatenate(los, axis=1) if len(los) > 1 else los[0]
    right = jnp.concatenate(rights, axis=0) if len(rights) > 1 else rights[0]
    a = mm(hi, right, NN)
    return pick(a[:, :128] + a[:, 128:] + mm(lo, right[:, :128], NN), order)


def diagonal(m, order):
    sub = iota(m.shape, 0) & 31
    lane = iota(m.shape, 1)
    kept = jnp.where((lane == sub) | (lane == sub + 96), m, 0.0)
    ones = ((iota((128, 128), 0) >> 6) == (iota((128, 128), 1) >> 6)).astype(F32).astype(BF16)
    hi, lo = split(kept)
    return pick(mm(hi, ones, NN) + mm(lo, ones, NN), order)


def columns_of(rows):
    z = lanes_in(jnp.concatenate([rows[:, m * 128 : m * 128 + 128] for m in range(8)], axis=0))
    t = z.T
    return jnp.concatenate([t[:64], t[64:]], axis=1)


def rows_of(v):
    t = lanes_out(jnp.concatenate([v[:, :32], v[:, 32:]], axis=0).T)
    return jnp.concatenate([t[m * 4 : m * 4 + 4] for m in range(8)], axis=1)


def rim(left, right):
    lane = iota(left.shape, 1)
    return jnp.where((((lane & 63) >> 2) & 7) < 4, right, left)


def fine_tables(device, own, left, right):
    wide, near = [], []
    for k in range(3):
        g = own[k : k + 1]
        r = rim(left[k : k + 1], right[k : k + 1])
        base = (device - 1) * 64
        wide.append([one_hot(192, g - base), one_hot(192, r - base)])
        near.append(one_hot(128, (g & 63) + jnp.where((g >> 6) == device, 0, 64)))
    return wide, near


def fine_both(hi, lo, x, wide):
    return jnp.concatenate(
        [
            forward(
                [hi[c, k] for k in range(3)],
                [lo[c, k] for k in range(3)],
                [gathered(x, wide[k][c]) for k in range(3)],
                (FINE_ORDER, RIM_ORDER)[c],
            )
            for c in range(2)
        ],
        axis=1,
    )


def fine_own(hi, lo, x, near):
    return forward(
        [hi[0, k] for k in range(3)],
        [lo[0, k] for k in range(3)],
        [gathered(x, near[k]) for k in range(3)],
        FINE_ORDER,
    )


def first_passes(device, x, sides, rhs, hi, lo, inverse, idx):
    wide, near = fine_tables(device, *idx)
    window = stacked(jnp.concatenate([sides[0], x, sides[1]], axis=1))
    r = rhs - fine_both(hi, lo, window, wide)
    d = inverse * r / CENTER
    r1 = r[:, :64] - fine_own(hi, lo, stacked(d), near)
    d1 = d[:, :64]
    d2 = KEEP[0] * d1 + GAIN[0] * (inverse[:, :64] * r1)
    return x + d1, jnp.concatenate([d2, r1], axis=1)


def last_passes(device, x, own, left, right, hi, lo, inverse, idx):
    wide, near = fine_tables(device, *idx)
    window = stacked(jnp.concatenate([left[:, :64], own[:, :64], right[:, :64]], axis=1))
    rims = rim(jnp.concatenate([left[:, 64:]] * 2, axis=1), jnp.concatenate([right[:, 64:]] * 2, axis=1))
    rim_d = rim(double(left[:, :64]), double(right[:, :64]))
    r = jnp.concatenate([own[:, 64:], rims[:, :64]], axis=1) - fine_both(hi, lo, window, wide)
    d_old = jnp.concatenate([own[:, :64], rim_d[:, :64]], axis=1)
    d = KEEP[1] * d_old + GAIN[1] * (inverse * r)
    residual = r[:, :64] - fine_own(hi, lo, stacked(d), near)
    return x + own[:, :64] + d[:, :64], residual


def indices(payload):
    return payload[8:11, :128].astype(I32)


def fine_start(device, own, left, right, own_blocks, left_blocks, right_blocks):
    parts = []
    for k in range(3):
        parts.append(tiles(own_blocks[k]))
    for k in range(3):
        parts.append(jnp.concatenate([tiles(left_blocks[k]), tiles(right_blocks[k])], axis=0))
    entries = jnp.concatenate([diagonal(parts[0], FINE_ORDER), diagonal(parts[3], RIM_ORDER)], axis=1)
    inverse = jnp.where(entries == 0.0, 0.0, 1.0 / entries)
    pairs = [split(p) for p in parts]
    hi = jnp.stack([p[0] for p in pairs]).reshape(2, 3, 512, 128)
    lo = jnp.stack([p[1] for p in pairs]).reshape(2, 3, 512, 128)
    x = [columns_of(p[:4]) for p in (left, own, right)]
    b = [columns_of(p[4:8]) for p in (left, own, right)]
    rhs = jnp.concatenate([b[1], rim(b[0], b[2])], axis=1)
    idx = [indices(p) for p in (own, left, right)]
    x1, send = first_passes(device[0, 0], x[1], (x[0], x[2]), rhs, hi, lo, inverse, idx)
    return hi, lo, inverse, rhs, x1, send, jnp.stack(idx)


def restrict(dest, residual, p_hi, p_lo):
    both = jnp.concatenate([residual[:32], residual[32:]], axis=1)
    place = (iota((32, 128), 1) & 63) >> 2
    hi, lo = split(both)
    hi, lo = hi.astype(F32), lo.astype(F32)
    r_hi = jnp.concatenate([jnp.where(place == FINE_ORDER[i], hi, 0.0) for i in range(16)], axis=0).astype(BF16)
    r_lo = jnp.concatenate([jnp.where(place == FINE_ORDER[i], lo, 0.0) for i in range(16)], axis=0).astype(BF16)
    pieces = []
    for e in range(2):
        u = mm(p_hi[e], r_hi, TN) + mm(p_hi[e], r_lo, TN) + mm(p_lo[e], r_hi, TN)
        pieces.append(u[:64, :64] + u[64:, 64:])
    x = stacked(jnp.concatenate(pieces, axis=1))
    out = []
    for q in range(XN * YN):
        table = (iota((256, 128), 0) + q * 256 == dest).astype(F32).astype(BF16)
        g = mm(x, table, NT)
        out.append(g[:64] + g[64:])
    return jnp.stack(out)


def fine_down(device, x, own, left, right, hi, lo, inverse, idx, dest, p_hi, p_lo):
    solution, residual = last_passes(
        device[0, 0], x, own, left, right, hi, lo, inverse, [idx[i] for i in range(3)]
    )
    return solution, restrict(dest, residual, p_hi, p_lo)


def fine_middle(device, x, left, right, rhs, hi, lo, inverse, idx):
    sides = (left[:, :64], right[:, :64])
    x1, send = first_passes(
        device[0, 0], x[:, :64], sides, rhs, hi, lo, inverse, [idx[i] for i in range(3)]
    )
    return x1, send


def fine_end(device, x, own, left, right, hi, lo, inverse, idx):
    solution, residual = last_passes(
        device[0, 0], x, own, left, right, hi, lo, inverse, [idx[i] for i in range(3)]
    )
    return rows_of(solution), rows_of(residual)


def prolong_parts(blocks):
    parts = [split(tiles(blocks[:, e, :])) for e in range(2)]
    return jnp.stack([p[0] for p in parts]), jnp.stack([p[1] for p in parts])


def sum_rows(parts):
    total = jnp.sum(parts, axis=0)
    return (jnp.stack([total[2 * t : 2 * t + 2] for t in range(TN_)]),)


def sum_all(parts):
    return (jnp.broadcast_to(jnp.sum(parts, axis=0)[None], parts.shape),)


def windows(parts, idx):
    x = stacked(jnp.concatenate([parts[t] for t in range(TN_)], axis=0))
    out = []
    for q in range(XN * YN):
        half = idx[:, (q // 2) * 128 : (q // 2) * 128 + 128]
        if q % 2 == 0:
            g = mm(x, one_hot(256, half), NN)
            g = g[:64] + g[64:]
        v = g[:, (q % 2) * 64 : (q % 2) * 64 + 64]
        out.append(jnp.concatenate([v[:32], v[32:]], axis=1))
    return (jnp.stack(out),)


A1_ROWS = 3 * R1 * 32
P1_ROWS = R1 * 32
A2_ROWS = 3 * R2 * 32
D1_AT = A1_ROWS + P1_ROWS + A2_ROWS
D2_AT = D1_AT + 64
IX_AT = D2_AT + 64
PACK_ROWS = IX_AT + 8


def level_pack(blocks, prolong, coarse, idx):
    a1 = [tiles(blocks[k]) for k in range(3)]
    a2 = [lanes_in(coarse[k].reshape(R2 * 32, 128)) for k in range(3)]
    pad = jnp.zeros((256, 128), F32)
    d1 = 1.0 / diagonal_plain(jnp.concatenate([a1[0], pad], axis=0))[:, :32]
    pad = jnp.zeros((448, 128), F32)
    d2 = 1.0 / diagonal_plain(jnp.concatenate([a2[0], pad], axis=0))[:, :8]
    return (
        jnp.concatenate(
            a1
            + [tiles(prolong)]
            + a2
            + [jnp.concatenate([d1] * 4, axis=1), jnp.concatenate([d2] * 16, axis=1), idx],
            axis=0,
        ),
    )


def diagonal_plain(m):
    return diagonal(m, PLAIN_ORDER)


def middle(place, parts, m3, m2, m1, p0, p1, p2, p3, far_low, far_high, unpack):
    slab = place[0, 0]
    sub = place[0, 1]
    packs = [m3, m2, m1, p0, p1, p2, p3]
    lane128 = iota((1, 128), 1)
    pieces = []
    for x in range(XN):
        w = parts[x]
        for y in range(1, YN):
            w = w + parts[y * XN + x]
        pieces.append(jnp.concatenate([w[:, :64], w[:, 64:]], axis=0))
    g = mm(stacked(jnp.concatenate(pieces, axis=1)), one_hot(256, unpack), NN)
    rhs = g[:64] + g[64:]
    quarter = iota((64, 128), 1) >> 5
    tiled = [far_low] + [p[D1_AT : D1_AT + 64] for p in packs] + [far_high]
    d1 = []
    for q in range(3):
        v = jnp.zeros((64, 128), F32)
        for m in range(4):
            if q * 4 + m < 9:
                v = jnp.where(quarter == m, tiled[q * 4 + m], v)
        d1.append(v)
    d1 = jnp.concatenate(d1, axis=1)
    eighth = (iota((64, 128), 1) >> 3) & 7
    d2 = jnp.zeros((64, 128), F32)
    for m in range(7):
        d2 = jnp.where(eighth == m + 1, packs[m][D2_AT : D2_AT + 64], d2)
    d2 = d2[:, :64]
    halves = [split(p[: D1_AT]) for p in packs]

    def rows(part, m, start, count):
        return halves[max(m, 0)][part][start : start + count]

    def pair(part, c, start, count):
        return jnp.concatenate(
            [rows(part, 2 * c - 1, start, count), rows(part, 2 * c, start, count)], axis=0
        )

    a_hi = [[pair(0, c, k * 256, 256) for k in range(3)] for c in range(4)]
    a_lo = [[pair(1, c, k * 256, 256) for k in range(3)] for c in range(4)]
    ix = [p[IX_AT : IX_AT + 8].astype(I32) for p in packs]
    base = (slab - 4) * R1 * NRHS
    starts = [0, 0, 0, 128]
    tables = []
    for c in range(4):
        line = []
        for k in range(3):
            even = ix[2 * c - 1][k : k + 1] - base if c > 0 else jnp.full((1, 128), -1, I32)
            odd = ix[2 * c][k : k + 1] - base
            at = jnp.where(((lane128 >> 5) & 1) == 0, even, odd)
            line.append(one_hot(256, at - starts[c]))
        tables.append(line)

    def apply1(v, chunks):
        x = stacked(v)
        return [
            forward(
                a_hi[c], a_lo[c], [gathered(x[:, starts[c] : starts[c] + 256], t) for t in tables[c]], PLAIN_ORDER
            )
            for c in chunks
        ]

    tail = jnp.zeros((64, 128), F32)
    inv = d1[:, :256]
    d = d1 * rhs / CENTER
    y = d[:, :256]
    r = rhs[:, :256] - jnp.concatenate(apply1(d, range(4)), axis=1)
    for t in range(2):
        step = KEEP[t] * d[:, :256] + GAIN[t] * (inv * r)
        d = jnp.concatenate([step, tail], axis=1)
        y = y + step
        r = r - jnp.concatenate(apply1(d, range(4)), axis=1)
    x = stacked(r)
    low = iota((32, 128), 1) < 64
    q_lane = (iota((32, 128), 1) & 63) >> 2
    first = (lane128 & 63) >> 2
    r_hi, r_lo = [], []
    for kk in range(4):
        g = mm(x, one_hot(256, first * 16 + kk * 4 + (lane128 & 3)), NN)
        r_hi.append(jnp.where(low, g[:32], g[32:64]))
        r_lo.append(jnp.where(low, g[64:96], g[96:128]))
    u = jnp.zeros((128, 128), F32)
    for m in range(7):
        keep = [q_lane == 2 * (m + 1) + j // 4 for j in range(R1)]
        b_hi = jnp.concatenate([jnp.where(keep[j], r_hi[j % 4], 0.0) for j in range(R1)], axis=0).astype(BF16)
        b_lo = jnp.concatenate([jnp.where(keep[j], r_lo[j % 4], 0.0) for j in range(R1)], axis=0).astype(BF16)
        p_hi, p_lo = rows(0, m, A1_ROWS, P1_ROWS), rows(1, m, A1_ROWS, P1_ROWS)
        u = u + mm(p_hi, b_hi, TN) + mm(p_hi, b_lo, TN) + mm(p_lo, b_hi, TN)
    r = u[:64, :64] + u[64:, 64:]
    c_hi, c_lo, c_tables = [], [], []
    c_base = (slab - 4) * R2 * NRHS
    group = (lane128 >> 3) & 7
    for k in range(3):
        start = A1_ROWS + P1_ROWS + k * 64
        c_hi.append(jnp.concatenate([rows(0, m - 1, start, 64) for m in range(8)], axis=0))
        c_lo.append(jnp.concatenate([rows(1, m - 1, start, 64) for m in range(8)], axis=0))
        at = jnp.full((1, 128), -1, I32)
        for m in range(7):
            at = jnp.where(group == m + 1, ix[m][3 + k : 4 + k] - c_base, at)
        c_tables.append(one_hot(64, at))
    d = d2 * r / CENTER
    z = d
    for t in range(3):
        s = stacked(d)
        r = r - forward(c_hi, c_lo, [gathered(s, c_tables[k]) for k in range(3)], PLAIN_ORDER)
        d = KEEP[t] * d + GAIN[t] * (d2 * r)
        z = z + d
    s = stacked(z)
    new = []
    for c in (1, 2):
        at = ((16 * c + ((lane128 & 63) >> 2)) >> 2) * 4 + (lane128 & 3)
        lift = forward(
            [pair(0, c, A1_ROWS, P1_ROWS)], [pair(1, c, A1_ROWS, P1_ROWS)], [gathered(s, one_hot(64, at))], PLAIN_ORDER
        )
        new.append(y[:, c * 64 : c * 64 + 64] + lift)
    y = jnp.concatenate([y[:, :64], new[0], new[1], y[:, 192:256], tail], axis=1)
    side = jnp.zeros((64, 64), F32)

    def at_centre(v):
        return jnp.concatenate([side, v, side, tail], axis=1)

    inv = inv[:, 64:192]
    r = rhs[:, 64:192] - jnp.concatenate(apply1(y, (1, 2)), axis=1)
    d = inv * r / CENTER
    y = y[:, 64:192] + d
    r = r - jnp.concatenate(apply1(at_centre(d), (1, 2)), axis=1)
    d = KEEP[0] * d + GAIN[0] * (inv * r)
    y = y + d
    r = r[:, 64:] - apply1(at_centre(d), (2,))[0]
    own = y[:, 64:] + KEEP[1] * d[:, 64:] + GAIN[1] * (inv[:, 64:] * r)
    pick_rows = (iota((8, 64), 1) == iota((8, 64), 0) + sub * 8).astype(F32).astype(BF16)
    hi, lo = split(own)
    o = mm(pick_rows, hi, NT) + mm(pick_rows, lo, NT)
    o = jnp.concatenate([o[:4], o[4:]], axis=1)
    return (jnp.broadcast_to(o[None], (TN_, 4, 128)),)


def fine_up(rows_ref, odd_ref, all_ref, x_ref, hi_ref, lo_ref, out_ref, line):
    for p in range(32):
        v = all_ref[rows_ref[p]]
        line[p * 4 : p * 4 + 4, :] = jnp.where(odd_ref[p] == 1, pltpu.roll(v, 64, 1), v)
    w = line[:, :64].T
    hi, lo = split(w)
    hi, lo = hi.astype(F32), lo.astype(F32)
    rights = [
        spread(double(hi[:, e * 64 : e * 64 + 64]), double(lo[:, e * 64 : e * 64 + 64])) for e in range(2)
    ]
    x = x_ref[...] + forward([hi_ref[0], hi_ref[1]], [lo_ref[0], lo_ref[1]], rights, FINE_ORDER)
    out_ref[...] = double(x)


def fine_up_call(rows, odd, gathered_rows, x, hi, lo):
    smem, vmem = pl.BlockSpec(memory_space=pltpu.SMEM), pl.BlockSpec(memory_space=pltpu.VMEM)
    return pl.pallas_call(
        fine_up,
        in_specs=[smem, smem, vmem, vmem, vmem, vmem],
        out_specs=vmem,
        out_shape=jax.ShapeDtypeStruct((64, 128), F32),
        scratch_shapes=[pltpu.VMEM((128, 128), F32)],
        compiler_params=pltpu.CompilerParams(vmem_limit_bytes=48 << 20),
        name="fine_up",
    )(rows, odd, gathered_rows, x, hi, lo)


XY = [[(y * TN_ + t) * XN + x for y in range(YN) for x in range(XN)] for t in range(TN_)]
ZC = [[y * TN_ + t for t in range(TN_)] for y in range(YN)]


def across(value):
    return lax.all_to_all(value, ("slab", "sub"), 0, 0, tiled=True, axis_index_groups=XY)


def along(value):
    return lax.all_to_all(value, "slab", 0, 0, tiled=True, axis_index_groups=ZC)


def shifted(value, axis, by):
    n = lax.axis_size(axis)
    return lax.ppermute(value, axis, [(i, i + by) for i in range(n) if 0 <= i + by < n])


def unpack_table():
    idx = np.full((1, 384), -1, np.int32)
    for rel in range(-4, 5):
        for row in range(R1):
            x, pair_row = row // 2, row % 2
            m = rel + 4 - (1 if x == 0 else 0)
            if 0 <= m < 8:
                for r in range(NRHS):
                    idx[0, (rel + 4) * 32 + row * 4 + r] = x * 64 + m * 8 + pair_row * 4 + r
    return idx


def lane_index(columns, times):
    t = columns.T
    v = (t[:, :, None] * NRHS + jnp.arange(NRHS, dtype=I32)).reshape(3, -1)
    return jnp.concatenate([v] * times, axis=1).astype(F32)


def places(values):
    return values.reshape(8, 2, -1).transpose(2, 1, 0).reshape(values.shape[1], 16)


def body(
    right_side,
    warm_start,
    fine_blocks,
    fine_columns,
    fine_prolong,
    owner_rows,
    send_slots,
    receive_rows,
    middle_blocks,
    middle_columns,
    middle_prolong,
    coarse_blocks,
    coarse_columns,
):
    both = ("slab", "sub")
    slab = lax.axis_index("slab").astype(I32)
    sub = lax.axis_index("sub").astype(I32)
    device = (slab * XN + sub).reshape(1, 1)
    place = jnp.stack([slab, sub]).reshape(1, 2)
    rhs4 = jnp.arange(NRHS, dtype=I32)

    g = places(fine_columns)
    g = (g // 16) * 64 + ((g % 2) * 8 + (g % 16) // 2) * 4
    g = (g[:, :, None] + rhs4).reshape(3, 64)
    g = jnp.concatenate([g, g], axis=1).astype(F32)
    own = jnp.concatenate([warm_start, right_side, jnp.pad(g, ((0, 5), (0, 896)))], axis=0)
    left, right = shifted(own, both, 1), shifted(own, both, -1)
    blocks = fine_blocks.transpose(1, 0, 2)
    left_blocks = shifted(blocks[:, 8:], both, 1)
    right_blocks = shifted(blocks[:, :8], both, -1)

    ix = jnp.concatenate([lane_index(middle_columns, 4), lane_index(coarse_columns, 16)], axis=0)
    (pack,) = kern(
        level_pack,
        [((PACK_ROWS, 128), F32)],
        [middle_blocks.transpose(1, 0, 2), middle_prolong, coarse_blocks.transpose(1, 0, 2), jnp.pad(ix, ((0, 2), (0, 0)))],
    )
    near = [shifted(pack, "slab", by) for by in (3, 2, 1)] + [pack] + [shifted(pack, "slab", -by) for by in (1, 2, 3)]
    inverse1 = pack[D1_AT : D1_AT + 64]
    far = [shifted(inverse1, "slab", 4), shifted(inverse1, "slab", -4)]
    p_hi, p_lo = kern(prolong_parts, [((2, 512, 128), BF16)] * 2, [fine_prolong])

    sends = ((64, 128), F32)
    hi, lo, inverse, rhs, x1, send, idx = kern(
        fine_start,
        [((2, 3, 512, 128), BF16)] * 2 + [sends, sends, ((64, 64), F32), sends, ((3, 3, 128), I32)],
        [device, own, left, right, blocks, left_blocks, right_blocks],
        smem=(0,),
    )
    o = places(owner_rows)
    dest = ((o // 256) * XN + (o % 8) // 2) * 256 + ((o // 8) % TN_) * 8 + (o % 2) * 4
    dest = (dest[:, :, None] + rhs4).reshape(1, 128)
    x3, dense = kern(
        fine_down,
        [((64, 64), F32), ((16, 64, 256), F32)],
        [device, x1, send, shifted(send, both, 1), shifted(send, both, -1), hi, lo, inverse, idx, dest, p_hi, p_lo],
        smem=(0,),
    )

    (part,) = kern(sum_rows, [((TN_, 2, 256), F32)], [across(dense)])
    (part,) = kern(sum_all, [((TN_, 2, 256), F32)], [along(part)])
    q = jnp.arange(XN * YN * 64, dtype=I32)
    rel = (q % 64) // 8 - 4 + (sub == 0).astype(I32)
    wanted = (q // 256) * TN_ + slab % TN_ + rel
    wanted = jnp.where(wanted // TN_ == slab // TN_, (wanted % TN_) * 8 + q % 8, -1)
    wanted = jnp.where((rel >= -4) & (wanted >= 0), wanted, -1)
    (part,) = kern(windows, [((16, 32, 128), F32)], [along(part), wanted.reshape(1, 1024)])
    part = across(part)

    (share,) = kern(
        middle,
        [((TN_, 4, 128), F32)],
        [place, part] + near + far + [jnp.asarray(unpack_table())],
        smem=(0,),
    )
    line = along(share)
    every = across(jnp.broadcast_to(line[None], (XN * YN, TN_, 4, 128)))
    at = ((o // 256) * XN + (o % 8) // 2) * TN_ + (o // 8) % TN_
    x = fine_up_call(
        at.reshape(32), (o % 2).reshape(32), every.reshape(XN * YN * TN_, 4, 128), x3, p_hi, p_lo
    )

    x1, send = kern(
        fine_middle,
        [((64, 64), F32), sends],
        [device, x, shifted(x, both, 1), shifted(x, both, -1), rhs, hi, lo, inverse, idx],
        smem=(0,),
    )
    return tuple(
        kern(
            fine_end,
            [((NRHS, 1024), F32)] * 2,
            [device, x1, send, shifted(send, both, 1), shifted(send, both, -1), hi, lo, inverse, idx],
            smem=(0,),
        )
    )


def solution(mesh):
    in_specs = (
        P(None, ("slab", "sub")),
        P(None, ("slab", "sub")),
        P(("slab", "sub"), None, None),
        P(("slab", "sub"), None),
        P(("slab", "sub"), None, None),
        P(("slab", "sub"), None),
        P(("slab", "sub"), None),
        P("slab", "sub", None, None),
        P("slab", None, None),
        P("slab", None),
        P("slab", None),
        P("slab", None, None),
        P("slab", None),
    )
    out_specs = (P(None, ("slab", "sub")), P(None, ("slab", "sub")))
    return jax.shard_map(body, mesh=mesh, in_specs=in_specs, out_specs=out_specs, check_vma=False)
```

```python
import jax
import jax.numpy as jnp
import numpy as np
from jax import lax
from jax.experimental import pallas as pl
from jax.experimental.pallas import tpu as pltpu
from jax.sharding import PartitionSpec as P

F32 = jnp.float32
BF16 = jnp.bfloat16
I32 = jnp.int32
BS = 64
NRHS = 4
R0 = 16
R1 = 8
R2 = 2
XN = 4
YN = 4
TN_ = 32

CENTER = 0.5 * (2.2 + 0.3)
HALF = 0.5 * (2.2 - 0.3)
SCALED = CENTER / HALF
FACTORS = [1.0 / SCALED]
for _ in range(3):
    FACTORS.append(1.0 / (2.0 * SCALED - FACTORS[-1]))
KEEP = [FACTORS[t + 1] * FACTORS[t] for t in range(3)]
GAIN = [2.0 * FACTORS[t + 1] / HALF for t in range(3)]

NN = ((1,), (0,))
NT = ((1,), (1,))
TN = ((0,), (0,))

FINE_ORDER = [(i % 2) * 8 + i // 2 for i in range(R0)]
RIM_ORDER = FINE_ORDER[8:] + FINE_ORDER[:8]
PLAIN_ORDER = list(range(16))


def kern(body, outs, args, smem=()):
    count = len(args)

    def kernel(*refs):
        ins = [r if i in smem else r[...] for i, r in enumerate(refs[:count])]
        for ref, value in zip(refs[count:], body(*ins)):
            ref[...] = value

    specs = [
        pl.BlockSpec(memory_space=pltpu.SMEM if i in smem else pltpu.VMEM) for i in range(count)
    ]
    return pl.pallas_call(
        kernel,
        in_specs=specs,
        out_specs=[pl.BlockSpec(memory_space=pltpu.VMEM) for _ in outs],
        out_shape=[jax.ShapeDtypeStruct(s, d) for s, d in outs],
        compiler_params=pltpu.CompilerParams(vmem_limit_bytes=48 << 20),
        name=body.__name__,
    )(*args)


def mm(a, b, dims):
    return lax.dot_general(a, b, (dims, ((), ())), preferred_element_type=F32)


def iota(shape, dim):
    return lax.broadcasted_iota(I32, shape, dim)


def split(v):
    hi = v.astype(BF16)
    return hi, (v - hi.astype(F32)).astype(BF16)


def stacked(v):
    hi, lo = split(v)
    return jnp.concatenate([hi, lo], axis=0)


def one_hot(size, idx):
    return (iota((size, idx.shape[1]), 0) == idx).astype(F32).astype(BF16)


def lanes_in(x):
    lane = iota(x.shape, 1)
    place = lane & 63
    return jnp.take_along_axis(x, (lane & 64) + 2 * (place & 31) + (place >> 5), axis=1)


def lanes_out(x):
    lane = iota(x.shape, 1)
    b = lane & 63
    return jnp.take_along_axis(x, (lane & 64) + (b & 1) * 32 + (b >> 1), axis=1)


def tiles(raw):
    return lanes_in(raw.reshape(raw.shape[0] * 32, 128))


def double(g):
    return jnp.concatenate([g, g], axis=1)


def spread(hi, lo):
    low = iota(hi.shape, 1) < 64
    zero = jnp.zeros_like(hi)
    top = jnp.concatenate([jnp.where(low, hi, zero), jnp.where(low, lo, zero)], axis=1)
    bottom = jnp.concatenate([jnp.where(low, zero, hi), jnp.where(low, zero, lo)], axis=1)
    return jnp.concatenate([top, bottom], axis=0).astype(BF16)


def gathered(x, table):
    g = mm(x, table, NN)
    return spread(g[:64], g[64:])


def pick(t, order):
    lane = iota((32, 128), 1)
    place = (lane & 63) >> 2
    y = jnp.zeros((32, 128), F32)
    for i in range(16):
        y = y + jnp.where(place == order[i], t[i * 32 : i * 32 + 32], 0.0)
    return jnp.concatenate([y[:, :64], y[:, 64:]], axis=0)


def forward(his, los, rights, order):
    hi = jnp.concatenate(his, axis=1) if len(his) > 1 else his[0]
    lo = jnp.concatenate(los, axis=1) if len(los) > 1 else los[0]
    right = jnp.concatenate(rights, axis=0) if len(rights) > 1 else rights[0]
    a = mm(hi, right, NN)
    return pick(a[:, :128] + a[:, 128:] + mm(lo, right[:, :128], NN), order)


def diagonal(m, order):
    sub = iota(m.shape, 0) & 31
    lane = iota(m.shape, 1)
    kept = jnp.where((lane == sub) | (lane == sub + 96), m, 0.0)
    ones = ((iota((128, 128), 0) >> 6) == (iota((128, 128), 1) >> 6)).astype(F32).astype(BF16)
    hi, lo = split(kept)
    return pick(mm(hi, ones, NN) + mm(lo, ones, NN), order)


def columns_of(rows):
    z = lanes_in(jnp.concatenate([rows[:, m * 128 : m * 128 + 128] for m in range(8)], axis=0))
    t = z.T
    return jnp.concatenate([t[:64], t[64:]], axis=1)


def rows_of(v):
    t = lanes_out(jnp.concatenate([v[:, :32], v[:, 32:]], axis=0).T)
    return jnp.concatenate([t[m * 4 : m * 4 + 4] for m in range(8)], axis=1)


def rim(left, right):
    lane = iota(left.shape, 1)
    return jnp.where((((lane & 63) >> 2) & 7) < 4, right, left)


def fine_tables(device, own, left, right):
    wide, near = [], []
    for k in range(3):
        g = own[k : k + 1]
        r = rim(left[k : k + 1], right[k : k + 1])
        base = (device - 1) * 64
        wide.append([one_hot(192, g - base), one_hot(192, r - base)])
        near.append(one_hot(128, (g & 63) + jnp.where((g >> 6) == device, 0, 64)))
    return wide, near


def fine_both(hi, lo, x, wide):
    return jnp.concatenate(
        [
            forward(
                [hi[c, k] for k in range(3)],
                [lo[c, k] for k in range(3)],
                [gathered(x, wide[k][c]) for k in range(3)],
                (FINE_ORDER, RIM_ORDER)[c],
            )
            for c in range(2)
        ],
        axis=1,
    )


def fine_own(hi, lo, x, near):
    return forward(
        [hi[0, k] for k in range(3)],
        [lo[0, k] for k in range(3)],
        [gathered(x, near[k]) for k in range(3)],
        FINE_ORDER,
    )


def first_passes(device, x, sides, rhs, hi, lo, inverse, idx):
    wide, near = fine_tables(device, *idx)
    window = stacked(jnp.concatenate([sides[0], x, sides[1]], axis=1))
    r = rhs - fine_both(hi, lo, window, wide)
    d = inverse * r / CENTER
    r1 = r[:, :64] - fine_own(hi, lo, stacked(d), near)
    d1 = d[:, :64]
    d2 = KEEP[0] * d1 + GAIN[0] * (inverse[:, :64] * r1)
    return x + d1, jnp.concatenate([d2, r1], axis=1)


def last_passes(device, x, own, left, right, hi, lo, inverse, idx):
    wide, near = fine_tables(device, *idx)
    window = stacked(jnp.concatenate([left[:, :64], own[:, :64], right[:, :64]], axis=1))
    rims = rim(jnp.concatenate([left[:, 64:]] * 2, axis=1), jnp.concatenate([right[:, 64:]] * 2, axis=1))
    rim_d = rim(double(left[:, :64]), double(right[:, :64]))
    r = jnp.concatenate([own[:, 64:], rims[:, :64]], axis=1) - fine_both(hi, lo, window, wide)
    d_old = jnp.concatenate([own[:, :64], rim_d[:, :64]], axis=1)
    d = KEEP[1] * d_old + GAIN[1] * (inverse * r)
    residual = r[:, :64] - fine_own(hi, lo, stacked(d), near)
    return x + own[:, :64] + d[:, :64], residual


def indices(payload):
    return payload[:3, 1024:1152].astype(I32)


def fine_start(device, own, left_all, right_all, own_blocks):
    parts = []
    for k in range(3):
        parts.append(tiles(own_blocks[k]))
    for k in range(3):
        parts.append(jnp.concatenate([tiles(left_all[k]), tiles(right_all[k])], axis=0))
    left, right = left_all[3], right_all[3]
    entries = jnp.concatenate([diagonal(parts[0], FINE_ORDER), diagonal(parts[3], RIM_ORDER)], axis=1)
    inverse = jnp.where(entries == 0.0, 0.0, 1.0 / entries)
    pairs = [split(p) for p in parts]
    hi = jnp.stack([p[0] for p in pairs]).reshape(2, 3, 512, 128)
    lo = jnp.stack([p[1] for p in pairs]).reshape(2, 3, 512, 128)
    x = [columns_of(p[:4, :1024]) for p in (left, own, right)]
    b = [columns_of(p[4:, :1024]) for p in (left, own, right)]
    rhs = jnp.concatenate([b[1], rim(b[0], b[2])], axis=1)
    idx = [indices(p) for p in (own, left, right)]
    x1, send = first_passes(device[0, 0], x[1], (x[0], x[2]), rhs, hi, lo, inverse, idx)
    return hi, lo, inverse, rhs, x1, send, jnp.stack(idx)


def restrict(dest, residual, p_hi, p_lo):
    both = jnp.concatenate([residual[:32], residual[32:]], axis=1)
    place = (iota((32, 128), 1) & 63) >> 2
    hi, lo = split(both)
    hi, lo = hi.astype(F32), lo.astype(F32)
    r_hi = jnp.concatenate([jnp.where(place == FINE_ORDER[i], hi, 0.0) for i in range(16)], axis=0).astype(BF16)
    r_lo = jnp.concatenate([jnp.where(place == FINE_ORDER[i], lo, 0.0) for i in range(16)], axis=0).astype(BF16)
    pieces = []
    for e in range(2):
        u = mm(p_hi[e], r_hi, TN) + mm(p_hi[e], r_lo, TN) + mm(p_lo[e], r_hi, TN)
        pieces.append(u[:64, :64] + u[64:, 64:])
    x = stacked(jnp.concatenate(pieces, axis=1))
    out = []
    for q in range(XN * YN):
        table = (iota((256, 128), 0) + q * 256 == dest).astype(F32).astype(BF16)
        g = mm(x, table, NT)
        out.append(g[:64] + g[64:])
    return jnp.stack(out)


def fine_down(device, x, own, left, right, hi, lo, inverse, idx, dest, p_hi, p_lo):
    solution, residual = last_passes(
        device[0, 0], x, own, left, right, hi, lo, inverse, [idx[i] for i in range(3)]
    )
    return solution, restrict(dest, residual, p_hi, p_lo)


def fine_middle(device, x, left, right, rhs, hi, lo, inverse, idx):
    sides = (left[:, :64], right[:, :64])
    x1, send = first_passes(
        device[0, 0], x[:, :64], sides, rhs, hi, lo, inverse, [idx[i] for i in range(3)]
    )
    return x1, send


def fine_end(device, x, own, left, right, hi, lo, inverse, idx):
    solution, residual = last_passes(
        device[0, 0], x, own, left, right, hi, lo, inverse, [idx[i] for i in range(3)]
    )
    return rows_of(solution), rows_of(residual)


def prolong_parts(blocks):
    parts = [split(tiles(blocks[:, e, :])) for e in range(2)]
    return jnp.stack([p[0] for p in parts]), jnp.stack([p[1] for p in parts])


def sum_rows(parts):
    total = jnp.sum(parts, axis=0)
    return (jnp.stack([total[2 * t : 2 * t + 2] for t in range(TN_)]),)


def sum_all(parts):
    return (jnp.broadcast_to(jnp.sum(parts, axis=0)[None], parts.shape),)


def windows(parts, idx):
    x = stacked(jnp.concatenate([parts[t] for t in range(TN_)], axis=0))
    out = []
    for q in range(XN * YN):
        half = idx[:, (q // 2) * 128 : (q // 2) * 128 + 128]
        if q % 2 == 0:
            g = mm(x, one_hot(256, half), NN)
            g = g[:64] + g[64:]
        v = g[:, (q % 2) * 64 : (q % 2) * 64 + 64]
        out.append(jnp.concatenate([v[:32], v[32:]], axis=1))
    return (jnp.stack(out),)


A1_ROWS = 3 * R1 * 32
P1_ROWS = R1 * 32
A2_ROWS = 3 * R2 * 32
D1_AT = A1_ROWS + P1_ROWS + A2_ROWS
D2_AT = D1_AT + 64
IX_AT = D2_AT + 64
PACK_ROWS = IX_AT + 8


def level_pack(blocks, prolong, coarse, idx):
    a1 = [tiles(blocks[k]) for k in range(3)]
    a2 = [lanes_in(coarse[k].reshape(R2 * 32, 128)) for k in range(3)]
    pad = jnp.zeros((256, 128), F32)
    d1 = 1.0 / diagonal_plain(jnp.concatenate([a1[0], pad], axis=0))[:, :32]
    pad = jnp.zeros((448, 128), F32)
    d2 = 1.0 / diagonal_plain(jnp.concatenate([a2[0], pad], axis=0))[:, :8]
    return (
        jnp.concatenate(
            a1
            + [tiles(prolong)]
            + a2
            + [jnp.concatenate([d1] * 4, axis=1), jnp.concatenate([d2] * 16, axis=1), idx],
            axis=0,
        ),
    )


def diagonal_plain(m):
    return diagonal(m, PLAIN_ORDER)


STARTS = [0, 0, 0, 128]


def middle_prep(place, m3, m2, m1, p0, p1, p2, p3, far_low, far_high):
    slab = place[0, 0]
    packs = [m3, m2, m1, p0, p1, p2, p3]
    lane128 = iota((1, 128), 1)
    quarter = iota((64, 128), 1) >> 5
    tiled = [far_low] + [p[D1_AT : D1_AT + 64] for p in packs] + [far_high]
    d1 = []
    for q in range(3):
        v = jnp.zeros((64, 128), F32)
        for m in range(4):
            if q * 4 + m < 9:
                v = jnp.where(quarter == m, tiled[q * 4 + m], v)
        d1.append(v)
    d1 = jnp.concatenate(d1, axis=1)
    eighth = (iota((64, 128), 1) >> 3) & 7
    d2 = jnp.zeros((64, 128), F32)
    for m in range(7):
        d2 = jnp.where(eighth == m + 1, packs[m][D2_AT : D2_AT + 64], d2)
    d2 = d2[:, :64]
    ix = [p[IX_AT : IX_AT + 8].astype(I32) for p in packs]
    base = (slab - 4) * R1 * NRHS
    tables = []
    for c in range(4):
        for k in range(3):
            even = ix[2 * c - 1][k : k + 1] - base if c > 0 else jnp.full((1, 128), -1, I32)
            odd = ix[2 * c][k : k + 1] - base
            at = jnp.where(((lane128 >> 5) & 1) == 0, even, odd)
            tables.append(one_hot(256, at - STARTS[c]))
    c_tables = []
    c_base = (slab - 4) * R2 * NRHS
    group = (lane128 >> 3) & 7
    for k in range(3):
        at = jnp.full((1, 128), -1, I32)
        for m in range(7):
            at = jnp.where(group == m + 1, ix[m][3 + k : 4 + k] - c_base, at)
        c_tables.append(one_hot(64, at))
    halves = [split(p[:D1_AT]) for p in packs]
    return (
        jnp.stack([h[0] for h in halves]),
        jnp.stack([h[1] for h in halves]),
        d1,
        d2,
        jnp.stack(tables),
        jnp.stack(c_tables),
    )


def middle(place, parts, b_hi, b_lo, d1, d2, tables, c_tables, unpack):
    sub = place[0, 1]
    blocks = (b_hi, b_lo)
    lane128 = iota((1, 128), 1)
    pieces = []
    for x in range(XN):
        w = parts[x]
        for y in range(1, YN):
            w = w + parts[y * XN + x]
        pieces.append(jnp.concatenate([w[:, :64], w[:, 64:]], axis=0))
    g = mm(stacked(jnp.concatenate(pieces, axis=1)), one_hot(256, unpack), NN)
    rhs = g[:64] + g[64:]
    def rows(part, m, start, count):
        return blocks[part][max(m, 0), start : start + count]

    def pair(part, c, start, count):
        return jnp.concatenate(
            [rows(part, 2 * c - 1, start, count), rows(part, 2 * c, start, count)], axis=0
        )

    a_hi = [[pair(0, c, k * 256, 256) for k in range(3)] for c in range(4)]
    a_lo = [[pair(1, c, k * 256, 256) for k in range(3)] for c in range(4)]

    def apply1(v, chunks):
        x = stacked(v)
        return [
            forward(
                a_hi[c], a_lo[c], [gathered(x[:, STARTS[c] : STARTS[c] + 256], tables[3 * c + k]) for k in range(3)], PLAIN_ORDER
            )
            for c in chunks
        ]

    tail = jnp.zeros((64, 128), F32)
    inv = d1[:, :256]
    d = d1 * rhs / CENTER
    y = d[:, :256]
    r = rhs[:, :256] - jnp.concatenate(apply1(d, range(4)), axis=1)
    for t in range(2):
        step = KEEP[t] * d[:, :256] + GAIN[t] * (inv * r)
        d = jnp.concatenate([step, tail], axis=1)
        y = y + step
        r = r - jnp.concatenate(apply1(d, range(4)), axis=1)
    x = stacked(r)
    low = iota((32, 128), 1) < 64
    q_lane = (iota((32, 128), 1) & 63) >> 2
    first = (lane128 & 63) >> 2
    r_hi, r_lo = [], []
    for kk in range(4):
        g = mm(x, one_hot(256, first * 16 + kk * 4 + (lane128 & 3)), NN)
        r_hi.append(jnp.where(low, g[:32], g[32:64]))
        r_lo.append(jnp.where(low, g[64:96], g[96:128]))
    u = jnp.zeros((128, 128), F32)
    for m in range(7):
        keep = [q_lane == 2 * (m + 1) + j // 4 for j in range(R1)]
        b_hi = jnp.concatenate([jnp.where(keep[j], r_hi[j % 4], 0.0) for j in range(R1)], axis=0).astype(BF16)
        b_lo = jnp.concatenate([jnp.where(keep[j], r_lo[j % 4], 0.0) for j in range(R1)], axis=0).astype(BF16)
        p_hi, p_lo = rows(0, m, A1_ROWS, P1_ROWS), rows(1, m, A1_ROWS, P1_ROWS)
        u = u + mm(p_hi, b_hi, TN) + mm(p_hi, b_lo, TN) + mm(p_lo, b_hi, TN)
    r = u[:64, :64] + u[64:, 64:]
    c_hi, c_lo = [], []
    for k in range(3):
        start = A1_ROWS + P1_ROWS + k * 64
        c_hi.append(jnp.concatenate([rows(0, m - 1, start, 64) for m in range(8)], axis=0))
        c_lo.append(jnp.concatenate([rows(1, m - 1, start, 64) for m in range(8)], axis=0))
    d = d2 * r / CENTER
    z = d
    for t in range(3):
        s = stacked(d)
        r = r - forward(c_hi, c_lo, [gathered(s, c_tables[k]) for k in range(3)], PLAIN_ORDER)
        d = KEEP[t] * d + GAIN[t] * (d2 * r)
        z = z + d
    s = stacked(z)
    new = []
    for c in (1, 2):
        at = ((16 * c + ((lane128 & 63) >> 2)) >> 2) * 4 + (lane128 & 3)
        lift = forward(
            [pair(0, c, A1_ROWS, P1_ROWS)], [pair(1, c, A1_ROWS, P1_ROWS)], [gathered(s, one_hot(64, at))], PLAIN_ORDER
        )
        new.append(y[:, c * 64 : c * 64 + 64] + lift)
    y = jnp.concatenate([y[:, :64], new[0], new[1], y[:, 192:256], tail], axis=1)
    side = jnp.zeros((64, 64), F32)

    def at_centre(v):
        return jnp.concatenate([side, v, side, tail], axis=1)

    inv = inv[:, 64:192]
    r = rhs[:, 64:192] - jnp.concatenate(apply1(y, (1, 2)), axis=1)
    d = inv * r / CENTER
    y = y[:, 64:192] + d
    r = r - jnp.concatenate(apply1(at_centre(d), (1, 2)), axis=1)
    d = KEEP[0] * d + GAIN[0] * (inv * r)
    y = y + d
    r = r[:, 64:] - apply1(at_centre(d), (2,))[0]
    own = y[:, 64:] + KEEP[1] * d[:, 64:] + GAIN[1] * (inv[:, 64:] * r)
    pick_rows = (iota((8, 64), 1) == iota((8, 64), 0) + sub * 8).astype(F32).astype(BF16)
    hi, lo = split(own)
    o = mm(pick_rows, hi, NT) + mm(pick_rows, lo, NT)
    o = jnp.concatenate([jnp.concatenate([o[:2], o[4:6]], axis=1), jnp.concatenate([o[2:4], o[6:]], axis=1)], axis=1)
    return (jnp.broadcast_to(o[None], (TN_, 2, 256)),)


def fine_up(rows_ref, odd_ref, all_ref, x_ref, hi_ref, lo_ref, out_ref, line):
    for p in range(32):
        v = all_ref[rows_ref[p]]
        v = jnp.concatenate([v[:, :128], v[:, 128:]], axis=0)
        line[p * 4 : p * 4 + 4, :] = jnp.where(odd_ref[p] == 1, pltpu.roll(v, 64, 1), v)
    w = line[:, :64].T
    hi, lo = split(w)
    hi, lo = hi.astype(F32), lo.astype(F32)
    rights = [
        spread(double(hi[:, e * 64 : e * 64 + 64]), double(lo[:, e * 64 : e * 64 + 64])) for e in range(2)
    ]
    x = x_ref[...] + forward([hi_ref[0], hi_ref[1]], [lo_ref[0], lo_ref[1]], rights, FINE_ORDER)
    out_ref[...] = double(x)


def fine_up_call(rows, odd, gathered_rows, x, hi, lo):
    smem, vmem = pl.BlockSpec(memory_space=pltpu.SMEM), pl.BlockSpec(memory_space=pltpu.VMEM)
    return pl.pallas_call(
        fine_up,
        in_specs=[smem, smem, vmem, vmem, vmem, vmem],
        out_specs=vmem,
        out_shape=jax.ShapeDtypeStruct((64, 128), F32),
        scratch_shapes=[pltpu.VMEM((128, 128), F32)],
        compiler_params=pltpu.CompilerParams(vmem_limit_bytes=48 << 20),
        name="fine_up",
    )(rows, odd, gathered_rows, x, hi, lo)


XY = [[(y * TN_ + t) * XN + x for y in range(YN) for x in range(XN)] for t in range(TN_)]
ZC = [[y * TN_ + t for t in range(TN_)] for y in range(YN)]


def across(value):
    return lax.all_to_all(value, ("slab", "sub"), 0, 0, tiled=True, axis_index_groups=XY)


def along(value):
    return lax.all_to_all(value, "slab", 0, 0, tiled=True, axis_index_groups=ZC)


def shifted(value, axis, by):
    n = lax.axis_size(axis)
    return lax.ppermute(value, axis, [(i, i + by) for i in range(n) if 0 <= i + by < n])


def unpack_table():
    idx = np.full((1, 384), -1, np.int32)
    for rel in range(-4, 5):
        for row in range(R1):
            x, pair_row = row // 2, row % 2
            m = rel + 4 - (1 if x == 0 else 0)
            if 0 <= m < 8:
                for r in range(NRHS):
                    idx[0, (rel + 4) * 32 + row * 4 + r] = x * 64 + m * 8 + pair_row * 4 + r
    return idx


def lane_index(columns, times):
    t = columns.T
    v = (t[:, :, None] * NRHS + jnp.arange(NRHS, dtype=I32)).reshape(3, -1)
    return jnp.concatenate([v] * times, axis=1).astype(F32)


def places(values):
    return values.reshape(8, 2, -1).transpose(2, 1, 0).reshape(values.shape[1], 16)


def body(
    right_side,
    warm_start,
    fine_blocks,
    fine_columns,
    fine_prolong,
    owner_rows,
    send_slots,
    receive_rows,
    middle_blocks,
    middle_columns,
    middle_prolong,
    coarse_blocks,
    coarse_columns,
):
    both = ("slab", "sub")
    slab = lax.axis_index("slab").astype(I32)
    sub = lax.axis_index("sub").astype(I32)
    device = (slab * XN + sub).reshape(1, 1)
    place = jnp.stack([slab, sub]).reshape(1, 2)
    rhs4 = jnp.arange(NRHS, dtype=I32)

    g = places(fine_columns)
    g = (g // 16) * 64 + ((g % 2) * 8 + (g % 16) // 2) * 4
    g = (g[:, :, None] + rhs4).reshape(3, 64)
    g = jnp.concatenate([g, g], axis=1).astype(F32)
    own = jnp.concatenate([warm_start, right_side], axis=0)
    own = jnp.concatenate([own, jnp.pad(g, ((0, 5), (0, 2944)))], axis=1)
    blocks = fine_blocks.transpose(1, 0, 2)
    low, high = (
        jnp.concatenate([part, own[None]], axis=0) for part in (blocks[:, :8], blocks[:, 8:])
    )

    ix = jnp.concatenate([lane_index(middle_columns, 4), lane_index(coarse_columns, 16)], axis=0)
    ix, low, high = lax.optimization_barrier((ix, low, high))
    left, right = shifted(high, both, 1), shifted(low, both, -1)
    (pack,) = kern(
        level_pack,
        [((PACK_ROWS, 128), F32)],
        [middle_blocks.transpose(1, 0, 2), middle_prolong, coarse_blocks.transpose(1, 0, 2), jnp.pad(ix, ((0, 2), (0, 0)))],
    )
    near = [shifted(pack, "slab", by) for by in (3, 2, 1)] + [pack] + [shifted(pack, "slab", -by) for by in (1, 2, 3)]
    inverse1 = pack[D1_AT : D1_AT + 64]
    far = [shifted(inverse1, "slab", 4), shifted(inverse1, "slab", -4)]
    p_hi, p_lo = kern(prolong_parts, [((2, 512, 128), BF16)] * 2, [fine_prolong])

    sends = ((64, 128), F32)
    hi, lo, inverse, rhs, x1, send, idx = kern(
        fine_start,
        [((2, 3, 512, 128), BF16)] * 2 + [sends, sends, ((64, 64), F32), sends, ((3, 3, 128), I32)],
        [device, own, left, right, blocks],
        smem=(0,),
    )
    idx, near[0], near[6], near[2] = lax.optimization_barrier((idx, near[0], near[6], near[2]))
    prepared = kern(
        middle_prep,
        [((7, D1_AT, 128), BF16)] * 2
        + [((64, 384), F32), ((64, 64), F32), ((12, 256, 128), BF16), ((3, 64, 128), BF16)],
        [place] + near + far,
        smem=(0,),
    )
    o = places(owner_rows)
    dest = ((o // 256) * XN + (o % 8) // 2) * 256 + ((o // 8) % TN_) * 8 + (o % 2) * 4
    dest = (dest[:, :, None] + rhs4).reshape(1, 128)
    x3, dense = kern(
        fine_down,
        [((64, 64), F32), ((16, 64, 256), F32)],
        [device, x1, send, shifted(send, both, 1), shifted(send, both, -1), hi, lo, inverse, idx, dest, p_hi, p_lo],
        smem=(0,),
    )

    (part,) = kern(sum_rows, [((TN_, 2, 256), F32)], [across(dense)])
    part, *prepared = lax.optimization_barrier((part, *prepared))
    (part,) = kern(sum_all, [((TN_, 2, 256), F32)], [along(part)])
    q = jnp.arange(XN * YN * 64, dtype=I32)
    rel = (q % 64) // 8 - 4 + (sub == 0).astype(I32)
    wanted = (q // 256) * TN_ + slab % TN_ + rel
    wanted = jnp.where(wanted // TN_ == slab // TN_, (wanted % TN_) * 8 + q % 8, -1)
    wanted = jnp.where((rel >= -4) & (wanted >= 0), wanted, -1)
    (part,) = kern(windows, [((16, 32, 128), F32)], [along(part), wanted.reshape(1, 1024)])
    part = across(part)

    (share,) = kern(
        middle,
        [((TN_, 2, 256), F32)],
        [place, part] + prepared + [jnp.asarray(unpack_table())],
        smem=(0,),
    )
    line = along(share)
    every = across(jnp.broadcast_to(line[None], (XN * YN, TN_, 2, 256)))
    at = ((o // 256) * XN + (o % 8) // 2) * TN_ + (o // 8) % TN_
    x = fine_up_call(
        at.reshape(32), (o % 2).reshape(32), every.reshape(XN * YN * TN_, 2, 256), x3, p_hi, p_lo
    )

    x1, send = kern(
        fine_middle,
        [((64, 64), F32), sends],
        [device, x, shifted(x, both, 1), shifted(x, both, -1), rhs, hi, lo, inverse, idx],
        smem=(0,),
    )
    return tuple(
        kern(
            fine_end,
            [((NRHS, 1024), F32)] * 2,
            [device, x1, send, shifted(send, both, 1), shifted(send, both, -1), hi, lo, inverse, idx],
            smem=(0,),
        )
    )


def solution(mesh):
    in_specs = (
        P(None, ("slab", "sub")),
        P(None, ("slab", "sub")),
        P(("slab", "sub"), None, None),
        P(("slab", "sub"), None),
        P(("slab", "sub"), None, None),
        P(("slab", "sub"), None),
        P(("slab", "sub"), None),
        P("slab", "sub", None, None),
        P("slab", None, None),
        P("slab", None),
        P("slab", None),
        P("slab", None, None),
        P("slab", None),
    )
    out_specs = (P(None, ("slab", "sub")), P(None, ("slab", "sub")))
    return jax.shard_map(body, mesh=mesh, in_specs=in_specs, out_specs=out_specs, check_vma=False)
```

```python
import jax
import jax.numpy as jnp
import numpy as np
from jax import lax
from jax.experimental import pallas as pl
from jax.experimental.pallas import tpu as pltpu
from jax.sharding import PartitionSpec as P

F32 = jnp.float32
BF16 = jnp.bfloat16
I32 = jnp.int32
BS = 64
NRHS = 4
R0 = 16
R1 = 8
R2 = 2
XN = 4
YN = 4
TN_ = 32

CENTER = 0.5 * (2.2 + 0.3)
HALF = 0.5 * (2.2 - 0.3)
SCALED = CENTER / HALF
FACTORS = [1.0 / SCALED]
for _ in range(3):
    FACTORS.append(1.0 / (2.0 * SCALED - FACTORS[-1]))
KEEP = [FACTORS[t + 1] * FACTORS[t] for t in range(3)]
GAIN = [2.0 * FACTORS[t + 1] / HALF for t in range(3)]

NN = ((1,), (0,))
NT = ((1,), (1,))
TN = ((0,), (0,))

FINE_ORDER = [(i % 2) * 8 + i // 2 for i in range(R0)]
RIM_ORDER = FINE_ORDER[8:] + FINE_ORDER[:8]
PLAIN_ORDER = list(range(16))


def kern(body, outs, args, smem=()):
    count = len(args)

    def kernel(*refs):
        ins = [r if i in smem else r[...] for i, r in enumerate(refs[:count])]
        for ref, value in zip(refs[count:], body(*ins)):
            ref[...] = value

    specs = [
        pl.BlockSpec(memory_space=pltpu.SMEM if i in smem else pltpu.VMEM) for i in range(count)
    ]
    return pl.pallas_call(
        kernel,
        in_specs=specs,
        out_specs=[pl.BlockSpec(memory_space=pltpu.VMEM) for _ in outs],
        out_shape=[jax.ShapeDtypeStruct(s, d) for s, d in outs],
        compiler_params=pltpu.CompilerParams(vmem_limit_bytes=48 << 20),
        name=body.__name__,
    )(*args)


def mm(a, b, dims):
    return lax.dot_general(a, b, (dims, ((), ())), preferred_element_type=F32)


def iota(shape, dim):
    return lax.broadcasted_iota(I32, shape, dim)


def split(v):
    hi = v.astype(BF16)
    return hi, (v - hi.astype(F32)).astype(BF16)


def stacked(v):
    hi, lo = split(v)
    return jnp.concatenate([hi, lo], axis=0)


def one_hot(size, idx):
    return (iota((size, idx.shape[1]), 0) == idx).astype(F32).astype(BF16)


def lanes_in(x):
    lane = iota(x.shape, 1)
    place = lane & 63
    return jnp.take_along_axis(x, (lane & 64) + 2 * (place & 31) + (place >> 5), axis=1)


def lanes_out(x):
    lane = iota(x.shape, 1)
    b = lane & 63
    return jnp.take_along_axis(x, (lane & 64) + (b & 1) * 32 + (b >> 1), axis=1)


def tiles(raw):
    return lanes_in(raw.reshape(raw.shape[0] * 32, 128))


def double(g):
    return jnp.concatenate([g, g], axis=1)


def spread(hi, lo):
    low = iota(hi.shape, 1) < 64
    zero = jnp.zeros_like(hi)
    top = jnp.concatenate([jnp.where(low, hi, zero), jnp.where(low, lo, zero)], axis=1)
    bottom = jnp.concatenate([jnp.where(low, zero, hi), jnp.where(low, zero, lo)], axis=1)
    return jnp.concatenate([top, bottom], axis=0).astype(BF16)


def gathered(x, table):
    g = mm(x, table, NN)
    return spread(g[:64], g[64:])


def pick(t, order):
    lane = iota((32, 128), 1)
    place = (lane & 63) >> 2
    y = jnp.zeros((32, 128), F32)
    for i in range(16):
        y = y + jnp.where(place == order[i], t[i * 32 : i * 32 + 32], 0.0)
    return jnp.concatenate([y[:, :64], y[:, 64:]], axis=0)


def forward(his, los, rights, order):
    hi = jnp.concatenate(his, axis=1) if len(his) > 1 else his[0]
    lo = jnp.concatenate(los, axis=1) if len(los) > 1 else los[0]
    right = jnp.concatenate(rights, axis=0) if len(rights) > 1 else rights[0]
    a = mm(hi, right, NN)
    return pick(a[:, :128] + a[:, 128:] + mm(lo, right[:, :128], NN), order)


def diagonal(m, order):
    sub = iota(m.shape, 0) & 31
    lane = iota(m.shape, 1)
    kept = jnp.where((lane == sub) | (lane == sub + 96), m, 0.0)
    ones = ((iota((128, 128), 0) >> 6) == (iota((128, 128), 1) >> 6)).astype(F32).astype(BF16)
    hi, lo = split(kept)
    return pick(mm(hi, ones, NN) + mm(lo, ones, NN), order)


def columns_of(rows):
    z = lanes_in(jnp.concatenate([rows[:, m * 128 : m * 128 + 128] for m in range(8)], axis=0))
    t = z.T
    return jnp.concatenate([t[:64], t[64:]], axis=1)


def rows_of(v):
    t = lanes_out(jnp.concatenate([v[:, :32], v[:, 32:]], axis=0).T)
    return jnp.concatenate([t[m * 4 : m * 4 + 4] for m in range(8)], axis=1)


def rim(left, right):
    lane = iota(left.shape, 1)
    return jnp.where((((lane & 63) >> 2) & 7) < 4, right, left)


def fine_tables(device, own, left, right):
    wide, near = [], []
    for k in range(3):
        g = own[k : k + 1]
        r = rim(left[k : k + 1], right[k : k + 1])
        base = (device - 1) * 64
        wide.append([one_hot(192, g - base), one_hot(192, r - base)])
        near.append(one_hot(128, (g & 63) + jnp.where((g >> 6) == device, 0, 64)))
    return wide, near


def fine_both(hi, lo, x, wide):
    return jnp.concatenate(
        [
            forward(
                [hi[c, k] for k in range(3)],
                [lo[c, k] for k in range(3)],
                [gathered(x, wide[k][c]) for k in range(3)],
                (FINE_ORDER, RIM_ORDER)[c],
            )
            for c in range(2)
        ],
        axis=1,
    )


def fine_own(hi, lo, x, near):
    return forward(
        [hi[0, k] for k in range(3)],
        [lo[0, k] for k in range(3)],
        [gathered(x, near[k]) for k in range(3)],
        FINE_ORDER,
    )


def first_passes(device, x, sides, rhs, hi, lo, inverse, idx):
    wide, near = fine_tables(device, *idx)
    window = stacked(jnp.concatenate([sides[0], x, sides[1]], axis=1))
    r = rhs - fine_both(hi, lo, window, wide)
    d = inverse * r / CENTER
    r1 = r[:, :64] - fine_own(hi, lo, stacked(d), near)
    d1 = d[:, :64]
    d2 = KEEP[0] * d1 + GAIN[0] * (inverse[:, :64] * r1)
    return x + d1, jnp.concatenate([d2, r1], axis=1)


def last_passes(device, x, own, left, right, hi, lo, inverse, idx):
    wide, near = fine_tables(device, *idx)
    window = stacked(jnp.concatenate([left[:, :64], own[:, :64], right[:, :64]], axis=1))
    rims = rim(jnp.concatenate([left[:, 64:]] * 2, axis=1), jnp.concatenate([right[:, 64:]] * 2, axis=1))
    rim_d = rim(double(left[:, :64]), double(right[:, :64]))
    r = jnp.concatenate([own[:, 64:], rims[:, :64]], axis=1) - fine_both(hi, lo, window, wide)
    d_old = jnp.concatenate([own[:, :64], rim_d[:, :64]], axis=1)
    d = KEEP[1] * d_old + GAIN[1] * (inverse * r)
    residual = r[:, :64] - fine_own(hi, lo, stacked(d), near)
    return x + own[:, :64] + d[:, :64], residual


def indices(payload):
    return payload[8:11, :128].astype(I32)


def fine_start(device, own, left, right, own_blocks, left_blocks, right_blocks):
    parts = []
    for k in range(3):
        parts.append(tiles(own_blocks[k]))
    for k in range(3):
        parts.append(jnp.concatenate([tiles(left_blocks[k]), tiles(right_blocks[k])], axis=0))
    entries = jnp.concatenate([diagonal(parts[0], FINE_ORDER), diagonal(parts[3], RIM_ORDER)], axis=1)
    inverse = jnp.where(entries == 0.0, 0.0, 1.0 / entries)
    pairs = [split(p) for p in parts]
    hi = jnp.stack([p[0] for p in pairs]).reshape(2, 3, 512, 128)
    lo = jnp.stack([p[1] for p in pairs]).reshape(2, 3, 512, 128)
    x = [columns_of(p[:4]) for p in (left, own, right)]
    b = [columns_of(p[4:8]) for p in (left, own, right)]
    rhs = jnp.concatenate([b[1], rim(b[0], b[2])], axis=1)
    idx = [indices(p) for p in (own, left, right)]
    x1, send = first_passes(device[0, 0], x[1], (x[0], x[2]), rhs, hi, lo, inverse, idx)
    return hi, lo, inverse, rhs, x1, send, jnp.stack(idx)


def restrict(dest, residual, p_hi, p_lo):
    both = jnp.concatenate([residual[:32], residual[32:]], axis=1)
    place = (iota((32, 128), 1) & 63) >> 2
    hi, lo = split(both)
    hi, lo = hi.astype(F32), lo.astype(F32)
    r_hi = jnp.concatenate([jnp.where(place == FINE_ORDER[i], hi, 0.0) for i in range(16)], axis=0).astype(BF16)
    r_lo = jnp.concatenate([jnp.where(place == FINE_ORDER[i], lo, 0.0) for i in range(16)], axis=0).astype(BF16)
    pieces = []
    for e in range(2):
        u = mm(p_hi[e], r_hi, TN) + mm(p_hi[e], r_lo, TN) + mm(p_lo[e], r_hi, TN)
        pieces.append(u[:64, :64] + u[64:, 64:])
    hi, lo = split(jnp.concatenate(pieces, axis=1))
    rows = jnp.broadcast_to(dest[1:2].astype(F32), (16, 128)).astype(BF16)
    x = jnp.concatenate([hi, lo, rows], axis=0)
    out = []
    for q in range(0, XN * YN, 2):
        table = (iota((128, 128), 0) + q * 64 == dest[:1]).astype(F32).astype(BF16)
        g = mm(x, table, NT)
        v, at = g[:64] + g[64:128], g[128:136]
        out.append(jnp.concatenate([jnp.concatenate([v[:32, :64], v[32:, :64]], axis=1), at], axis=0))
        at = jnp.concatenate([at[:, 64:], at[:, :64]], axis=1)
        out.append(jnp.concatenate([jnp.concatenate([v[:32, 64:], v[32:, 64:]], axis=1), at], axis=0))
    return jnp.stack(out)


def fine_down(device, x, own, left, right, hi, lo, inverse, idx, dest, p_hi, p_lo):
    solution, residual = last_passes(
        device[0, 0], x, own, left, right, hi, lo, inverse, [idx[i] for i in range(3)]
    )
    return solution, restrict(dest, residual, p_hi, p_lo)


def fine_middle(device, x, left, right, rhs, hi, lo, inverse, idx):
    sides = (left[:, :64], right[:, :64])
    x1, send = first_passes(
        device[0, 0], x[:, :64], sides, rhs, hi, lo, inverse, [idx[i] for i in range(3)]
    )
    return x1, send


def fine_end(device, x, own, left, right, hi, lo, inverse, idx):
    solution, residual = last_passes(
        device[0, 0], x, own, left, right, hi, lo, inverse, [idx[i] for i in range(3)]
    )
    return rows_of(solution), rows_of(residual)


def prolong_parts(blocks):
    parts = [split(tiles(blocks[:, e, :])) for e in range(2)]
    return jnp.stack([p[0] for p in parts]), jnp.stack([p[1] for p in parts])


def sum_rows(parts):
    total = jnp.zeros((128, 256), F32)
    for q in range(0, XN * YN, 2):
        v = jnp.concatenate(
            [jnp.concatenate([parts[q + i, :32, :64], parts[q + i, :32, 64:]], axis=0) for i in range(2)], axis=1
        )
        at = jnp.concatenate([parts[q + i, 32:33, :64] for i in range(2)], axis=1).astype(I32)
        table = (iota((256, 128), 0) + 1 == at).astype(F32).astype(BF16)
        total = total + mm(stacked(v), table, NT)
    total = total[:64] + total[64:]
    return (jnp.stack([total[2 * t : 2 * t + 2] for t in range(TN_)]),)


def sum_all(parts):
    return (jnp.broadcast_to(jnp.sum(parts, axis=0)[None], parts.shape),)


def windows(parts, idx):
    x = stacked(jnp.concatenate([parts[t] for t in range(TN_)], axis=0))
    out = []
    for q in range(XN * YN):
        half = idx[:, (q // 2) * 128 : (q // 2) * 128 + 128]
        if q % 2 == 0:
            g = mm(x, one_hot(256, half), NN)
            g = g[:64] + g[64:]
        v = g[:, (q % 2) * 64 : (q % 2) * 64 + 64]
        out.append(jnp.concatenate([v[:32], v[32:]], axis=1))
    return (jnp.stack(out),)


A1_ROWS = 3 * R1 * 32
P1_ROWS = R1 * 32
A2_ROWS = 3 * R2 * 32
D1_AT = A1_ROWS + P1_ROWS
D2_AT = D1_AT + 64
IX_AT = D2_AT + 64
A2_AT = IX_AT + 8
PACK_ROWS = A2_AT + A2_ROWS


def level_pack(blocks, prolong, coarse, idx):
    a1 = [tiles(blocks[k]) for k in range(3)]
    a2 = [lanes_in(coarse[k].reshape(R2 * 32, 128)) for k in range(3)]
    pad = jnp.zeros((256, 128), F32)
    d1 = 1.0 / diagonal_plain(jnp.concatenate([a1[0], pad], axis=0))[:, :32]
    pad = jnp.zeros((448, 128), F32)
    d2 = 1.0 / diagonal_plain(jnp.concatenate([a2[0], pad], axis=0))[:, :8]
    return (
        jnp.concatenate(
            a1
            + [tiles(prolong)]
            + [jnp.concatenate([d1] * 4, axis=1), jnp.concatenate([d2] * 16, axis=1), idx]
            + a2,
            axis=0,
        ),
    )


def diagonal_plain(m):
    return diagonal(m, PLAIN_ORDER)


STARTS = [0, 0, 0, 128]


def middle_prep(place, p0, m2, p2, crossed, twin, twin_m2, twin_p2, far_low, far_high):
    slab = place[0, 0]
    even = (slab & 1) == 0
    top = A2_AT
    m3 = jnp.where(even, crossed, twin_m2[:top])
    p3 = jnp.where(even, twin_p2[:top], crossed)
    m1 = jnp.where(even, twin_m2, twin)
    p1 = jnp.where(even, twin, twin_p2)
    packs = [m3, m2, m1, p0, p1, p2, p3]
    lane128 = iota((1, 128), 1)
    quarter = iota((64, 128), 1) >> 5
    tiled = [far_low] + [p[D1_AT : D1_AT + 64] for p in packs] + [far_high]
    d1 = []
    for q in range(3):
        v = jnp.zeros((64, 128), F32)
        for m in range(4):
            if q * 4 + m < 9:
                v = jnp.where(quarter == m, tiled[q * 4 + m], v)
        d1.append(v)
    d1 = jnp.concatenate(d1, axis=1)
    eighth = (iota((64, 128), 1) >> 3) & 7
    d2 = jnp.zeros((64, 128), F32)
    for m in range(7):
        d2 = jnp.where(eighth == m + 1, packs[m][D2_AT : D2_AT + 64], d2)
    d2 = d2[:, :64]
    ix = [p[IX_AT : IX_AT + 8].astype(I32) for p in packs]
    base = (slab - 4) * R1 * NRHS
    tables = []
    for c in range(4):
        for k in range(3):
            one = ix[2 * c - 1][k : k + 1] - base if c > 0 else jnp.full((1, 128), -1, I32)
            two = ix[2 * c][k : k + 1] - base
            at = jnp.where(((lane128 >> 5) & 1) == 0, one, two)
            tables.append(one_hot(256, at - STARTS[c]))
    c_tables = []
    c_base = (slab - 4) * R2 * NRHS
    group = (lane128 >> 3) & 7
    for k in range(3):
        at = jnp.full((1, 128), -1, I32)
        for m in range(1, 6):
            at = jnp.where(group == m + 1, ix[m][3 + k : 4 + k] - c_base, at)
        c_tables.append(one_hot(64, at))
    halves = [split(p[:D1_AT]) for p in packs]
    coarse = [split(p[A2_AT:]) for p in packs[1:6]]
    return (
        jnp.stack([h[0] for h in halves]),
        jnp.stack([h[1] for h in halves]),
        jnp.stack([h[0] for h in coarse]),
        jnp.stack([h[1] for h in coarse]),
        d1,
        d2,
        jnp.stack(tables),
        jnp.stack(c_tables),
    )


def middle(place, parts, b_hi, b_lo, q_hi, q_lo, d1, d2, tables, c_tables, unpack):
    sub = place[0, 1]
    blocks = (b_hi, b_lo)
    lane128 = iota((1, 128), 1)
    pieces = []
    for x in range(XN):
        w = parts[x]
        for y in range(1, YN):
            w = w + parts[y * XN + x]
        pieces.append(jnp.concatenate([w[:, :64], w[:, 64:]], axis=0))
    g = mm(stacked(jnp.concatenate(pieces, axis=1)), one_hot(256, unpack), NN)
    rhs = g[:64] + g[64:]
    def rows(part, m, start, count):
        return blocks[part][max(m, 0), start : start + count]

    def pair(part, c, start, count):
        return jnp.concatenate(
            [rows(part, 2 * c - 1, start, count), rows(part, 2 * c, start, count)], axis=0
        )

    a_hi = [[pair(0, c, k * 256, 256) for k in range(3)] for c in range(4)]
    a_lo = [[pair(1, c, k * 256, 256) for k in range(3)] for c in range(4)]

    def apply1(v, chunks):
        x = stacked(v)
        return [
            forward(
                a_hi[c], a_lo[c], [gathered(x[:, STARTS[c] : STARTS[c] + 256], tables[3 * c + k]) for k in range(3)], PLAIN_ORDER
            )
            for c in chunks
        ]

    tail = jnp.zeros((64, 128), F32)
    inv = d1[:, :256]
    d = d1 * rhs / CENTER
    y = d[:, :256]
    r = rhs[:, :256] - jnp.concatenate(apply1(d, range(4)), axis=1)
    for t in range(2):
        step = KEEP[t] * d[:, :256] + GAIN[t] * (inv * r)
        d = jnp.concatenate([step, tail], axis=1)
        y = y + step
        r = r - jnp.concatenate(apply1(d, range(4)), axis=1)
    x = stacked(r)
    low = iota((32, 128), 1) < 64
    q_lane = (iota((32, 128), 1) & 63) >> 2
    first = (lane128 & 63) >> 2
    r_hi, r_lo = [], []
    for kk in range(4):
        g = mm(x, one_hot(256, first * 16 + kk * 4 + (lane128 & 3)), NN)
        r_hi.append(jnp.where(low, g[:32], g[32:64]))
        r_lo.append(jnp.where(low, g[64:96], g[96:128]))
    u = jnp.zeros((128, 128), F32)
    for m in range(7):
        keep = [q_lane == 2 * (m + 1) + j // 4 for j in range(R1)]
        b_hi = jnp.concatenate([jnp.where(keep[j], r_hi[j % 4], 0.0) for j in range(R1)], axis=0).astype(BF16)
        b_lo = jnp.concatenate([jnp.where(keep[j], r_lo[j % 4], 0.0) for j in range(R1)], axis=0).astype(BF16)
        p_hi, p_lo = rows(0, m, A1_ROWS, P1_ROWS), rows(1, m, A1_ROWS, P1_ROWS)
        u = u + mm(p_hi, b_hi, TN) + mm(p_hi, b_lo, TN) + mm(p_lo, b_hi, TN)
    r = u[:64, :64] + u[64:, 64:]
    c_hi, c_lo = [], []
    for k in range(3):
        near = [min(max(m - 2, 0), 4) for m in range(8)]
        c_hi.append(jnp.concatenate([q_hi[n, k * 64 : k * 64 + 64] for n in near], axis=0))
        c_lo.append(jnp.concatenate([q_lo[n, k * 64 : k * 64 + 64] for n in near], axis=0))
    d = d2 * r / CENTER
    z = d
    for t in range(3):
        s = stacked(d)
        r = r - forward(c_hi, c_lo, [gathered(s, c_tables[k]) for k in range(3)], PLAIN_ORDER)
        d = KEEP[t] * d + GAIN[t] * (d2 * r)
        z = z + d
    s = stacked(z)
    new = []
    for c in (1, 2):
        at = ((16 * c + ((lane128 & 63) >> 2)) >> 2) * 4 + (lane128 & 3)
        lift = forward(
            [pair(0, c, A1_ROWS, P1_ROWS)], [pair(1, c, A1_ROWS, P1_ROWS)], [gathered(s, one_hot(64, at))], PLAIN_ORDER
        )
        new.append(y[:, c * 64 : c * 64 + 64] + lift)
    y = jnp.concatenate([y[:, :64], new[0], new[1], y[:, 192:256], tail], axis=1)
    side = jnp.zeros((64, 64), F32)

    def at_centre(v):
        return jnp.concatenate([side, v, side, tail], axis=1)

    inv = inv[:, 64:192]
    r = rhs[:, 64:192] - jnp.concatenate(apply1(y, (1, 2)), axis=1)
    d = inv * r / CENTER
    y = y[:, 64:192] + d
    r = r - jnp.concatenate(apply1(at_centre(d), (1, 2)), axis=1)
    d = KEEP[0] * d + GAIN[0] * (inv * r)
    y = y + d
    r = r[:, 64:] - apply1(at_centre(d), (2,))[0]
    own = y[:, 64:] + KEEP[1] * d[:, 64:] + GAIN[1] * (inv[:, 64:] * r)
    pick_rows = (iota((8, 64), 1) == iota((8, 64), 0) + sub * 8).astype(F32).astype(BF16)
    hi, lo = split(own)
    o = mm(pick_rows, hi, NT) + mm(pick_rows, lo, NT)
    o = jnp.concatenate([jnp.concatenate([o[:2], o[4:6]], axis=1), jnp.concatenate([o[2:4], o[6:]], axis=1)], axis=1)
    return (jnp.broadcast_to(o[None], (TN_, 2, 256)),)


def fine_up(rows_ref, odd_ref, all_ref, x_ref, hi_ref, lo_ref, out_ref, line):
    for p in range(32):
        v = all_ref[rows_ref[p]]
        v = jnp.concatenate([v[:, :128], v[:, 128:]], axis=0)
        line[p * 4 : p * 4 + 4, :] = jnp.where(odd_ref[p] == 1, pltpu.roll(v, 64, 1), v)
    w = line[:, :64].T
    hi, lo = split(w)
    hi, lo = hi.astype(F32), lo.astype(F32)
    rights = [
        spread(double(hi[:, e * 64 : e * 64 + 64]), double(lo[:, e * 64 : e * 64 + 64])) for e in range(2)
    ]
    x = x_ref[...] + forward([hi_ref[0], hi_ref[1]], [lo_ref[0], lo_ref[1]], rights, FINE_ORDER)
    out_ref[...] = double(x)


def fine_up_call(rows, odd, gathered_rows, x, hi, lo):
    smem, vmem = pl.BlockSpec(memory_space=pltpu.SMEM), pl.BlockSpec(memory_space=pltpu.VMEM)
    return pl.pallas_call(
        fine_up,
        in_specs=[smem, smem, vmem, vmem, vmem, vmem],
        out_specs=vmem,
        out_shape=jax.ShapeDtypeStruct((64, 128), F32),
        scratch_shapes=[pltpu.VMEM((128, 128), F32)],
        compiler_params=pltpu.CompilerParams(vmem_limit_bytes=48 << 20),
        name="fine_up",
    )(rows, odd, gathered_rows, x, hi, lo)


XY = [[(y * TN_ + t) * XN + x for y in range(YN) for x in range(XN)] for t in range(TN_)]
ZC = [[y * TN_ + t for t in range(TN_)] for y in range(YN)]


def across(value):
    return lax.all_to_all(value, ("slab", "sub"), 0, 0, tiled=True, axis_index_groups=XY)


def along(value):
    return lax.all_to_all(value, "slab", 0, 0, tiled=True, axis_index_groups=ZC)


def shifted(value, axis, by):
    n = lax.axis_size(axis)
    return lax.ppermute(value, axis, [(i, i + by) for i in range(n) if 0 <= i + by < n])


def unpack_table(spot):
    lane = jnp.arange(384, dtype=I32)
    rel, row = lane // 32 - 4, (lane % 32) // 4
    x = (spot + rel) % XN
    part = ((rel >= 0) & (rel < 4)).astype(I32)
    idx = x * 64 + part * 32 + lane % 32
    keep = (rel <= 4) & ((rel < 4) | (row < 4)) & ((rel > -4) | (row >= 4))
    return jnp.where(keep, idx, -1).reshape(1, 384)


def lane_index(columns, times):
    t = columns.T
    v = (t[:, :, None] * NRHS + jnp.arange(NRHS, dtype=I32)).reshape(3, -1)
    return jnp.concatenate([v] * times, axis=1).astype(F32)


def places(values):
    return values.reshape(8, 2, -1).transpose(2, 1, 0).reshape(values.shape[1], 16)


def body(
    right_side,
    warm_start,
    fine_blocks,
    fine_columns,
    fine_prolong,
    owner_rows,
    send_slots,
    receive_rows,
    middle_blocks,
    middle_columns,
    middle_prolong,
    coarse_blocks,
    coarse_columns,
):
    both = ("slab", "sub")
    slab = lax.axis_index("slab").astype(I32)
    sub = lax.axis_index("sub").astype(I32)
    device = (slab * XN + sub).reshape(1, 1)
    place = jnp.stack([slab, sub]).reshape(1, 2)
    rhs4 = jnp.arange(NRHS, dtype=I32)

    g = places(fine_columns)
    g = (g // 16) * 64 + ((g % 2) * 8 + (g % 16) // 2) * 4
    g = (g[:, :, None] + rhs4).reshape(3, 64)
    g = jnp.concatenate([g, g], axis=1).astype(F32)
    own = jnp.concatenate([warm_start, right_side, jnp.pad(g, ((0, 5), (0, 896)))], axis=0)
    blocks = fine_blocks.transpose(1, 0, 2)
    left_blocks, right_blocks = shifted(blocks[:, 8:], both, 1), shifted(blocks[:, :8], both, -1)
    left, right = shifted(own, both, 1), shifted(own, both, -1)

    ix = jnp.concatenate([lane_index(middle_columns, 4), lane_index(coarse_columns, 16)], axis=0)
    (pack,) = kern(
        level_pack,
        [((PACK_ROWS, 128), F32)],
        [middle_blocks.transpose(1, 0, 2), middle_prolong, coarse_blocks.transpose(1, 0, 2), jnp.pad(ix, ((0, 2), (0, 0)))],
    )
    left, right, pack = lax.optimization_barrier((left, right, pack))
    m2, p2 = shifted(pack, "slab", 2), shifted(pack, "slab", -2)
    count = lax.axis_size("slab")
    pairs = [(i, i + 3 if i % 2 else i - 3) for i in range(count)]
    crossed = lax.ppermute(pack[:A2_AT], "slab", [p for p in pairs if 0 <= p[1] < count])
    inverse1 = pack[D1_AT : D1_AT + 64]
    far = [shifted(inverse1, "slab", 4), shifted(inverse1, "slab", -4)]
    p_hi, p_lo = kern(prolong_parts, [((2, 512, 128), BF16)] * 2, [fine_prolong])

    sends = ((64, 128), F32)
    hi, lo, inverse, rhs, x1, send, idx = kern(
        fine_start,
        [((2, 3, 512, 128), BF16)] * 2 + [sends, sends, ((64, 64), F32), sends, ((3, 3, 128), I32)],
        [device, own, left, right, blocks, left_blocks, right_blocks],
        smem=(0,),
    )
    o = places(owner_rows)
    t = (o // 8) % TN_
    dest = ((o // 256) * XN + t % XN) * 64 + (t // XN) * 8 + places(send_slots) * 4
    dest_row = (t // XN) * 32 + (o % 8) * 4 + 1
    dest = jnp.concatenate([(v[:, :, None] + rhs4).reshape(1, 128) for v in (dest, dest_row)], axis=0)
    x3, dense = kern(
        fine_down,
        [((64, 64), F32), ((16, 40, 128), F32)],
        [device, x1, send, shifted(send, both, 1), shifted(send, both, -1), hi, lo, inverse, idx, dest, p_hi, p_lo],
        smem=(0,),
    )

    dense, m2, p2, crossed = lax.optimization_barrier((dense, m2, p2, crossed))
    swap = [(i, i ^ 1) for i in range(count)]
    twins = [lax.ppermute(v, "slab", swap) for v in (pack, m2, p2)]
    prepared = kern(
        middle_prep,
        [((7, D1_AT, 128), BF16)] * 2
        + [((5, A2_ROWS, 128), BF16)] * 2
        + [((64, 384), F32), ((64, 64), F32), ((12, 256, 128), BF16), ((3, 64, 128), BF16)],
        [place, pack, m2, p2, crossed, *twins, *far],
        smem=(0,),
    )

    (part,) = kern(sum_rows, [((TN_, 2, 256), F32)], [across(dense)])
    part, *prepared = lax.optimization_barrier((part, *prepared))
    (part,) = kern(sum_all, [((TN_, 2, 256), F32)], [along(part)])
    q = jnp.arange(XN * YN * 64, dtype=I32)
    spot = slab % TN_
    near_by = (sub - spot) % XN
    row = (q % 32) // 4
    rel = jnp.where((q % 64) // 32 == 1, near_by, near_by - 4)
    rel = jnp.where(((q % 64) // 32 == 0) & (near_by == 0) & (row < 4), 4, rel)
    wanted = (q // 256) * TN_ + spot + rel
    wanted = jnp.where(wanted // TN_ == slab // TN_, (wanted % TN_) // XN * 32 + q % 32, -1)
    wanted = jnp.where(wanted >= 0, wanted, -1)
    (part,) = kern(windows, [((16, 32, 128), F32)], [along(part), wanted.reshape(1, 1024)])
    part = across(part)

    (share,) = kern(
        middle,
        [((TN_, 2, 256), F32)],
        [place, part] + prepared + [unpack_table(slab % TN_)],
        smem=(0,),
    )
    line = along(share)
    every = across(jnp.broadcast_to(line[None], (XN * YN, TN_, 2, 256)))
    at = ((o // 256) * XN + (o % 8) // 2) * TN_ + (o // 8) % TN_
    x = fine_up_call(
        at.reshape(32), (o % 2).reshape(32), every.reshape(XN * YN * TN_, 2, 256), x3, p_hi, p_lo
    )

    x1, send = kern(
        fine_middle,
        [((64, 64), F32), sends],
        [device, x, shifted(x, both, 1), shifted(x, both, -1), rhs, hi, lo, inverse, idx],
        smem=(0,),
    )
    return tuple(
        kern(
            fine_end,
            [((NRHS, 1024), F32)] * 2,
            [device, x1, send, shifted(send, both, 1), shifted(send, both, -1), hi, lo, inverse, idx],
            smem=(0,),
        )
    )


def solution(mesh):
    in_specs = (
        P(None, ("slab", "sub")),
        P(None, ("slab", "sub")),
        P(("slab", "sub"), None, None),
        P(("slab", "sub"), None),
        P(("slab", "sub"), None, None),
        P(("slab", "sub"), None),
        P(("slab", "sub"), None),
        P("slab", "sub", None, None),
        P("slab", None, None),
        P("slab", None),
        P("slab", None),
        P("slab", None, None),
        P("slab", None),
    )
    out_specs = (P(None, ("slab", "sub")), P(None, ("slab", "sub")))
    return jax.shard_map(body, mesh=mesh, in_specs=in_specs, out_specs=out_specs, check_vma=False)
```

```python
import jax
import jax.numpy as jnp
import numpy as np
from jax import lax
from jax.experimental import pallas as pl
from jax.experimental.pallas import tpu as pltpu
from jax.sharding import PartitionSpec as P

F32 = jnp.float32
BF16 = jnp.bfloat16
I32 = jnp.int32
BS = 64
NRHS = 4
R0 = 16
R1 = 8
R2 = 2
XN = 4
YN = 4
TN_ = 32

CENTER = 0.5 * (2.2 + 0.3)
HALF = 0.5 * (2.2 - 0.3)
SCALED = CENTER / HALF
FACTORS = [1.0 / SCALED]
for _ in range(3):
    FACTORS.append(1.0 / (2.0 * SCALED - FACTORS[-1]))
KEEP = [FACTORS[t + 1] * FACTORS[t] for t in range(3)]
GAIN = [2.0 * FACTORS[t + 1] / HALF for t in range(3)]

NN = ((1,), (0,))
NT = ((1,), (1,))
TN = ((0,), (0,))

FINE_ORDER = [(i % 2) * 8 + i // 2 for i in range(R0)]
RIM_ORDER = FINE_ORDER[8:] + FINE_ORDER[:8]
PLAIN_ORDER = list(range(16))


def kern(body, outs, args, smem=()):
    count = len(args)

    def kernel(*refs):
        ins = [r if i in smem else r[...] for i, r in enumerate(refs[:count])]
        for ref, value in zip(refs[count:], body(*ins)):
            ref[...] = value

    specs = [
        pl.BlockSpec(memory_space=pltpu.SMEM if i in smem else pltpu.VMEM) for i in range(count)
    ]
    return pl.pallas_call(
        kernel,
        in_specs=specs,
        out_specs=[pl.BlockSpec(memory_space=pltpu.VMEM) for _ in outs],
        out_shape=[jax.ShapeDtypeStruct(s, d) for s, d in outs],
        compiler_params=pltpu.CompilerParams(vmem_limit_bytes=12 << 20),
        name=body.__name__,
    )(*args)


def mm(a, b, dims):
    return lax.dot_general(a, b, (dims, ((), ())), preferred_element_type=F32)


def iota(shape, dim):
    return lax.broadcasted_iota(I32, shape, dim)


def split(v):
    hi = v.astype(BF16)
    return hi, (v - hi.astype(F32)).astype(BF16)


def stacked(v):
    hi, lo = split(v)
    return jnp.concatenate([hi, lo], axis=0)


def one_hot(size, idx):
    return (iota((size, idx.shape[1]), 0) == idx).astype(F32).astype(BF16)


def lanes_in(x):
    lane = iota(x.shape, 1)
    place = lane & 63
    return jnp.take_along_axis(x, (lane & 64) + 2 * (place & 31) + (place >> 5), axis=1)


def lanes_out(x):
    lane = iota(x.shape, 1)
    b = lane & 63
    return jnp.take_along_axis(x, (lane & 64) + (b & 1) * 32 + (b >> 1), axis=1)


def tiles(raw):
    return lanes_in(raw.reshape(raw.shape[0] * 32, 128))


def double(g):
    return jnp.concatenate([g, g], axis=1)


def spread(hi, lo):
    low = iota(hi.shape, 1) < 64
    zero = jnp.zeros_like(hi)
    top = jnp.concatenate([jnp.where(low, hi, zero), jnp.where(low, lo, zero)], axis=1)
    bottom = jnp.concatenate([jnp.where(low, zero, hi), jnp.where(low, zero, lo)], axis=1)
    return jnp.concatenate([top, bottom], axis=0).astype(BF16)


def gathered(x, table):
    g = mm(x, table, NN)
    return spread(g[:64], g[64:])


def pick(t, order):
    lane = iota((32, 128), 1)
    place = (lane & 63) >> 2
    y = jnp.zeros((32, 128), F32)
    for i in range(16):
        y = y + jnp.where(place == order[i], t[i * 32 : i * 32 + 32], 0.0)
    return jnp.concatenate([y[:, :64], y[:, 64:]], axis=0)


def forward(his, los, rights, order):
    hi = jnp.concatenate(his, axis=1) if len(his) > 1 else his[0]
    lo = jnp.concatenate(los, axis=1) if len(los) > 1 else los[0]
    right = jnp.concatenate(rights, axis=0) if len(rights) > 1 else rights[0]
    a = mm(hi, right, NN)
    return pick(a[:, :128] + a[:, 128:] + mm(lo, right[:, :128], NN), order)


def diagonal(m, order):
    sub = iota(m.shape, 0) & 31
    lane = iota(m.shape, 1)
    kept = jnp.where((lane == sub) | (lane == sub + 96), m, 0.0)
    ones = ((iota((128, 128), 0) >> 6) == (iota((128, 128), 1) >> 6)).astype(F32).astype(BF16)
    hi, lo = split(kept)
    return pick(mm(hi, ones, NN) + mm(lo, ones, NN), order)


def columns_of(rows):
    z = lanes_in(jnp.concatenate([rows[:, m * 128 : m * 128 + 128] for m in range(8)], axis=0))
    t = z.T
    return jnp.concatenate([t[:64], t[64:]], axis=1)


def rows_of(v):
    t = lanes_out(jnp.concatenate([v[:, :32], v[:, 32:]], axis=0).T)
    return jnp.concatenate([t[m * 4 : m * 4 + 4] for m in range(8)], axis=1)


def rim(left, right):
    lane = iota(left.shape, 1)
    return jnp.where((((lane & 63) >> 2) & 7) < 4, right, left)


def fine_tables(device, own, left, right):
    wide, near = [], []
    for k in range(3):
        g = own[k : k + 1]
        r = rim(left[k : k + 1], right[k : k + 1])
        base = (device - 1) * 64
        wide.append([one_hot(192, g - base), one_hot(192, r - base)])
        near.append(one_hot(128, (g & 63) + jnp.where((g >> 6) == device, 0, 64)))
    return wide, near


def fine_both(hi, lo, x, wide):
    return jnp.concatenate(
        [
            forward(
                [hi[c, k] for k in range(3)],
                [lo[c, k] for k in range(3)],
                [gathered(x, wide[k][c]) for k in range(3)],
                (FINE_ORDER, RIM_ORDER)[c],
            )
            for c in range(2)
        ],
        axis=1,
    )


def fine_own(hi, lo, x, near):
    return forward(
        [hi[0, k] for k in range(3)],
        [lo[0, k] for k in range(3)],
        [gathered(x, near[k]) for k in range(3)],
        FINE_ORDER,
    )


def first_passes(device, x, sides, rhs, hi, lo, inverse, idx):
    wide, near = fine_tables(device, *idx)
    window = stacked(jnp.concatenate([sides[0], x, sides[1]], axis=1))
    r = rhs - fine_both(hi, lo, window, wide)
    d = inverse * r / CENTER
    r1 = r[:, :64] - fine_own(hi, lo, stacked(d), near)
    d1 = d[:, :64]
    d2 = KEEP[0] * d1 + GAIN[0] * (inverse[:, :64] * r1)
    return x + d1, jnp.concatenate([d2, r1], axis=1)


def last_passes(device, x, own, left, right, hi, lo, inverse, idx):
    wide, near = fine_tables(device, *idx)
    window = stacked(jnp.concatenate([left[:, :64], own[:, :64], right[:, :64]], axis=1))
    rims = rim(jnp.concatenate([left[:, 64:]] * 2, axis=1), jnp.concatenate([right[:, 64:]] * 2, axis=1))
    rim_d = rim(double(left[:, :64]), double(right[:, :64]))
    r = jnp.concatenate([own[:, 64:], rims[:, :64]], axis=1) - fine_both(hi, lo, window, wide)
    d_old = jnp.concatenate([own[:, :64], rim_d[:, :64]], axis=1)
    d = KEEP[1] * d_old + GAIN[1] * (inverse * r)
    residual = r[:, :64] - fine_own(hi, lo, stacked(d), near)
    return x + own[:, :64] + d[:, :64], residual


def indices(payload):
    return payload[:3, 1024:1152].astype(I32)


def fine_start(device, own, left_all, right_all, own_blocks):
    parts = []
    for k in range(3):
        parts.append(tiles(own_blocks[k]))
    for k in range(3):
        parts.append(jnp.concatenate([tiles(left_all[k]), tiles(right_all[k])], axis=0))
    left, right = left_all[3], right_all[3]
    entries = jnp.concatenate([diagonal(parts[0], FINE_ORDER), diagonal(parts[3], RIM_ORDER)], axis=1)
    inverse = jnp.where(entries == 0.0, 0.0, 1.0 / entries)
    pairs = [split(p) for p in parts]
    hi = jnp.stack([p[0] for p in pairs]).reshape(2, 3, 512, 128)
    lo = jnp.stack([p[1] for p in pairs]).reshape(2, 3, 512, 128)
    x = [columns_of(p[:4, :1024]) for p in (left, own, right)]
    b = [columns_of(p[4:, :1024]) for p in (left, own, right)]
    rhs = jnp.concatenate([b[1], rim(b[0], b[2])], axis=1)
    idx = [indices(p) for p in (own, left, right)]
    x1, send = first_passes(device[0, 0], x[1], (x[0], x[2]), rhs, hi, lo, inverse, idx)
    return hi, lo, inverse, rhs, x1, send, jnp.stack(idx)


def restrict(dest, residual, p_hi, p_lo):
    both = jnp.concatenate([residual[:32], residual[32:]], axis=1)
    place = (iota((32, 128), 1) & 63) >> 2
    hi, lo = split(both)
    hi, lo = hi.astype(F32), lo.astype(F32)
    r_hi = jnp.concatenate([jnp.where(place == FINE_ORDER[i], hi, 0.0) for i in range(16)], axis=0).astype(BF16)
    r_lo = jnp.concatenate([jnp.where(place == FINE_ORDER[i], lo, 0.0) for i in range(16)], axis=0).astype(BF16)
    pieces = []
    for e in range(2):
        u = mm(p_hi[e], r_hi, TN) + mm(p_hi[e], r_lo, TN) + mm(p_lo[e], r_hi, TN)
        pieces.append(u[:64, :64] + u[64:, 64:])
    hi, lo = split(jnp.concatenate(pieces, axis=1))
    rows = jnp.broadcast_to(dest[1:2].astype(F32), (16, 128)).astype(BF16)
    x = jnp.concatenate([hi, lo, rows], axis=0)
    out = []
    for q in range(0, XN * YN, 2):
        table = (iota((128, 128), 0) + q * 64 == dest[:1]).astype(F32).astype(BF16)
        g = mm(x, table, NT)
        v, at = g[:64] + g[64:128], g[128:136]
        out.append(jnp.concatenate([jnp.concatenate([v[:32, :64], v[32:, :64]], axis=1), at], axis=0))
        at = jnp.concatenate([at[:, 64:], at[:, :64]], axis=1)
        out.append(jnp.concatenate([jnp.concatenate([v[:32, 64:], v[32:, 64:]], axis=1), at], axis=0))
    return jnp.stack(out)


def fine_down(device, x, own, left, right, hi, lo, inverse, idx, dest, p_hi, p_lo):
    solution, residual = last_passes(
        device[0, 0], x, own, left, right, hi, lo, inverse, [idx[i] for i in range(3)]
    )
    return solution, restrict(dest, residual, p_hi, p_lo)


def fine_middle(device, x, left, right, rhs, hi, lo, inverse, idx):
    sides = (left[:, :64], right[:, :64])
    x1, send = first_passes(
        device[0, 0], x[:, :64], sides, rhs, hi, lo, inverse, [idx[i] for i in range(3)]
    )
    return x1, send


def fine_end(device, x, own, left, right, hi, lo, inverse, idx):
    solution, residual = last_passes(
        device[0, 0], x, own, left, right, hi, lo, inverse, [idx[i] for i in range(3)]
    )
    return rows_of(solution), rows_of(residual)


def prolong_parts(blocks):
    parts = [split(tiles(blocks[:, e, :])) for e in range(2)]
    return jnp.stack([p[0] for p in parts]), jnp.stack([p[1] for p in parts])


def sum_rows(parts):
    total = jnp.zeros((128, 256), F32)
    for q in range(0, XN * YN, 2):
        v = jnp.concatenate(
            [jnp.concatenate([parts[q + i, :32, :64], parts[q + i, :32, 64:]], axis=0) for i in range(2)], axis=1
        )
        at = jnp.concatenate([parts[q + i, 32:33, :64] for i in range(2)], axis=1).astype(I32)
        table = (iota((256, 128), 0) + 1 == at).astype(F32).astype(BF16)
        total = total + mm(stacked(v), table, NT)
    total = total[:64] + total[64:]
    return (jnp.stack([total[2 * t : 2 * t + 2] for t in range(TN_)]),)


def sum_all(parts):
    return (jnp.broadcast_to(jnp.sum(parts, axis=0)[None], parts.shape),)


def windows(parts, idx):
    x = stacked(jnp.concatenate([parts[t] for t in range(TN_)], axis=0))
    out = []
    for q in range(XN * YN):
        half = idx[:, (q // 2) * 128 : (q // 2) * 128 + 128]
        if q % 2 == 0:
            g = mm(x, one_hot(256, half), NN)
            g = g[:64] + g[64:]
        v = g[:, (q % 2) * 64 : (q % 2) * 64 + 64]
        out.append(jnp.concatenate([v[:32], v[32:]], axis=1))
    return (jnp.stack(out),)


A1_ROWS = 3 * R1 * 32
P1_ROWS = R1 * 32
A2_ROWS = 3 * R2 * 32
D1_AT = A1_ROWS + P1_ROWS
D2_AT = D1_AT + 64
IX_AT = D2_AT + 64
A2_AT = IX_AT + 8
PACK_ROWS = A2_AT + A2_ROWS


def level_pack(blocks, prolong, coarse, idx):
    a1 = [tiles(blocks[k]) for k in range(3)]
    a2 = [lanes_in(coarse[k].reshape(R2 * 32, 128)) for k in range(3)]
    pad = jnp.zeros((256, 128), F32)
    d1 = 1.0 / diagonal_plain(jnp.concatenate([a1[0], pad], axis=0))[:, :32]
    pad = jnp.zeros((448, 128), F32)
    d2 = 1.0 / diagonal_plain(jnp.concatenate([a2[0], pad], axis=0))[:, :8]
    return (
        jnp.concatenate(
            a1
            + [tiles(prolong)]
            + [jnp.concatenate([d1] * 4, axis=1), jnp.concatenate([d2] * 16, axis=1), idx]
            + a2,
            axis=0,
        ),
    )


def diagonal_plain(m):
    return diagonal(m, PLAIN_ORDER)


STARTS = [0, 0, 0, 128]


def middle_prep(place, p0, m2, p2, crossed, swapped, far):
    slab = place[0, 0]
    even = (slab & 1) == 0
    top = A2_AT
    twin, twin_m2, twin_p2 = (swapped[i * PACK_ROWS : (i + 1) * PACK_ROWS] for i in range(3))
    far_twin = swapped[3 * PACK_ROWS :]
    far_low = jnp.where(even, far, far_twin)
    far_high = jnp.where(even, far_twin, far)
    m3 = jnp.where(even, crossed, twin_m2[:top])
    p3 = jnp.where(even, twin_p2[:top], crossed)
    m1 = jnp.where(even, twin_m2, twin)
    p1 = jnp.where(even, twin, twin_p2)
    packs = [m3, m2, m1, p0, p1, p2, p3]
    lane128 = iota((1, 128), 1)
    quarter = iota((64, 128), 1) >> 5
    tiled = [far_low] + [p[D1_AT : D1_AT + 64] for p in packs] + [far_high]
    d1 = []
    for q in range(3):
        v = jnp.zeros((64, 128), F32)
        for m in range(4):
            if q * 4 + m < 9:
                v = jnp.where(quarter == m, tiled[q * 4 + m], v)
        d1.append(v)
    d1 = jnp.concatenate(d1, axis=1)
    eighth = (iota((64, 128), 1) >> 3) & 7
    d2 = jnp.zeros((64, 128), F32)
    for m in range(7):
        d2 = jnp.where(eighth == m + 1, packs[m][D2_AT : D2_AT + 64], d2)
    d2 = d2[:, :64]
    ix = [p[IX_AT : IX_AT + 8].astype(I32) for p in packs]
    base = (slab - 4) * R1 * NRHS
    tables = []
    for c in range(4):
        for k in range(3):
            one = ix[2 * c - 1][k : k + 1] - base if c > 0 else jnp.full((1, 128), -1, I32)
            two = ix[2 * c][k : k + 1] - base
            at = jnp.where(((lane128 >> 5) & 1) == 0, one, two)
            tables.append(one_hot(256, at - STARTS[c]))
    c_tables = []
    c_base = (slab - 4) * R2 * NRHS
    group = (lane128 >> 3) & 7
    for k in range(3):
        at = jnp.full((1, 128), -1, I32)
        for m in range(1, 6):
            at = jnp.where(group == m + 1, ix[m][3 + k : 4 + k] - c_base, at)
        c_tables.append(one_hot(64, at))
    halves = [split(p[:D1_AT]) for p in packs]
    coarse = [split(p[A2_AT:]) for p in packs[1:6]]
    return (
        jnp.stack([h[0] for h in halves]),
        jnp.stack([h[1] for h in halves]),
        jnp.stack([h[0] for h in coarse]),
        jnp.stack([h[1] for h in coarse]),
        d1,
        d2,
        jnp.stack(tables),
        jnp.stack(c_tables),
    )


def middle(place, parts, b_hi, b_lo, q_hi, q_lo, d1, d2, tables, c_tables, unpack):
    sub = place[0, 1]
    blocks = (b_hi, b_lo)
    lane128 = iota((1, 128), 1)
    pieces = []
    for x in range(XN):
        w = parts[x]
        for y in range(1, YN):
            w = w + parts[y * XN + x]
        pieces.append(jnp.concatenate([w[:, :64], w[:, 64:]], axis=0))
    g = mm(stacked(jnp.concatenate(pieces, axis=1)), one_hot(256, unpack), NN)
    rhs = g[:64] + g[64:]
    def rows(part, m, start, count):
        return blocks[part][max(m, 0), start : start + count]

    def pair(part, c, start, count):
        return jnp.concatenate(
            [rows(part, 2 * c - 1, start, count), rows(part, 2 * c, start, count)], axis=0
        )

    a_hi = [[pair(0, c, k * 256, 256) for k in range(3)] for c in range(4)]
    a_lo = [[pair(1, c, k * 256, 256) for k in range(3)] for c in range(4)]

    def apply1(v, chunks):
        x = stacked(v)
        return [
            forward(
                a_hi[c], a_lo[c], [gathered(x[:, STARTS[c] : STARTS[c] + 256], tables[3 * c + k]) for k in range(3)], PLAIN_ORDER
            )
            for c in chunks
        ]

    tail = jnp.zeros((64, 128), F32)
    inv = d1[:, :256]
    d = d1 * rhs / CENTER
    y = d[:, :256]
    r = rhs[:, :256] - jnp.concatenate(apply1(d, range(4)), axis=1)
    for t in range(2):
        step = KEEP[t] * d[:, :256] + GAIN[t] * (inv * r)
        d = jnp.concatenate([step, tail], axis=1)
        y = y + step
        r = r - jnp.concatenate(apply1(d, range(4)), axis=1)
    x = stacked(r)
    low = iota((32, 128), 1) < 64
    q_lane = (iota((32, 128), 1) & 63) >> 2
    first = (lane128 & 63) >> 2
    r_hi, r_lo = [], []
    for kk in range(4):
        g = mm(x, one_hot(256, first * 16 + kk * 4 + (lane128 & 3)), NN)
        r_hi.append(jnp.where(low, g[:32], g[32:64]))
        r_lo.append(jnp.where(low, g[64:96], g[96:128]))
    u = jnp.zeros((128, 128), F32)
    for m in range(7):
        keep = [q_lane == 2 * (m + 1) + j // 4 for j in range(R1)]
        b_hi = jnp.concatenate([jnp.where(keep[j], r_hi[j % 4], 0.0) for j in range(R1)], axis=0).astype(BF16)
        b_lo = jnp.concatenate([jnp.where(keep[j], r_lo[j % 4], 0.0) for j in range(R1)], axis=0).astype(BF16)
        p_hi, p_lo = rows(0, m, A1_ROWS, P1_ROWS), rows(1, m, A1_ROWS, P1_ROWS)
        u = u + mm(p_hi, b_hi, TN) + mm(p_hi, b_lo, TN) + mm(p_lo, b_hi, TN)
    r = u[:64, :64] + u[64:, 64:]
    c_hi, c_lo = [], []
    for k in range(3):
        near = [min(max(m - 2, 0), 4) for m in range(8)]
        c_hi.append(jnp.concatenate([q_hi[n, k * 64 : k * 64 + 64] for n in near], axis=0))
        c_lo.append(jnp.concatenate([q_lo[n, k * 64 : k * 64 + 64] for n in near], axis=0))
    d = d2 * r / CENTER
    z = d
    for t in range(3):
        s = stacked(d)
        r = r - forward(c_hi, c_lo, [gathered(s, c_tables[k]) for k in range(3)], PLAIN_ORDER)
        d = KEEP[t] * d + GAIN[t] * (d2 * r)
        z = z + d
    s = stacked(z)
    new = []
    for c in (1, 2):
        at = ((16 * c + ((lane128 & 63) >> 2)) >> 2) * 4 + (lane128 & 3)
        lift = forward(
            [pair(0, c, A1_ROWS, P1_ROWS)], [pair(1, c, A1_ROWS, P1_ROWS)], [gathered(s, one_hot(64, at))], PLAIN_ORDER
        )
        new.append(y[:, c * 64 : c * 64 + 64] + lift)
    y = jnp.concatenate([y[:, :64], new[0], new[1], y[:, 192:256], tail], axis=1)
    side = jnp.zeros((64, 64), F32)

    def at_centre(v):
        return jnp.concatenate([side, v, side, tail], axis=1)

    inv = inv[:, 64:192]
    r = rhs[:, 64:192] - jnp.concatenate(apply1(y, (1, 2)), axis=1)
    d = inv * r / CENTER
    y = y[:, 64:192] + d
    r = r - jnp.concatenate(apply1(at_centre(d), (1, 2)), axis=1)
    d = KEEP[0] * d + GAIN[0] * (inv * r)
    y = y + d
    r = r[:, 64:] - apply1(at_centre(d), (2,))[0]
    own = y[:, 64:] + KEEP[1] * d[:, 64:] + GAIN[1] * (inv[:, 64:] * r)
    pick_rows = (iota((8, 64), 1) == iota((8, 64), 0) + sub * 8).astype(F32).astype(BF16)
    hi, lo = split(own)
    o = mm(pick_rows, hi, NT) + mm(pick_rows, lo, NT)
    o = jnp.concatenate([jnp.concatenate([o[:2], o[4:6]], axis=1), jnp.concatenate([o[2:4], o[6:]], axis=1)], axis=1)
    return (jnp.broadcast_to(o[None], (TN_, 2, 256)),)


def fine_up(rows_ref, odd_ref, all_ref, x_ref, hi_ref, lo_ref, out_ref, line):
    for p in range(32):
        v = all_ref[rows_ref[p]]
        v = jnp.concatenate([v[:, :128], v[:, 128:]], axis=0)
        line[p * 4 : p * 4 + 4, :] = jnp.where(odd_ref[p] == 1, pltpu.roll(v, 64, 1), v)
    w = line[:, :64].T
    hi, lo = split(w)
    hi, lo = hi.astype(F32), lo.astype(F32)
    rights = [
        spread(double(hi[:, e * 64 : e * 64 + 64]), double(lo[:, e * 64 : e * 64 + 64])) for e in range(2)
    ]
    x = x_ref[...] + forward([hi_ref[0], hi_ref[1]], [lo_ref[0], lo_ref[1]], rights, FINE_ORDER)
    out_ref[...] = double(x)


def fine_up_call(rows, odd, gathered_rows, x, hi, lo):
    smem, vmem = pl.BlockSpec(memory_space=pltpu.SMEM), pl.BlockSpec(memory_space=pltpu.VMEM)
    return pl.pallas_call(
        fine_up,
        in_specs=[smem, smem, vmem, vmem, vmem, vmem],
        out_specs=vmem,
        out_shape=jax.ShapeDtypeStruct((64, 128), F32),
        scratch_shapes=[pltpu.VMEM((128, 128), F32)],
        compiler_params=pltpu.CompilerParams(vmem_limit_bytes=12 << 20),
        name="fine_up",
    )(rows, odd, gathered_rows, x, hi, lo)


XY = [[(y * TN_ + t) * XN + x for y in range(YN) for x in range(XN)] for t in range(TN_)]
ZC = [[y * TN_ + t for t in range(TN_)] for y in range(YN)]


def across(value):
    return lax.all_to_all(value, ("slab", "sub"), 0, 0, tiled=True, axis_index_groups=XY)


def along(value):
    return lax.all_to_all(value, "slab", 0, 0, tiled=True, axis_index_groups=ZC)


def shifted(value, axis, by):
    n = lax.axis_size(axis)
    return lax.ppermute(value, axis, [(i, i + by) for i in range(n) if 0 <= i + by < n])


def unpack_table(spot):
    lane = jnp.arange(384, dtype=I32)
    rel, row = lane // 32 - 4, (lane % 32) // 4
    x = (spot + rel) % XN
    part = ((rel >= 0) & (rel < 4)).astype(I32)
    idx = x * 64 + part * 32 + lane % 32
    keep = (rel <= 4) & ((rel < 4) | (row < 4)) & ((rel > -4) | (row >= 4))
    return jnp.where(keep, idx, -1).reshape(1, 384)


def lane_index(columns, times):
    t = columns.T
    v = (t[:, :, None] * NRHS + jnp.arange(NRHS, dtype=I32)).reshape(3, -1)
    return jnp.concatenate([v] * times, axis=1).astype(F32)


def places(values):
    return values.reshape(8, 2, -1).transpose(2, 1, 0).reshape(values.shape[1], 16)


def body(
    right_side,
    warm_start,
    fine_blocks,
    fine_columns,
    fine_prolong,
    owner_rows,
    send_slots,
    receive_rows,
    middle_blocks,
    middle_columns,
    middle_prolong,
    coarse_blocks,
    coarse_columns,
):
    both = ("slab", "sub")
    slab = lax.axis_index("slab").astype(I32)
    sub = lax.axis_index("sub").astype(I32)
    device = (slab * XN + sub).reshape(1, 1)
    place = jnp.stack([slab, sub]).reshape(1, 2)
    rhs4 = jnp.arange(NRHS, dtype=I32)

    g = places(fine_columns)
    g = (g // 16) * 64 + ((g % 2) * 8 + (g % 16) // 2) * 4
    g = (g[:, :, None] + rhs4).reshape(3, 64)
    g = jnp.concatenate([g, g], axis=1).astype(F32)
    own = jnp.concatenate([warm_start, right_side], axis=0)
    own = jnp.concatenate([own, jnp.pad(g, ((0, 5), (0, 2944)))], axis=1)
    blocks = fine_blocks.transpose(1, 0, 2)
    low, high = (
        jnp.concatenate([part, own[None]], axis=0) for part in (blocks[:, :8], blocks[:, 8:])
    )

    ix = jnp.concatenate([lane_index(middle_columns, 4), lane_index(coarse_columns, 16)], axis=0)
    ix, low, high = lax.optimization_barrier((ix, low, high))
    left, right = shifted(high, both, 1), shifted(low, both, -1)
    (pack,) = kern(
        level_pack,
        [((PACK_ROWS, 128), F32)],
        [middle_blocks.transpose(1, 0, 2), middle_prolong, coarse_blocks.transpose(1, 0, 2), jnp.pad(ix, ((0, 2), (0, 0)))],
    )
    p_hi, p_lo = kern(prolong_parts, [((2, 512, 128), BF16)] * 2, [fine_prolong])

    sends = ((64, 128), F32)
    hi, lo, inverse, rhs, x1, send, idx = kern(
        fine_start,
        [((2, 3, 512, 128), BF16)] * 2 + [sends, sends, ((64, 64), F32), sends, ((3, 3, 128), I32)],
        [device, own, left, right, blocks],
        smem=(0,),
    )
    send, pack = lax.optimization_barrier((send, pack))
    count = lax.axis_size("slab")
    m2, p2 = shifted(pack, "slab", 2), shifted(pack, "slab", -2)

    def crossing(value, by):
        pairs = [(i, i + by if i % 2 == by % 2 else i - by) for i in range(count)]
        return lax.ppermute(value, "slab", [p for p in pairs if 0 <= p[1] < count])

    crossed = crossing(pack[:A2_AT], 3)
    far = crossing(pack[D1_AT : D1_AT + 64], 4)
    o = places(owner_rows)
    t = (o // 8) % TN_
    dest = ((o // 256) * XN + t % XN) * 64 + (t // XN) * 8 + places(send_slots) * 4
    dest_row = (t // XN) * 32 + (o % 8) * 4 + 1
    dest = jnp.concatenate([(v[:, :, None] + rhs4).reshape(1, 128) for v in (dest, dest_row)], axis=0)
    x3, dense = kern(
        fine_down,
        [((64, 64), F32), ((16, 40, 128), F32)],
        [device, x1, send, shifted(send, both, 1), shifted(send, both, -1), hi, lo, inverse, idx, dest, p_hi, p_lo],
        smem=(0,),
    )

    (part,) = kern(sum_rows, [((TN_, 2, 256), F32)], [across(dense)])
    part, m2, p2, crossed, far = lax.optimization_barrier((part, m2, p2, crossed, far))
    twin = jnp.concatenate([pack, m2, p2, crossed[D1_AT : D1_AT + 64]], axis=0)
    twin = lax.ppermute(twin, "slab", [(i, i ^ 1) for i in range(count)])
    prepared = kern(
        middle_prep,
        [((7, D1_AT, 128), BF16)] * 2
        + [((5, A2_ROWS, 128), BF16)] * 2
        + [((64, 384), F32), ((64, 64), F32), ((12, 256, 128), BF16), ((3, 64, 128), BF16)],
        [place, pack, m2, p2, crossed, twin, far],
        smem=(0,),
    )
    (part,) = kern(sum_all, [((TN_, 2, 256), F32)], [along(part)])
    q = jnp.arange(XN * YN * 64, dtype=I32)
    spot = slab % TN_
    near_by = (sub - spot) % XN
    row = (q % 32) // 4
    rel = jnp.where((q % 64) // 32 == 1, near_by, near_by - 4)
    rel = jnp.where(((q % 64) // 32 == 0) & (near_by == 0) & (row < 4), 4, rel)
    wanted = (q // 256) * TN_ + spot + rel
    wanted = jnp.where(wanted // TN_ == slab // TN_, (wanted % TN_) // XN * 32 + q % 32, -1)
    wanted = jnp.where(wanted >= 0, wanted, -1)
    (part,) = kern(windows, [((16, 32, 128), F32)], [along(part), wanted.reshape(1, 1024)])
    part = across(part)

    (share,) = kern(
        middle,
        [((TN_, 2, 256), F32)],
        [place, part] + list(prepared) + [unpack_table(slab % TN_)],
        smem=(0,),
    )
    line = along(share)
    every = across(jnp.broadcast_to(line[None], (XN * YN, TN_, 2, 256)))
    at = ((o // 256) * XN + (o % 8) // 2) * TN_ + (o // 8) % TN_
    x = fine_up_call(
        at.reshape(32), (o % 2).reshape(32), every.reshape(XN * YN * TN_, 2, 256), x3, p_hi, p_lo
    )

    x1, send = kern(
        fine_middle,
        [((64, 64), F32), sends],
        [device, x, shifted(x, both, 1), shifted(x, both, -1), rhs, hi, lo, inverse, idx],
        smem=(0,),
    )
    return tuple(
        kern(
            fine_end,
            [((NRHS, 1024), F32)] * 2,
            [device, x1, send, shifted(send, both, 1), shifted(send, both, -1), hi, lo, inverse, idx],
            smem=(0,),
        )
    )


def solution(mesh):
    in_specs = (
        P(None, ("slab", "sub")),
        P(None, ("slab", "sub")),
        P(("slab", "sub"), None, None),
        P(("slab", "sub"), None),
        P(("slab", "sub"), None, None),
        P(("slab", "sub"), None),
        P(("slab", "sub"), None),
        P("slab", "sub", None, None),
        P("slab", None, None),
        P("slab", None),
        P("slab", None),
        P("slab", None, None),
        P("slab", None),
    )
    out_specs = (P(None, ("slab", "sub")), P(None, ("slab", "sub")))
    return jax.shard_map(body, mesh=mesh, in_specs=in_specs, out_specs=out_specs, check_vma=False)
```

```python
import jax
import jax.numpy as jnp
import numpy as np
from jax import lax
from jax.experimental import pallas as pl
from jax.experimental.pallas import tpu as pltpu
from jax.sharding import PartitionSpec as P

F32 = jnp.float32
BF16 = jnp.bfloat16
I32 = jnp.int32
BS = 64
NRHS = 4
R0 = 16
R1 = 8
R2 = 2
XN = 4
YN = 4
TN_ = 32

CENTER = 0.5 * (2.2 + 0.3)
HALF = 0.5 * (2.2 - 0.3)
SCALED = CENTER / HALF
FACTORS = [1.0 / SCALED]
for _ in range(3):
    FACTORS.append(1.0 / (2.0 * SCALED - FACTORS[-1]))
KEEP = [FACTORS[t + 1] * FACTORS[t] for t in range(3)]
GAIN = [2.0 * FACTORS[t + 1] / HALF for t in range(3)]

NN = ((1,), (0,))
NT = ((1,), (1,))
TN = ((0,), (0,))

FINE_ORDER = [(i % 2) * 8 + i // 2 for i in range(R0)]
RIM_ORDER = FINE_ORDER[8:] + FINE_ORDER[:8]
PLAIN_ORDER = list(range(16))


def kern(body, outs, args, smem=(), own=(), own_outs=False):
    count = len(args)

    def kernel(*refs):
        ins = [r if i in smem else r[...] for i, r in enumerate(refs[:count])]
        for ref, value in zip(refs[count:], body(*ins)):
            ref[...] = value

    vmem = pl.BlockSpec(memory_space=pltpu.VMEM)
    specs = [
        pl.BlockSpec(memory_space=pltpu.SMEM) if i in smem else pl.BlockSpec() if i in own else vmem
        for i in range(count)
    ]
    return pl.pallas_call(
        kernel,
        in_specs=specs,
        out_specs=[pl.BlockSpec() if own_outs else vmem for _ in outs],
        out_shape=[jax.ShapeDtypeStruct(s, d) for s, d in outs],
        compiler_params=pltpu.CompilerParams(vmem_limit_bytes=32 << 20),
        name=body.__name__,
    )(*args)


def mm(a, b, dims):
    return lax.dot_general(a, b, (dims, ((), ())), preferred_element_type=F32)


def iota(shape, dim):
    return lax.broadcasted_iota(I32, shape, dim)


def split(v):
    hi = v.astype(BF16)
    return hi, (v - hi.astype(F32)).astype(BF16)


def stacked(v):
    hi, lo = split(v)
    return jnp.concatenate([hi, lo], axis=0)


def one_hot(size, idx):
    return (iota((size, idx.shape[1]), 0) == idx).astype(F32).astype(BF16)


def lanes_in(x):
    lane = iota(x.shape, 1)
    place = lane & 63
    return jnp.take_along_axis(x, (lane & 64) + 2 * (place & 31) + (place >> 5), axis=1)


def lanes_out(x):
    lane = iota(x.shape, 1)
    b = lane & 63
    return jnp.take_along_axis(x, (lane & 64) + (b & 1) * 32 + (b >> 1), axis=1)


def tiles(raw):
    return lanes_in(raw.reshape(raw.shape[0] * 32, 128))


def double(g):
    return jnp.concatenate([g, g], axis=1)


def spread(hi, lo):
    low = iota(hi.shape, 1) < 64
    zero = jnp.zeros_like(hi)
    top = jnp.concatenate([jnp.where(low, hi, zero), jnp.where(low, lo, zero)], axis=1)
    bottom = jnp.concatenate([jnp.where(low, zero, hi), jnp.where(low, zero, lo)], axis=1)
    return jnp.concatenate([top, bottom], axis=0).astype(BF16)


def gathered(x, table):
    g = mm(x, table, NN)
    return spread(g[:64], g[64:])


def pick(t, order):
    lane = iota((32, 128), 1)
    place = (lane & 63) >> 2
    y = jnp.zeros((32, 128), F32)
    for i in range(16):
        y = y + jnp.where(place == order[i], t[i * 32 : i * 32 + 32], 0.0)
    return jnp.concatenate([y[:, :64], y[:, 64:]], axis=0)


def forward(his, los, rights, order):
    hi = jnp.concatenate(his, axis=1) if len(his) > 1 else his[0]
    lo = jnp.concatenate(los, axis=1) if len(los) > 1 else los[0]
    right = jnp.concatenate(rights, axis=0) if len(rights) > 1 else rights[0]
    a = mm(hi, right, NN)
    return pick(a[:, :128] + a[:, 128:] + mm(lo, right[:, :128], NN), order)


def diagonal(m, order):
    sub = iota(m.shape, 0) & 31
    lane = iota(m.shape, 1)
    kept = jnp.where((lane == sub) | (lane == sub + 96), m, 0.0)
    ones = ((iota((128, 128), 0) >> 6) == (iota((128, 128), 1) >> 6)).astype(F32).astype(BF16)
    hi, lo = split(kept)
    return pick(mm(hi, ones, NN) + mm(lo, ones, NN), order)


def columns_of(rows):
    z = lanes_in(jnp.concatenate([rows[:, m * 128 : m * 128 + 128] for m in range(8)], axis=0))
    t = z.T
    return jnp.concatenate([t[:64], t[64:]], axis=1)


def rows_of(v):
    t = lanes_out(jnp.concatenate([v[:, :32], v[:, 32:]], axis=0).T)
    return jnp.concatenate([t[m * 4 : m * 4 + 4] for m in range(8)], axis=1)


def rim(left, right):
    lane = iota(left.shape, 1)
    return jnp.where((((lane & 63) >> 2) & 7) < 4, right, left)


def fine_tables(device, own, left, right):
    wide, near = [], []
    for k in range(3):
        g = own[k : k + 1]
        r = rim(left[k : k + 1], right[k : k + 1])
        base = (device - 1) * 64
        wide.append([one_hot(192, g - base), one_hot(192, r - base)])
        near.append(one_hot(128, (g & 63) + jnp.where((g >> 6) == device, 0, 64)))
    return wide, near


def fine_both(hi, lo, x, wide):
    return jnp.concatenate(
        [
            forward(
                [hi[c, k] for k in range(3)],
                [lo[c, k] for k in range(3)],
                [gathered(x, wide[k][c]) for k in range(3)],
                (FINE_ORDER, RIM_ORDER)[c],
            )
            for c in range(2)
        ],
        axis=1,
    )


def fine_own(hi, lo, x, near):
    return forward(
        [hi[0, k] for k in range(3)],
        [lo[0, k] for k in range(3)],
        [gathered(x, near[k]) for k in range(3)],
        FINE_ORDER,
    )


def first_passes(device, x, sides, rhs, hi, lo, inverse, idx):
    wide, near = fine_tables(device, *idx)
    window = stacked(jnp.concatenate([sides[0], x, sides[1]], axis=1))
    r = rhs - fine_both(hi, lo, window, wide)
    d = inverse * r / CENTER
    r1 = r[:, :64] - fine_own(hi, lo, stacked(d), near)
    d1 = d[:, :64]
    d2 = KEEP[0] * d1 + GAIN[0] * (inverse[:, :64] * r1)
    return x + d1, jnp.concatenate([d2, r1], axis=1)


def last_passes(device, x, own, left, right, hi, lo, inverse, idx):
    wide, near = fine_tables(device, *idx)
    window = stacked(jnp.concatenate([left[:, :64], own[:, :64], right[:, :64]], axis=1))
    rims = rim(jnp.concatenate([left[:, 64:]] * 2, axis=1), jnp.concatenate([right[:, 64:]] * 2, axis=1))
    rim_d = rim(double(left[:, :64]), double(right[:, :64]))
    r = jnp.concatenate([own[:, 64:], rims[:, :64]], axis=1) - fine_both(hi, lo, window, wide)
    d_old = jnp.concatenate([own[:, :64], rim_d[:, :64]], axis=1)
    d = KEEP[1] * d_old + GAIN[1] * (inverse * r)
    residual = r[:, :64] - fine_own(hi, lo, stacked(d), near)
    return x + own[:, :64] + d[:, :64], residual


def indices(payload):
    return payload[8:11, :128].astype(I32)


def fine_start(device, own, left, right, own_blocks, left_blocks, right_blocks):
    parts = []
    for k in range(3):
        parts.append(tiles(own_blocks[k]))
    for k in range(3):
        parts.append(jnp.concatenate([tiles(left_blocks[k]), tiles(right_blocks[k])], axis=0))
    entries = jnp.concatenate([diagonal(parts[0], FINE_ORDER), diagonal(parts[3], RIM_ORDER)], axis=1)
    inverse = jnp.where(entries == 0.0, 0.0, 1.0 / entries)
    pairs = [split(p) for p in parts]
    hi = jnp.stack([p[0] for p in pairs]).reshape(2, 3, 512, 128)
    lo = jnp.stack([p[1] for p in pairs]).reshape(2, 3, 512, 128)
    x = [columns_of(p[:4]) for p in (left, own, right)]
    b = [columns_of(p[4:8]) for p in (left, own, right)]
    rhs = jnp.concatenate([b[1], rim(b[0], b[2])], axis=1)
    idx = [indices(p) for p in (own, left, right)]
    x1, send = first_passes(device[0, 0], x[1], (x[0], x[2]), rhs, hi, lo, inverse, idx)
    return hi, lo, inverse, rhs, x1, send, jnp.stack(idx)


def restrict(dest, residual, p_hi, p_lo):
    both = jnp.concatenate([residual[:32], residual[32:]], axis=1)
    place = (iota((32, 128), 1) & 63) >> 2
    hi, lo = split(both)
    hi, lo = hi.astype(F32), lo.astype(F32)
    r_hi = jnp.concatenate([jnp.where(place == FINE_ORDER[i], hi, 0.0) for i in range(16)], axis=0).astype(BF16)
    r_lo = jnp.concatenate([jnp.where(place == FINE_ORDER[i], lo, 0.0) for i in range(16)], axis=0).astype(BF16)
    pieces = []
    for e in range(2):
        u = mm(p_hi[e], r_hi, TN) + mm(p_hi[e], r_lo, TN) + mm(p_lo[e], r_hi, TN)
        pieces.append(u[:64, :64] + u[64:, 64:])
    hi, lo = split(jnp.concatenate(pieces, axis=1))
    rows = jnp.broadcast_to(dest[1:2].astype(F32), (16, 128)).astype(BF16)
    x = jnp.concatenate([hi, lo, rows], axis=0)
    out = []
    for q in range(0, XN * YN, 2):
        table = (iota((128, 128), 0) + q * 64 == dest[:1]).astype(F32).astype(BF16)
        g = mm(x, table, NT)
        v, at = g[:64] + g[64:128], g[128:136]
        out.append(jnp.concatenate([jnp.concatenate([v[:32, :64], v[32:, :64]], axis=1), at], axis=0))
        at = jnp.concatenate([at[:, 64:], at[:, :64]], axis=1)
        out.append(jnp.concatenate([jnp.concatenate([v[:32, 64:], v[32:, 64:]], axis=1), at], axis=0))
    return jnp.stack(out)


def fine_down(device, x, own, left, right, hi, lo, inverse, idx, dest, p_hi, p_lo):
    solution, residual = last_passes(
        device[0, 0], x, own, left, right, hi, lo, inverse, [idx[i] for i in range(3)]
    )
    return solution, restrict(dest, residual, p_hi, p_lo)


def fine_middle(device, x, left, right, rhs, hi, lo, inverse, idx):
    sides = (left[:, :64], right[:, :64])
    x1, send = first_passes(
        device[0, 0], x[:, :64], sides, rhs, hi, lo, inverse, [idx[i] for i in range(3)]
    )
    return x1, send


def fine_end(device, x, own, left, right, hi, lo, inverse, idx):
    solution, residual = last_passes(
        device[0, 0], x, own, left, right, hi, lo, inverse, [idx[i] for i in range(3)]
    )
    return rows_of(solution), rows_of(residual)


def prolong_parts(blocks):
    parts = [split(tiles(blocks[:, e, :])) for e in range(2)]
    return jnp.stack([p[0] for p in parts]), jnp.stack([p[1] for p in parts])


def sum_rows(parts):
    total = jnp.zeros((128, 256), F32)
    for q in range(0, XN * YN, 2):
        v = jnp.concatenate(
            [jnp.concatenate([parts[q + i, :32, :64], parts[q + i, :32, 64:]], axis=0) for i in range(2)], axis=1
        )
        at = jnp.concatenate([parts[q + i, 32:33, :64] for i in range(2)], axis=1).astype(I32)
        table = (iota((256, 128), 0) + 1 == at).astype(F32).astype(BF16)
        total = total + mm(stacked(v), table, NT)
    total = total[:64] + total[64:]
    return (jnp.stack([total[2 * t : 2 * t + 2] for t in range(TN_)]),)


def sum_all(parts):
    return (jnp.broadcast_to(jnp.sum(parts, axis=0)[None], parts.shape),)


def windows(parts, idx):
    x = stacked(jnp.concatenate([parts[t] for t in range(TN_)], axis=0))
    out = []
    for q in range(XN * YN):
        half = idx[:, (q // 2) * 128 : (q // 2) * 128 + 128]
        if q % 2 == 0:
            g = mm(x, one_hot(256, half), NN)
            g = g[:64] + g[64:]
        v = g[:, (q % 2) * 64 : (q % 2) * 64 + 64]
        out.append(jnp.concatenate([v[:32], v[32:]], axis=1))
    return (jnp.stack(out),)


A1_ROWS = 3 * R1 * 32
P1_ROWS = R1 * 32
A2_ROWS = 3 * R2 * 32
D1_AT = A1_ROWS + P1_ROWS
D2_AT = D1_AT + 64
IX_AT = D2_AT + 64
A2_AT = IX_AT + 8
PACK_ROWS = A2_AT + A2_ROWS


def level_pack(blocks, prolong, coarse, idx):
    a1 = [tiles(blocks[k]) for k in range(3)]
    a2 = [lanes_in(coarse[k].reshape(R2 * 32, 128)) for k in range(3)]
    pad = jnp.zeros((256, 128), F32)
    d1 = 1.0 / diagonal_plain(jnp.concatenate([a1[0], pad], axis=0))[:, :32]
    pad = jnp.zeros((448, 128), F32)
    d2 = 1.0 / diagonal_plain(jnp.concatenate([a2[0], pad], axis=0))[:, :8]
    return (
        jnp.concatenate(
            a1
            + [tiles(prolong)]
            + [jnp.concatenate([d1] * 4, axis=1), jnp.concatenate([d2] * 16, axis=1), idx]
            + a2,
            axis=0,
        ),
    )


def diagonal_plain(m):
    return diagonal(m, PLAIN_ORDER)


STARTS = [0, 0, 0, 128]


def middle_prep(place, p0, m2, p2, crossed, swapped, far):
    slab = place[0, 0]
    even = (slab & 1) == 0
    top = A2_AT
    twin, twin_m2, twin_p2 = (swapped[i * PACK_ROWS : (i + 1) * PACK_ROWS] for i in range(3))
    far_twin = swapped[3 * PACK_ROWS :]
    far_low = jnp.where(even, far, far_twin)
    far_high = jnp.where(even, far_twin, far)
    m3 = jnp.where(even, crossed, twin_m2[:top])
    p3 = jnp.where(even, twin_p2[:top], crossed)
    m1 = jnp.where(even, twin_m2, twin)
    p1 = jnp.where(even, twin, twin_p2)
    packs = [m3, m2, m1, p0, p1, p2, p3]
    lane128 = iota((1, 128), 1)
    quarter = iota((64, 128), 1) >> 5
    tiled = [far_low] + [p[D1_AT : D1_AT + 64] for p in packs] + [far_high]
    d1 = []
    for q in range(3):
        v = jnp.zeros((64, 128), F32)
        for m in range(4):
            if q * 4 + m < 9:
                v = jnp.where(quarter == m, tiled[q * 4 + m], v)
        d1.append(v)
    d1 = jnp.concatenate(d1, axis=1)
    eighth = (iota((64, 128), 1) >> 3) & 7
    d2 = jnp.zeros((64, 128), F32)
    for m in range(7):
        d2 = jnp.where(eighth == m + 1, packs[m][D2_AT : D2_AT + 64], d2)
    d2 = d2[:, :64]
    ix = [p[IX_AT : IX_AT + 8].astype(I32) for p in packs]
    base = (slab - 4) * R1 * NRHS
    tables = []
    for c in range(4):
        for k in range(3):
            one = ix[2 * c - 1][k : k + 1] - base if c > 0 else jnp.full((1, 128), -1, I32)
            two = ix[2 * c][k : k + 1] - base
            at = jnp.where(((lane128 >> 5) & 1) == 0, one, two)
            tables.append(one_hot(256, at - STARTS[c]))
    c_tables = []
    c_base = (slab - 4) * R2 * NRHS
    group = (lane128 >> 3) & 7
    for k in range(3):
        at = jnp.full((1, 128), -1, I32)
        for m in range(1, 6):
            at = jnp.where(group == m + 1, ix[m][3 + k : 4 + k] - c_base, at)
        c_tables.append(one_hot(64, at))
    halves = [split(p[:D1_AT]) for p in packs]
    coarse = [split(p[A2_AT:]) for p in packs[1:6]]
    return (
        jnp.stack([h[0] for h in halves]),
        jnp.stack([h[1] for h in halves]),
        jnp.stack([h[0] for h in coarse]),
        jnp.stack([h[1] for h in coarse]),
        d1,
        d2,
        jnp.stack(tables),
        jnp.stack(c_tables),
    )


def middle(place, parts, b_hi, b_lo, q_hi, q_lo, d1, d2, tables, c_tables, unpack):
    sub = place[0, 1]
    blocks = (b_hi, b_lo)
    lane128 = iota((1, 128), 1)
    pieces = []
    for x in range(XN):
        w = parts[x]
        for y in range(1, YN):
            w = w + parts[y * XN + x]
        pieces.append(jnp.concatenate([w[:, :64], w[:, 64:]], axis=0))
    g = mm(stacked(jnp.concatenate(pieces, axis=1)), one_hot(256, unpack), NN)
    rhs = g[:64] + g[64:]
    def rows(part, m, start, count):
        return blocks[part][max(m, 0), start : start + count]

    def pair(part, c, start, count):
        return jnp.concatenate(
            [rows(part, 2 * c - 1, start, count), rows(part, 2 * c, start, count)], axis=0
        )

    a_hi = [[pair(0, c, k * 256, 256) for k in range(3)] for c in range(4)]
    a_lo = [[pair(1, c, k * 256, 256) for k in range(3)] for c in range(4)]

    def apply1(v, chunks):
        x = stacked(v)
        return [
            forward(
                a_hi[c], a_lo[c], [gathered(x[:, STARTS[c] : STARTS[c] + 256], tables[3 * c + k]) for k in range(3)], PLAIN_ORDER
            )
            for c in chunks
        ]

    tail = jnp.zeros((64, 128), F32)
    inv = d1[:, :256]
    d = d1 * rhs / CENTER
    y = d[:, :256]
    r = rhs[:, :256] - jnp.concatenate(apply1(d, range(4)), axis=1)
    for t in range(2):
        step = KEEP[t] * d[:, :256] + GAIN[t] * (inv * r)
        d = jnp.concatenate([step, tail], axis=1)
        y = y + step
        r = r - jnp.concatenate(apply1(d, range(4)), axis=1)
    x = stacked(r)
    low = iota((32, 128), 1) < 64
    q_lane = (iota((32, 128), 1) & 63) >> 2
    first = (lane128 & 63) >> 2
    r_hi, r_lo = [], []
    for kk in range(4):
        g = mm(x, one_hot(256, first * 16 + kk * 4 + (lane128 & 3)), NN)
        r_hi.append(jnp.where(low, g[:32], g[32:64]))
        r_lo.append(jnp.where(low, g[64:96], g[96:128]))
    u = jnp.zeros((128, 128), F32)
    for m in range(7):
        keep = [q_lane == 2 * (m + 1) + j // 4 for j in range(R1)]
        b_hi = jnp.concatenate([jnp.where(keep[j], r_hi[j % 4], 0.0) for j in range(R1)], axis=0).astype(BF16)
        b_lo = jnp.concatenate([jnp.where(keep[j], r_lo[j % 4], 0.0) for j in range(R1)], axis=0).astype(BF16)
        p_hi, p_lo = rows(0, m, A1_ROWS, P1_ROWS), rows(1, m, A1_ROWS, P1_ROWS)
        u = u + mm(p_hi, b_hi, TN) + mm(p_hi, b_lo, TN) + mm(p_lo, b_hi, TN)
    r = u[:64, :64] + u[64:, 64:]
    c_hi, c_lo = [], []
    for k in range(3):
        near = [min(max(m - 2, 0), 4) for m in range(8)]
        c_hi.append(jnp.concatenate([q_hi[n, k * 64 : k * 64 + 64] for n in near], axis=0))
        c_lo.append(jnp.concatenate([q_lo[n, k * 64 : k * 64 + 64] for n in near], axis=0))
    d = d2 * r / CENTER
    z = d
    for t in range(3):
        s = stacked(d)
        r = r - forward(c_hi, c_lo, [gathered(s, c_tables[k]) for k in range(3)], PLAIN_ORDER)
        d = KEEP[t] * d + GAIN[t] * (d2 * r)
        z = z + d
    s = stacked(z)
    new = []
    for c in (1, 2):
        at = ((16 * c + ((lane128 & 63) >> 2)) >> 2) * 4 + (lane128 & 3)
        lift = forward(
            [pair(0, c, A1_ROWS, P1_ROWS)], [pair(1, c, A1_ROWS, P1_ROWS)], [gathered(s, one_hot(64, at))], PLAIN_ORDER
        )
        new.append(y[:, c * 64 : c * 64 + 64] + lift)
    y = jnp.concatenate([y[:, :64], new[0], new[1], y[:, 192:256], tail], axis=1)
    side = jnp.zeros((64, 64), F32)

    def at_centre(v):
        return jnp.concatenate([side, v, side, tail], axis=1)

    inv = inv[:, 64:192]
    r = rhs[:, 64:192] - jnp.concatenate(apply1(y, (1, 2)), axis=1)
    d = inv * r / CENTER
    y = y[:, 64:192] + d
    r = r - jnp.concatenate(apply1(at_centre(d), (1, 2)), axis=1)
    d = KEEP[0] * d + GAIN[0] * (inv * r)
    y = y + d
    r = r[:, 64:] - apply1(at_centre(d), (2,))[0]
    own = y[:, 64:] + KEEP[1] * d[:, 64:] + GAIN[1] * (inv[:, 64:] * r)
    pick_rows = (iota((8, 64), 1) == iota((8, 64), 0) + sub * 8).astype(F32).astype(BF16)
    hi, lo = split(own)
    o = mm(pick_rows, hi, NT) + mm(pick_rows, lo, NT)
    o = jnp.concatenate([jnp.concatenate([o[:2], o[4:6]], axis=1), jnp.concatenate([o[2:4], o[6:]], axis=1)], axis=1)
    return (jnp.broadcast_to(o[None], (TN_, 2, 256)),)


def level_cycle(place, parts, p0, m2, p2, crossed, swapped, far, unpack):
    return middle(place, parts, *middle_prep(place, p0, m2, p2, crossed, swapped, far), unpack)


def fine_up(rows_ref, odd_ref, all_ref, x_ref, hi_ref, lo_ref, out_ref, line):
    for p in range(32):
        v = all_ref[rows_ref[p]]
        v = jnp.concatenate([v[:, :128], v[:, 128:]], axis=0)
        line[p * 4 : p * 4 + 4, :] = jnp.where(odd_ref[p] == 1, pltpu.roll(v, 64, 1), v)
    w = line[:, :64].T
    hi, lo = split(w)
    hi, lo = hi.astype(F32), lo.astype(F32)
    rights = [
        spread(double(hi[:, e * 64 : e * 64 + 64]), double(lo[:, e * 64 : e * 64 + 64])) for e in range(2)
    ]
    x = x_ref[...] + forward([hi_ref[0], hi_ref[1]], [lo_ref[0], lo_ref[1]], rights, FINE_ORDER)
    out_ref[...] = double(x)


def fine_up_call(rows, odd, gathered_rows, x, hi, lo):
    smem, vmem = pl.BlockSpec(memory_space=pltpu.SMEM), pl.BlockSpec(memory_space=pltpu.VMEM)
    return pl.pallas_call(
        fine_up,
        in_specs=[smem, smem, vmem, vmem, vmem, vmem],
        out_specs=vmem,
        out_shape=jax.ShapeDtypeStruct((64, 128), F32),
        scratch_shapes=[pltpu.VMEM((128, 128), F32)],
        compiler_params=pltpu.CompilerParams(vmem_limit_bytes=32 << 20),
        name="fine_up",
    )(rows, odd, gathered_rows, x, hi, lo)


XY = [[(y * TN_ + t) * XN + x for y in range(YN) for x in range(XN)] for t in range(TN_)]
ZC = [[y * TN_ + t for t in range(TN_)] for y in range(YN)]


def across(value):
    return lax.all_to_all(value, ("slab", "sub"), 0, 0, tiled=True, axis_index_groups=XY)


def along(value):
    return lax.all_to_all(value, "slab", 0, 0, tiled=True, axis_index_groups=ZC)


def shifted(value, axis, by):
    n = lax.axis_size(axis)
    return lax.ppermute(value, axis, [(i, i + by) for i in range(n) if 0 <= i + by < n])


def unpack_table(spot):
    lane = jnp.arange(384, dtype=I32)
    rel, row = lane // 32 - 4, (lane % 32) // 4
    x = (spot + rel) % XN
    part = ((rel >= 0) & (rel < 4)).astype(I32)
    idx = x * 64 + part * 32 + lane % 32
    keep = (rel <= 4) & ((rel < 4) | (row < 4)) & ((rel > -4) | (row >= 4))
    return jnp.where(keep, idx, -1).reshape(1, 384)


def lane_index(columns, times):
    t = columns.T
    v = (t[:, :, None] * NRHS + jnp.arange(NRHS, dtype=I32)).reshape(3, -1)
    return jnp.concatenate([v] * times, axis=1).astype(F32)


def places(values):
    return values.reshape(8, 2, -1).transpose(2, 1, 0).reshape(values.shape[1], 16)


def body(
    right_side,
    warm_start,
    fine_blocks,
    fine_columns,
    fine_prolong,
    owner_rows,
    send_slots,
    receive_rows,
    middle_blocks,
    middle_columns,
    middle_prolong,
    coarse_blocks,
    coarse_columns,
):
    both = ("slab", "sub")
    slab = lax.axis_index("slab").astype(I32)
    sub = lax.axis_index("sub").astype(I32)
    device = (slab * XN + sub).reshape(1, 1)
    place = jnp.stack([slab, sub]).reshape(1, 2)
    rhs4 = jnp.arange(NRHS, dtype=I32)

    g = places(fine_columns)
    g = (g // 16) * 64 + ((g % 2) * 8 + (g % 16) // 2) * 4
    g = (g[:, :, None] + rhs4).reshape(3, 64)
    g = jnp.concatenate([g, g], axis=1).astype(F32)
    own = jnp.concatenate([warm_start, right_side, jnp.pad(g, ((0, 5), (0, 896)))], axis=0)
    blocks = fine_blocks.transpose(1, 0, 2)
    left_blocks, right_blocks = shifted(blocks[:, 8:], both, 1), shifted(blocks[:, :8], both, -1)
    left, right = shifted(own, both, 1), shifted(own, both, -1)

    ix = jnp.concatenate([lane_index(middle_columns, 4), lane_index(coarse_columns, 16)], axis=0)
    (pack,) = kern(
        level_pack,
        [((PACK_ROWS, 128), F32)],
        [middle_blocks.transpose(1, 0, 2), middle_prolong, coarse_blocks.transpose(1, 0, 2), jnp.pad(ix, ((0, 2), (0, 0)))],
    )
    left, right, pack = lax.optimization_barrier((left, right, pack))
    m2, p2 = shifted(pack, "slab", 2), shifted(pack, "slab", -2)
    count = lax.axis_size("slab")

    def crossing(value, by):
        pairs = [(i, i + by if i % 2 == by % 2 else i - by) for i in range(count)]
        return lax.ppermute(value, "slab", [p for p in pairs if 0 <= p[1] < count])

    crossed = crossing(pack[:A2_AT], 3)
    far = crossing(pack[D1_AT : D1_AT + 64], 4)
    p_hi, p_lo = kern(prolong_parts, [((2, 512, 128), BF16)] * 2, [fine_prolong])

    sends = ((64, 128), F32)
    hi, lo, inverse, rhs, x1, send, idx = kern(
        fine_start,
        [((2, 3, 512, 128), BF16)] * 2 + [sends, sends, ((64, 64), F32), sends, ((3, 3, 128), I32)],
        [device, own, left, right, blocks, left_blocks, right_blocks],
        smem=(0,),
        own=range(1, 7),
    )
    o = places(owner_rows)
    t = (o // 8) % TN_
    dest = ((o // 256) * XN + t % XN) * 64 + (t // XN) * 8 + places(send_slots) * 4
    dest_row = (t // XN) * 32 + (o % 8) * 4 + 1
    dest = jnp.concatenate([(v[:, :, None] + rhs4).reshape(1, 128) for v in (dest, dest_row)], axis=0)
    x3, dense = kern(
        fine_down,
        [((64, 64), F32), ((16, 40, 128), F32)],
        [device, x1, send, shifted(send, both, 1), shifted(send, both, -1), hi, lo, inverse, idx, dest, p_hi, p_lo],
        smem=(0,),
    )

    dense, m2, p2, crossed = lax.optimization_barrier((dense, m2, p2, crossed))
    twin = jnp.concatenate([pack, m2, p2, crossed[D1_AT : D1_AT + 64]], axis=0)
    twin = lax.ppermute(twin, "slab", [(i, i ^ 1) for i in range(count)])

    (part,) = kern(sum_rows, [((TN_, 2, 256), F32)], [across(dense)])
    (part,) = kern(sum_all, [((TN_, 2, 256), F32)], [along(part)])
    q = jnp.arange(XN * YN * 64, dtype=I32)
    spot = slab % TN_
    near_by = (sub - spot) % XN
    row = (q % 32) // 4
    rel = jnp.where((q % 64) // 32 == 1, near_by, near_by - 4)
    rel = jnp.where(((q % 64) // 32 == 0) & (near_by == 0) & (row < 4), 4, rel)
    wanted = (q // 256) * TN_ + spot + rel
    wanted = jnp.where(wanted // TN_ == slab // TN_, (wanted % TN_) // XN * 32 + q % 32, -1)
    wanted = jnp.where(wanted >= 0, wanted, -1)
    (part,) = kern(windows, [((16, 32, 128), F32)], [along(part), wanted.reshape(1, 1024)])
    part = across(part)

    (share,) = kern(
        level_cycle,
        [((TN_, 2, 256), F32)],
        [place, part, pack, m2, p2, crossed, twin, far, unpack_table(slab % TN_)],
        smem=(0,),
        own=range(2, 8),
    )
    line = along(share)
    every = across(jnp.broadcast_to(line[None], (XN * YN, TN_, 2, 256)))
    at = ((o // 256) * XN + (o % 8) // 2) * TN_ + (o // 8) % TN_
    x = fine_up_call(
        at.reshape(32), (o % 2).reshape(32), every.reshape(XN * YN * TN_, 2, 256), x3, p_hi, p_lo
    )

    x1, send = kern(
        fine_middle,
        [((64, 64), F32), sends],
        [device, x, shifted(x, both, 1), shifted(x, both, -1), rhs, hi, lo, inverse, idx],
        smem=(0,),
    )
    return tuple(
        kern(
            fine_end,
            [((NRHS, 1024), F32)] * 2,
            [device, x1, send, shifted(send, both, 1), shifted(send, both, -1), hi, lo, inverse, idx],
            smem=(0,),
        )
    )


def solution(mesh):
    in_specs = (
        P(None, ("slab", "sub")),
        P(None, ("slab", "sub")),
        P(("slab", "sub"), None, None),
        P(("slab", "sub"), None),
        P(("slab", "sub"), None, None),
        P(("slab", "sub"), None),
        P(("slab", "sub"), None),
        P("slab", "sub", None, None),
        P("slab", None, None),
        P("slab", None),
        P("slab", None),
        P("slab", None, None),
        P("slab", None),
    )
    out_specs = (P(None, ("slab", "sub")), P(None, ("slab", "sub")))
    return jax.shard_map(body, mesh=mesh, in_specs=in_specs, out_specs=out_specs, check_vma=False)
```

```python
import jax
import jax.numpy as jnp
from jax import lax
from jax.experimental import pallas as pl
from jax.experimental.pallas import tpu as pltpu
from jax.sharding import PartitionSpec as P

F32 = jnp.float32
BF16 = jnp.bfloat16
I32 = jnp.int32
BS = 64
NRHS = 4
R0 = 16
R1 = 8
R2 = 2
XN = 4
YN = 4
TN_ = 32

CENTER = 0.5 * (2.2 + 0.3)
HALF = 0.5 * (2.2 - 0.3)
SCALED = CENTER / HALF
FACTORS = [1.0 / SCALED]
for _ in range(3):
    FACTORS.append(1.0 / (2.0 * SCALED - FACTORS[-1]))
KEEP = [FACTORS[t + 1] * FACTORS[t] for t in range(3)]
GAIN = [2.0 * FACTORS[t + 1] / HALF for t in range(3)]

NN = ((1,), (0,))
NT = ((1,), (1,))
TN = ((0,), (0,))

FINE_ORDER = [(i % 2) * 8 + i // 2 for i in range(R0)]
RIM_ORDER = FINE_ORDER[8:] + FINE_ORDER[:8]
PLAIN_ORDER = list(range(16))


def kern(body, outs, args, smem=(), own=(), own_outs=False):
    count = len(args)

    def kernel(*refs):
        ins = [r if i in smem else r[...] for i, r in enumerate(refs[:count])]
        for ref, value in zip(refs[count:], body(*ins)):
            ref[...] = value

    vmem = pl.BlockSpec(memory_space=pltpu.VMEM)
    specs = [
        pl.BlockSpec(memory_space=pltpu.SMEM) if i in smem else pl.BlockSpec() if i in own else vmem
        for i in range(count)
    ]
    return pl.pallas_call(
        kernel,
        in_specs=specs,
        out_specs=[pl.BlockSpec() if own_outs else vmem for _ in outs],
        out_shape=[jax.ShapeDtypeStruct(s, d) for s, d in outs],
        compiler_params=pltpu.CompilerParams(vmem_limit_bytes=32 << 20),
        name=body.__name__,
    )(*args)


def mm(a, b, dims):
    return lax.dot_general(a, b, (dims, ((), ())), preferred_element_type=F32)


def iota(shape, dim):
    return lax.broadcasted_iota(I32, shape, dim)


def split(v):
    hi = v.astype(BF16)
    return hi, (v - hi.astype(F32)).astype(BF16)


def stacked(v):
    hi, lo = split(v)
    return jnp.concatenate([hi, lo], axis=0)


def one_hot(size, idx):
    return (iota((size, idx.shape[1]), 0) == idx).astype(F32).astype(BF16)


def lanes_in(x):
    lane = iota(x.shape, 1)
    place = lane & 63
    return jnp.take_along_axis(x, (lane & 64) + 2 * (place & 31) + (place >> 5), axis=1)


def lanes_out(x):
    lane = iota(x.shape, 1)
    b = lane & 63
    return jnp.take_along_axis(x, (lane & 64) + (b & 1) * 32 + (b >> 1), axis=1)


def tiles(raw):
    return lanes_in(raw.reshape(raw.shape[0] * 32, 128))


def double(g):
    return jnp.concatenate([g, g], axis=1)


def spread(hi, lo):
    low = iota(hi.shape, 1) < 64
    zero = jnp.zeros_like(hi)
    top = jnp.concatenate([jnp.where(low, hi, zero), jnp.where(low, lo, zero)], axis=1)
    bottom = jnp.concatenate([jnp.where(low, zero, hi), jnp.where(low, zero, lo)], axis=1)
    return jnp.concatenate([top, bottom], axis=0).astype(BF16)


def gathered(x, table):
    g = mm(x, table, NN)
    return spread(g[:64], g[64:])


def pick(t, order):
    lane = iota((32, 128), 1)
    place = (lane & 63) >> 2
    y = jnp.zeros((32, 128), F32)
    for i in range(16):
        y = y + jnp.where(place == order[i], t[i * 32 : i * 32 + 32], 0.0)
    return jnp.concatenate([y[:, :64], y[:, 64:]], axis=0)


def forward(his, los, rights, order):
    hi = jnp.concatenate(his, axis=1) if len(his) > 1 else his[0]
    lo = jnp.concatenate(los, axis=1) if len(los) > 1 else los[0]
    right = jnp.concatenate(rights, axis=0) if len(rights) > 1 else rights[0]
    a = mm(hi, right, NN)
    return pick(a[:, :128] + a[:, 128:] + mm(lo, right[:, :128], NN), order)


def diagonal(m, order):
    sub = iota(m.shape, 0) & 31
    lane = iota(m.shape, 1)
    kept = jnp.where((lane == sub) | (lane == sub + 96), m, 0.0)
    ones = ((iota((128, 128), 0) >> 6) == (iota((128, 128), 1) >> 6)).astype(F32).astype(BF16)
    hi, lo = split(kept)
    return pick(mm(hi, ones, NN) + mm(lo, ones, NN), order)


def columns_of(rows):
    z = lanes_in(jnp.concatenate([rows[:, m * 128 : m * 128 + 128] for m in range(8)], axis=0))
    t = z.T
    return jnp.concatenate([t[:64], t[64:]], axis=1)


def rows_of(v):
    t = lanes_out(jnp.concatenate([v[:, :32], v[:, 32:]], axis=0).T)
    return jnp.concatenate([t[m * 4 : m * 4 + 4] for m in range(8)], axis=1)


def rim(left, right):
    lane = iota(left.shape, 1)
    return jnp.where((((lane & 63) >> 2) & 7) < 4, right, left)


def fine_tables(device, own, left, right):
    wide, near = [], []
    for k in range(3):
        g = own[k : k + 1]
        r = rim(left[k : k + 1], right[k : k + 1])
        base = (device - 1) * 64
        wide.append([one_hot(192, g - base), one_hot(192, r - base)])
        near.append(one_hot(128, (g & 63) + jnp.where((g >> 6) == device, 0, 64)))
    return wide, near


def fine_both(hi, lo, x, wide):
    return jnp.concatenate(
        [
            forward(
                [hi[c, k] for k in range(3)],
                [lo[c, k] for k in range(3)],
                [gathered(x, wide[k][c]) for k in range(3)],
                (FINE_ORDER, RIM_ORDER)[c],
            )
            for c in range(2)
        ],
        axis=1,
    )


def fine_own(hi, lo, x, near):
    return forward(
        [hi[0, k] for k in range(3)],
        [lo[0, k] for k in range(3)],
        [gathered(x, near[k]) for k in range(3)],
        FINE_ORDER,
    )


def first_passes(device, x, sides, rhs, hi, lo, inverse, idx):
    wide, near = fine_tables(device, *idx)
    window = stacked(jnp.concatenate([sides[0], x, sides[1]], axis=1))
    r = rhs - fine_both(hi, lo, window, wide)
    d = inverse * r / CENTER
    r1 = r[:, :64] - fine_own(hi, lo, stacked(d), near)
    d1 = d[:, :64]
    d2 = KEEP[0] * d1 + GAIN[0] * (inverse[:, :64] * r1)
    return x + d1, jnp.concatenate([d2, r1], axis=1)


def last_passes(device, x, own, left, right, hi, lo, inverse, idx):
    wide, near = fine_tables(device, *idx)
    window = stacked(jnp.concatenate([left[:, :64], own[:, :64], right[:, :64]], axis=1))
    rims = rim(jnp.concatenate([left[:, 64:]] * 2, axis=1), jnp.concatenate([right[:, 64:]] * 2, axis=1))
    rim_d = rim(double(left[:, :64]), double(right[:, :64]))
    r = jnp.concatenate([own[:, 64:], rims[:, :64]], axis=1) - fine_both(hi, lo, window, wide)
    d_old = jnp.concatenate([own[:, :64], rim_d[:, :64]], axis=1)
    d = KEEP[1] * d_old + GAIN[1] * (inverse * r)
    residual = r[:, :64] - fine_own(hi, lo, stacked(d), near)
    return x + own[:, :64] + d[:, :64], residual


def indices(payload):
    return payload[:3, 1024:1152].astype(I32)


def fine_start(device, own, left_all, right_all, own_blocks):
    parts = []
    for k in range(3):
        parts.append(tiles(own_blocks[k]))
    for k in range(3):
        parts.append(jnp.concatenate([tiles(left_all[k]), tiles(right_all[k])], axis=0))
    entries = jnp.concatenate([diagonal(parts[0], FINE_ORDER), diagonal(parts[3], RIM_ORDER)], axis=1)
    inverse = jnp.where(entries == 0.0, 0.0, 1.0 / entries)
    pairs = [split(p) for p in parts]
    hi = jnp.stack([p[0] for p in pairs]).reshape(2, 3, 512, 128)
    lo = jnp.stack([p[1] for p in pairs]).reshape(2, 3, 512, 128)
    left, right = left_all[3], right_all[3]
    x = [columns_of(p[:4, :1024]) for p in (left, own, right)]
    b = [columns_of(p[4:, :1024]) for p in (left, own, right)]
    rhs = jnp.concatenate([b[1], rim(b[0], b[2])], axis=1)
    idx = [indices(p) for p in (own, left, right)]
    x1, send = first_passes(device[0, 0], x[1], (x[0], x[2]), rhs, hi, lo, inverse, idx)
    return hi, lo, inverse, rhs, x1, send, jnp.stack(idx)


def lanes_of(values, first=0):
    lane = iota((1, 128), 1)
    v = jnp.zeros((1, 128), I32)
    for n, value in enumerate(values):
        v = jnp.where((lane >> 2) == first + n, value * NRHS + (lane & 3), v)
    return v


def repeated(v, width):
    shift = width
    while shift < 128:
        v = v + pltpu.roll(v, shift, 1)
        shift *= 2
    return v


def payload(x, b, columns):
    lines = []
    for k in range(3):
        values = [None] * R0
        for i in range(R0):
            g = columns[i, k]
            values[FINE_ORDER[i]] = (g >> 4) * 16 + (g & 1) * 8 + ((g & 15) >> 1)
        lines.append(repeated(lanes_of(values), 64))
    v = jnp.concatenate(lines + [jnp.zeros((5, 128), I32)], axis=0).astype(F32)
    return (jnp.concatenate([jnp.concatenate([x, b], axis=0), v, jnp.zeros((8, 2944), F32)], axis=1),)


def restrict(dest, residual, p_hi, p_lo):
    both = jnp.concatenate([residual[:32], residual[32:]], axis=1)
    place = (iota((32, 128), 1) & 63) >> 2
    hi, lo = split(both)
    hi, lo = hi.astype(F32), lo.astype(F32)
    r_hi = jnp.concatenate([jnp.where(place == FINE_ORDER[i], hi, 0.0) for i in range(16)], axis=0).astype(BF16)
    r_lo = jnp.concatenate([jnp.where(place == FINE_ORDER[i], lo, 0.0) for i in range(16)], axis=0).astype(BF16)
    pieces = []
    for e in range(2):
        u = mm(p_hi[e], r_hi, TN) + mm(p_hi[e], r_lo, TN) + mm(p_lo[e], r_hi, TN)
        pieces.append(u[:64, :64] + u[64:, 64:])
    hi, lo = split(jnp.concatenate(pieces, axis=1))
    rows = jnp.broadcast_to(dest[1:2].astype(F32), (16, 128)).astype(BF16)
    x = jnp.concatenate([hi, lo, rows], axis=0)
    out = []
    for q in range(0, XN * YN, 2):
        table = (iota((128, 128), 0) + q * 64 == dest[:1]).astype(F32).astype(BF16)
        g = mm(x, table, NT)
        v, at = g[:64] + g[64:128], g[128:136]
        out.append(jnp.concatenate([jnp.concatenate([v[:32, :64], v[32:, :64]], axis=1), at], axis=0))
        at = jnp.concatenate([at[:, 64:], at[:, :64]], axis=1)
        out.append(jnp.concatenate([jnp.concatenate([v[:32, 64:], v[32:, 64:]], axis=1), at], axis=0))
    return jnp.stack(out)


def fine_down(device, x, own, left, right, hi, lo, inverse, idx, owner, slot, p_hi, p_lo):
    spots, lines = [None] * 32, [None] * 32
    for e in range(2):
        for i in range(R0):
            j, at = owner[i, e], e * R0 + FINE_ORDER[i]
            t = (j >> 3) & (TN_ - 1)
            spots[at] = ((j >> 8) * XN + (t & (XN - 1))) * 16 + (t >> 2) * 2 + slot[i, e]
            lines[at] = (t >> 2) * 8 + (j & 7)
    dest = jnp.concatenate([lanes_of(spots), lanes_of(lines) + 1], axis=0)
    solution, residual = last_passes(
        device[0, 0], x, own, left, right, hi, lo, inverse, [idx[i] for i in range(3)]
    )
    return solution, restrict(dest, residual, p_hi, p_lo)


def fine_middle(device, x, left, right, rhs, hi, lo, inverse, idx):
    sides = (left[:, :64], right[:, :64])
    x1, send = first_passes(
        device[0, 0], x[:, :64], sides, rhs, hi, lo, inverse, [idx[i] for i in range(3)]
    )
    return x1, send


def fine_end(device, x, own, left, right, hi, lo, inverse, idx):
    solution, residual = last_passes(
        device[0, 0], x, own, left, right, hi, lo, inverse, [idx[i] for i in range(3)]
    )
    return rows_of(solution), rows_of(residual)


def prolong_parts(blocks):
    parts = [split(tiles(blocks[:, e, :])) for e in range(2)]
    return jnp.stack([p[0] for p in parts]), jnp.stack([p[1] for p in parts])


def sum_rows(parts):
    total = jnp.zeros((128, 256), F32)
    for q in range(0, XN * YN, 2):
        v = jnp.concatenate(
            [jnp.concatenate([parts[q + i, :32, :64], parts[q + i, :32, 64:]], axis=0) for i in range(2)], axis=1
        )
        at = jnp.concatenate([parts[q + i, 32:33, :64] for i in range(2)], axis=1).astype(I32)
        table = (iota((256, 128), 0) + 1 == at).astype(F32).astype(BF16)
        total = total + mm(stacked(v), table, NT)
    total = total[:64] + total[64:]
    return (jnp.stack([total[2 * t : 2 * t + 2] for t in range(TN_)]),)


def sum_all(parts):
    return (jnp.broadcast_to(jnp.sum(parts, axis=0)[None], parts.shape),)


def windows(parts, idx):
    x = stacked(jnp.concatenate([parts[t] for t in range(TN_)], axis=0))
    out = []
    for q in range(XN * YN):
        half = idx[:, (q // 2) * 128 : (q // 2) * 128 + 128]
        if q % 2 == 0:
            g = mm(x, one_hot(256, half), NN)
            g = g[:64] + g[64:]
        v = g[:, (q % 2) * 64 : (q % 2) * 64 + 64]
        out.append(jnp.concatenate([v[:32], v[32:]], axis=1))
    return (jnp.stack(out),)


A1_ROWS = 3 * R1 * 32
P1_ROWS = R1 * 32
A2_ROWS = 3 * R2 * 32
D1_AT = A1_ROWS + P1_ROWS
D2_AT = D1_AT + 64
IX_AT = D2_AT + 64
A2_AT = IX_AT + 8
PACK_ROWS = A2_AT + A2_ROWS


def level_pack(blocks, prolong, coarse, columns, coarse_columns):
    lines = [repeated(lanes_of([columns[i, k] for i in range(R1)]), 32) for k in range(3)]
    lines += [repeated(lanes_of([coarse_columns[i, k] for i in range(R2)]), 8) for k in range(3)]
    idx = jnp.concatenate(lines + [jnp.zeros((2, 128), I32)], axis=0).astype(F32)
    a1 = [tiles(blocks[k]) for k in range(3)]
    a2 = [lanes_in(coarse[k].reshape(R2 * 32, 128)) for k in range(3)]
    pad = jnp.zeros((256, 128), F32)
    d1 = 1.0 / diagonal_plain(jnp.concatenate([a1[0], pad], axis=0))[:, :32]
    pad = jnp.zeros((448, 128), F32)
    d2 = 1.0 / diagonal_plain(jnp.concatenate([a2[0], pad], axis=0))[:, :8]
    return (
        jnp.concatenate(
            a1
            + [tiles(prolong)]
            + [jnp.concatenate([d1] * 4, axis=1), jnp.concatenate([d2] * 16, axis=1), idx]
            + a2,
            axis=0,
        ),
    )


def diagonal_plain(m):
    return diagonal(m, PLAIN_ORDER)


STARTS = [0, 0, 0, 128]


def middle_prep(place, p0, m2, p2, crossed, swapped, far):
    slab = place[0, 0]
    even = (slab & 1) == 0
    top = A2_AT
    twin, twin_m2, twin_p2 = (swapped[i * PACK_ROWS : (i + 1) * PACK_ROWS] for i in range(3))
    far_twin = swapped[3 * PACK_ROWS :]
    far_low = jnp.where(even, far, far_twin)
    far_high = jnp.where(even, far_twin, far)
    m3 = jnp.where(even, crossed, twin_m2[:top])
    p3 = jnp.where(even, twin_p2[:top], crossed)
    m1 = jnp.where(even, twin_m2, twin)
    p1 = jnp.where(even, twin, twin_p2)
    packs = [m3, m2, m1, p0, p1, p2, p3]
    lane128 = iota((1, 128), 1)
    quarter = iota((64, 128), 1) >> 5
    tiled = [far_low] + [p[D1_AT : D1_AT + 64] for p in packs] + [far_high]
    d1 = []
    for q in range(3):
        v = jnp.zeros((64, 128), F32)
        for m in range(4):
            if q * 4 + m < 9:
                v = jnp.where(quarter == m, tiled[q * 4 + m], v)
        d1.append(v)
    d1 = jnp.concatenate(d1, axis=1)
    eighth = (iota((64, 128), 1) >> 3) & 7
    d2 = jnp.zeros((64, 128), F32)
    for m in range(7):
        d2 = jnp.where(eighth == m + 1, packs[m][D2_AT : D2_AT + 64], d2)
    d2 = d2[:, :64]
    ix = [p[IX_AT : IX_AT + 8].astype(I32) for p in packs]
    base = (slab - 4) * R1 * NRHS
    tables = []
    for c in range(4):
        for k in range(3):
            one = ix[2 * c - 1][k : k + 1] - base if c > 0 else jnp.full((1, 128), -1, I32)
            two = ix[2 * c][k : k + 1] - base
            at = jnp.where(((lane128 >> 5) & 1) == 0, one, two)
            tables.append(one_hot(256, at - STARTS[c]))
    c_tables = []
    c_base = (slab - 4) * R2 * NRHS
    group = (lane128 >> 3) & 7
    for k in range(3):
        at = jnp.full((1, 128), -1, I32)
        for m in range(1, 6):
            at = jnp.where(group == m + 1, ix[m][3 + k : 4 + k] - c_base, at)
        c_tables.append(one_hot(64, at))
    halves = [split(p[:D1_AT]) for p in packs]
    coarse = [split(p[A2_AT:]) for p in packs[1:6]]
    return (
        jnp.stack([h[0] for h in halves]),
        jnp.stack([h[1] for h in halves]),
        jnp.stack([h[0] for h in coarse]),
        jnp.stack([h[1] for h in coarse]),
        d1,
        d2,
        jnp.stack(tables),
        jnp.stack(c_tables),
    )


def middle(place, parts, b_hi, b_lo, q_hi, q_lo, d1, d2, tables, c_tables, unpack):
    sub = place[0, 1]
    blocks = (b_hi, b_lo)
    lane128 = iota((1, 128), 1)
    pieces = []
    for x in range(XN):
        w = parts[x]
        for y in range(1, YN):
            w = w + parts[y * XN + x]
        pieces.append(jnp.concatenate([w[:, :64], w[:, 64:]], axis=0))
    g = mm(stacked(jnp.concatenate(pieces, axis=1)), one_hot(256, unpack), NN)
    rhs = g[:64] + g[64:]
    def rows(part, m, start, count):
        return blocks[part][max(m, 0), start : start + count]

    def pair(part, c, start, count):
        return jnp.concatenate(
            [rows(part, 2 * c - 1, start, count), rows(part, 2 * c, start, count)], axis=0
        )

    a_hi = [[pair(0, c, k * 256, 256) for k in range(3)] for c in range(4)]
    a_lo = [[pair(1, c, k * 256, 256) for k in range(3)] for c in range(4)]

    def apply1(v, chunks):
        x = stacked(v)
        return [
            forward(
                a_hi[c], a_lo[c], [gathered(x[:, STARTS[c] : STARTS[c] + 256], tables[3 * c + k]) for k in range(3)], PLAIN_ORDER
            )
            for c in chunks
        ]

    tail = jnp.zeros((64, 128), F32)
    inv = d1[:, :256]
    d = d1 * rhs / CENTER
    y = d[:, :256]
    r = rhs[:, :256] - jnp.concatenate(apply1(d, range(4)), axis=1)
    for t in range(2):
        step = KEEP[t] * d[:, :256] + GAIN[t] * (inv * r)
        d = jnp.concatenate([step, tail], axis=1)
        y = y + step
        r = r - jnp.concatenate(apply1(d, range(4)), axis=1)
    x = stacked(r)
    low = iota((32, 128), 1) < 64
    q_lane = (iota((32, 128), 1) & 63) >> 2
    first = (lane128 & 63) >> 2
    r_hi, r_lo = [], []
    for kk in range(4):
        g = mm(x, one_hot(256, first * 16 + kk * 4 + (lane128 & 3)), NN)
        r_hi.append(jnp.where(low, g[:32], g[32:64]))
        r_lo.append(jnp.where(low, g[64:96], g[96:128]))
    u = jnp.zeros((128, 128), F32)
    for m in range(7):
        keep = [q_lane == 2 * (m + 1) + j // 4 for j in range(R1)]
        b_hi = jnp.concatenate([jnp.where(keep[j], r_hi[j % 4], 0.0) for j in range(R1)], axis=0).astype(BF16)
        b_lo = jnp.concatenate([jnp.where(keep[j], r_lo[j % 4], 0.0) for j in range(R1)], axis=0).astype(BF16)
        p_hi, p_lo = rows(0, m, A1_ROWS, P1_ROWS), rows(1, m, A1_ROWS, P1_ROWS)
        u = u + mm(p_hi, b_hi, TN) + mm(p_hi, b_lo, TN) + mm(p_lo, b_hi, TN)
    r = u[:64, :64] + u[64:, 64:]
    c_hi, c_lo = [], []
    for k in range(3):
        near = [min(max(m - 2, 0), 4) for m in range(8)]
        c_hi.append(jnp.concatenate([q_hi[n, k * 64 : k * 64 + 64] for n in near], axis=0))
        c_lo.append(jnp.concatenate([q_lo[n, k * 64 : k * 64 + 64] for n in near], axis=0))
    d = d2 * r / CENTER
    z = d
    for t in range(3):
        s = stacked(d)
        r = r - forward(c_hi, c_lo, [gathered(s, c_tables[k]) for k in range(3)], PLAIN_ORDER)
        d = KEEP[t] * d + GAIN[t] * (d2 * r)
        z = z + d
    s = stacked(z)
    new = []
    for c in (1, 2):
        at = ((16 * c + ((lane128 & 63) >> 2)) >> 2) * 4 + (lane128 & 3)
        lift = forward(
            [pair(0, c, A1_ROWS, P1_ROWS)], [pair(1, c, A1_ROWS, P1_ROWS)], [gathered(s, one_hot(64, at))], PLAIN_ORDER
        )
        new.append(y[:, c * 64 : c * 64 + 64] + lift)
    y = jnp.concatenate([y[:, :64], new[0], new[1], y[:, 192:256], tail], axis=1)
    side = jnp.zeros((64, 64), F32)

    def at_centre(v):
        return jnp.concatenate([side, v, side, tail], axis=1)

    inv = inv[:, 64:192]
    r = rhs[:, 64:192] - jnp.concatenate(apply1(y, (1, 2)), axis=1)
    d = inv * r / CENTER
    y = y[:, 64:192] + d
    r = r - jnp.concatenate(apply1(at_centre(d), (1, 2)), axis=1)
    d = KEEP[0] * d + GAIN[0] * (inv * r)
    y = y + d
    r = r[:, 64:] - apply1(at_centre(d), (2,))[0]
    own = y[:, 64:] + KEEP[1] * d[:, 64:] + GAIN[1] * (inv[:, 64:] * r)
    pick_rows = (iota((8, 64), 1) == iota((8, 64), 0) + sub * 8).astype(F32).astype(BF16)
    hi, lo = split(own)
    o = mm(pick_rows, hi, NT) + mm(pick_rows, lo, NT)
    o = jnp.concatenate([jnp.concatenate([o[:2], o[4:6]], axis=1), jnp.concatenate([o[2:4], o[6:]], axis=1)], axis=1)
    return (jnp.broadcast_to(o[None], (TN_, 2, 256)),)


def level_cycle(place, parts, p0, m2, p2, crossed, swapped, far, unpack):
    return middle(place, parts, *middle_prep(place, p0, m2, p2, crossed, swapped, far), unpack)


def fine_up(owner_ref, all_ref, x_ref, hi_ref, lo_ref, out_ref, line):
    for n in range(32):
        e, i = n // R0, n % R0
        p, j = e * R0 + FINE_ORDER[i], owner_ref[i, e]
        v = all_ref[((j >> 8) * XN + ((j & 7) >> 1)) * TN_ + ((j >> 3) & (TN_ - 1))]
        v = jnp.concatenate([v[:, :128], v[:, 128:]], axis=0)
        line[p * 4 : p * 4 + 4, :] = jnp.where((j & 1) == 1, pltpu.roll(v, 64, 1), v)
    w = line[:, :64].T
    hi, lo = split(w)
    hi, lo = hi.astype(F32), lo.astype(F32)
    rights = [
        spread(double(hi[:, e * 64 : e * 64 + 64]), double(lo[:, e * 64 : e * 64 + 64])) for e in range(2)
    ]
    x = x_ref[...] + forward([hi_ref[0], hi_ref[1]], [lo_ref[0], lo_ref[1]], rights, FINE_ORDER)
    out_ref[...] = double(x)


def fine_up_call(owner, gathered_rows, x, hi, lo):
    smem, vmem = pl.BlockSpec(memory_space=pltpu.SMEM), pl.BlockSpec(memory_space=pltpu.VMEM)
    return pl.pallas_call(
        fine_up,
        in_specs=[smem, vmem, vmem, vmem, vmem],
        out_specs=vmem,
        out_shape=jax.ShapeDtypeStruct((64, 128), F32),
        scratch_shapes=[pltpu.VMEM((128, 128), F32)],
        compiler_params=pltpu.CompilerParams(vmem_limit_bytes=32 << 20),
        name="fine_up",
    )(owner, gathered_rows, x, hi, lo)


XY = [[(y * TN_ + t) * XN + x for y in range(YN) for x in range(XN)] for t in range(TN_)]
ZC = [[y * TN_ + t for t in range(TN_)] for y in range(YN)]


def across(value):
    return lax.all_to_all(value, ("slab", "sub"), 0, 0, tiled=True, axis_index_groups=XY)


def along(value):
    return lax.all_to_all(value, "slab", 0, 0, tiled=True, axis_index_groups=ZC)


def shifted(value, axis, by):
    n = lax.axis_size(axis)
    return lax.ppermute(value, axis, [(i, i + by) for i in range(n) if 0 <= i + by < n])


def unpack_table(spot):
    lane = jnp.arange(384, dtype=I32)
    rel, row = lane // 32 - 4, (lane % 32) // 4
    x = (spot + rel) % XN
    part = ((rel >= 0) & (rel < 4)).astype(I32)
    idx = x * 64 + part * 32 + lane % 32
    keep = (rel <= 4) & ((rel < 4) | (row < 4)) & ((rel > -4) | (row >= 4))
    return jnp.where(keep, idx, -1).reshape(1, 384)


def body(
    right_side,
    warm_start,
    fine_blocks,
    fine_columns,
    fine_prolong,
    owner_rows,
    send_slots,
    receive_rows,
    middle_blocks,
    middle_columns,
    middle_prolong,
    coarse_blocks,
    coarse_columns,
):
    both = ("slab", "sub")
    slab = lax.axis_index("slab").astype(I32)
    sub = lax.axis_index("sub").astype(I32)
    device = (slab * XN + sub).reshape(1, 1)
    place = jnp.stack([slab, sub]).reshape(1, 2)

    (own,) = kern(payload, [((8, 4096), F32)], [warm_start, right_side, fine_columns], smem=(2,))
    blocks = fine_blocks.transpose(1, 0, 2)
    low, high = (jnp.concatenate([part, own[None]], axis=0) for part in (blocks[:, :8], blocks[:, 8:]))
    middle_columns, low, high = lax.optimization_barrier((middle_columns, low, high))
    left, right = shifted(high, both, 1), shifted(low, both, -1)

    (pack,) = kern(
        level_pack,
        [((PACK_ROWS, 128), F32)],
        [middle_blocks.transpose(1, 0, 2), middle_prolong, coarse_blocks.transpose(1, 0, 2), middle_columns, coarse_columns],
        smem=(3, 4),
    )
    m2, p2 = shifted(pack, "slab", 2), shifted(pack, "slab", -2)
    count = lax.axis_size("slab")

    def crossing(value, by):
        pairs = [(i, i + by if i % 2 == by % 2 else i - by) for i in range(count)]
        return lax.ppermute(value, "slab", [p for p in pairs if 0 <= p[1] < count])

    p_hi, p_lo = kern(prolong_parts, [((2, 512, 128), BF16)] * 2, [fine_prolong])

    sends = ((64, 128), F32)
    hi, lo, inverse, rhs, x1, send, idx = kern(
        fine_start,
        [((2, 3, 512, 128), BF16)] * 2 + [sends, sends, ((64, 64), F32), sends, ((3, 3, 128), I32)],
        [device, own, left, right, blocks],
        smem=(0,),
        own=range(1, 5),
    )
    send, pack = lax.optimization_barrier((send, pack))
    crossed = crossing(pack[:A2_AT], 3)
    x3, dense = kern(
        fine_down,
        [((64, 64), F32), ((16, 40, 128), F32)],
        [device, x1, send, shifted(send, both, 1), shifted(send, both, -1), hi, lo, inverse, idx, owner_rows, send_slots, p_hi, p_lo],
        smem=(0, 9, 10),
    )

    dense, m2, p2, crossed = lax.optimization_barrier((dense, m2, p2, crossed))
    (part,) = kern(sum_rows, [((TN_, 2, 256), F32)], [across(dense)])
    (part,) = kern(sum_all, [((TN_, 2, 256), F32)], [along(part)])
    part, m2, p2, crossed, pack = lax.optimization_barrier((part, m2, p2, crossed, pack))
    twin = jnp.concatenate([pack, m2, p2, crossed[D1_AT : D1_AT + 64]], axis=0)
    twin = lax.ppermute(twin, "slab", [(i, i ^ 1) for i in range(count)])
    far = crossing(pack[D1_AT : D1_AT + 64], 4)
    q = jnp.arange(XN * YN * 64, dtype=I32)
    spot = slab % TN_
    near_by = (sub - spot) % XN
    row = (q % 32) // 4
    rel = jnp.where((q % 64) // 32 == 1, near_by, near_by - 4)
    rel = jnp.where(((q % 64) // 32 == 0) & (near_by == 0) & (row < 4), 4, rel)
    wanted = (q // 256) * TN_ + spot + rel
    wanted = jnp.where(wanted // TN_ == slab // TN_, (wanted % TN_) // XN * 32 + q % 32, -1)
    wanted = jnp.where(wanted >= 0, wanted, -1)
    (part,) = kern(windows, [((16, 32, 128), F32)], [along(part), wanted.reshape(1, 1024)])
    part = across(part)

    (share,) = kern(
        level_cycle,
        [((TN_, 2, 256), F32)],
        [place, part, pack, m2, p2, crossed, twin, far, unpack_table(slab % TN_)],
        smem=(0,),
        own=range(2, 8),
    )
    line = along(share)
    every = across(jnp.broadcast_to(line[None], (XN * YN, TN_, 2, 256)))
    x = fine_up_call(owner_rows, every.reshape(XN * YN * TN_, 2, 256), x3, p_hi, p_lo)

    x1, send = kern(
        fine_middle,
        [((64, 64), F32), sends],
        [device, x, shifted(x, both, 1), shifted(x, both, -1), rhs, hi, lo, inverse, idx],
        smem=(0,),
    )
    return tuple(
        kern(
            fine_end,
            [((NRHS, 1024), F32)] * 2,
            [device, x1, send, shifted(send, both, 1), shifted(send, both, -1), hi, lo, inverse, idx],
            smem=(0,),
        )
    )


def solution(mesh):
    in_specs = (
        P(None, ("slab", "sub")),
        P(None, ("slab", "sub")),
        P(("slab", "sub"), None, None),
        P(("slab", "sub"), None),
        P(("slab", "sub"), None, None),
        P(("slab", "sub"), None),
        P(("slab", "sub"), None),
        P("slab", "sub", None, None),
        P("slab", None, None),
        P("slab", None),
        P("slab", None),
        P("slab", None, None),
        P("slab", None),
    )
    out_specs = (P(None, ("slab", "sub")), P(None, ("slab", "sub")))
    return jax.shard_map(body, mesh=mesh, in_specs=in_specs, out_specs=out_specs, check_vma=False)
```

```python
import jax
import jax.numpy as jnp
from jax import lax
from jax.experimental import pallas as pl
from jax.experimental.pallas import tpu as pltpu
from jax.sharding import PartitionSpec as P

F32 = jnp.float32
BF16 = jnp.bfloat16
I32 = jnp.int32
BS = 64
NRHS = 4
R0 = 16
R1 = 8
R2 = 2
XN = 4
YN = 4
TN_ = 32

CENTER = 0.5 * (2.2 + 0.3)
HALF = 0.5 * (2.2 - 0.3)
SCALED = CENTER / HALF
FACTORS = [1.0 / SCALED]
for _ in range(3):
    FACTORS.append(1.0 / (2.0 * SCALED - FACTORS[-1]))
KEEP = [FACTORS[t + 1] * FACTORS[t] for t in range(3)]
GAIN = [2.0 * FACTORS[t + 1] / HALF for t in range(3)]

NN = ((1,), (0,))
NT = ((1,), (1,))
TN = ((0,), (0,))

FINE_ORDER = [(i % 2) * 8 + i // 2 for i in range(R0)]
RIM_ORDER = FINE_ORDER[8:] + FINE_ORDER[:8]
PLAIN_ORDER = list(range(16))


def kern(body, outs, args, smem=(), own=(), own_outs=False):
    count = len(args)

    def kernel(*refs):
        ins = [r if i in smem else r[...] for i, r in enumerate(refs[:count])]
        for ref, value in zip(refs[count:], body(*ins)):
            ref[...] = value

    vmem = pl.BlockSpec(memory_space=pltpu.VMEM)
    specs = [
        pl.BlockSpec(memory_space=pltpu.SMEM) if i in smem else pl.BlockSpec() if i in own else vmem
        for i in range(count)
    ]
    return pl.pallas_call(
        kernel,
        in_specs=specs,
        out_specs=[pl.BlockSpec() if own_outs else vmem for _ in outs],
        out_shape=[jax.ShapeDtypeStruct(s, d) for s, d in outs],
        compiler_params=pltpu.CompilerParams(vmem_limit_bytes=32 << 20),
        name=body.__name__,
    )(*args)


def mm(a, b, dims):
    return lax.dot_general(a, b, (dims, ((), ())), preferred_element_type=F32)


def iota(shape, dim):
    return lax.broadcasted_iota(I32, shape, dim)


def split(v):
    hi = v.astype(BF16)
    return hi, (v - hi.astype(F32)).astype(BF16)


def stacked(v):
    hi, lo = split(v)
    return jnp.concatenate([hi, lo], axis=0)


def one_hot(size, idx):
    return (iota((size, idx.shape[1]), 0) == idx).astype(F32).astype(BF16)


def lanes_in(x):
    lane = iota(x.shape, 1)
    place = lane & 63
    return jnp.take_along_axis(x, (lane & 64) + 2 * (place & 31) + (place >> 5), axis=1)


def lanes_out(x):
    lane = iota(x.shape, 1)
    b = lane & 63
    return jnp.take_along_axis(x, (lane & 64) + (b & 1) * 32 + (b >> 1), axis=1)


def tiles(raw):
    return lanes_in(raw.reshape(raw.shape[0] * 32, 128))


def double(g):
    return jnp.concatenate([g, g], axis=1)


def spread(hi, lo):
    low = iota(hi.shape, 1) < 64
    zero = jnp.zeros_like(hi)
    top = jnp.concatenate([jnp.where(low, hi, zero), jnp.where(low, lo, zero)], axis=1)
    bottom = jnp.concatenate([jnp.where(low, zero, hi), jnp.where(low, zero, lo)], axis=1)
    return jnp.concatenate([top, bottom], axis=0).astype(BF16)


def gathered(x, table):
    g = mm(x, table, NN)
    return spread(g[:64], g[64:])


def pick(t, order):
    lane = iota((32, 128), 1)
    place = (lane & 63) >> 2
    y = jnp.zeros((32, 128), F32)
    for i in range(16):
        y = y + jnp.where(place == order[i], t[i * 32 : i * 32 + 32], 0.0)
    return jnp.concatenate([y[:, :64], y[:, 64:]], axis=0)


def forward(his, los, rights, order):
    hi = jnp.concatenate(his, axis=1) if len(his) > 1 else his[0]
    lo = jnp.concatenate(los, axis=1) if len(los) > 1 else los[0]
    right = jnp.concatenate(rights, axis=0) if len(rights) > 1 else rights[0]
    a = mm(hi, right, NN)
    return pick(a[:, :128] + a[:, 128:] + mm(lo, right[:, :128], NN), order)


def diagonal(m, order):
    sub = iota(m.shape, 0) & 31
    lane = iota(m.shape, 1)
    kept = jnp.where((lane == sub) | (lane == sub + 96), m, 0.0)
    ones = ((iota((128, 128), 0) >> 6) == (iota((128, 128), 1) >> 6)).astype(F32).astype(BF16)
    hi, lo = split(kept)
    return pick(mm(hi, ones, NN) + mm(lo, ones, NN), order)


def columns_of(rows):
    z = lanes_in(jnp.concatenate([rows[:, m * 128 : m * 128 + 128] for m in range(8)], axis=0))
    t = z.T
    return jnp.concatenate([t[:64], t[64:]], axis=1)


def rows_of(v):
    t = lanes_out(jnp.concatenate([v[:, :32], v[:, 32:]], axis=0).T)
    return jnp.concatenate([t[m * 4 : m * 4 + 4] for m in range(8)], axis=1)


def rim(left, right):
    lane = iota(left.shape, 1)
    return jnp.where((((lane & 63) >> 2) & 7) < 4, right, left)


def fine_tables(device, own, left, right):
    wide, near = [], []
    for k in range(3):
        g = own[k : k + 1]
        r = rim(left[k : k + 1], right[k : k + 1])
        base = (device - 1) * 64
        wide.append([one_hot(192, g - base), one_hot(192, r - base)])
        near.append(one_hot(128, (g & 63) + jnp.where((g >> 6) == device, 0, 64)))
    return wide, near


def fine_both(hi, lo, x, wide):
    return jnp.concatenate(
        [
            forward(
                [hi[c, k] for k in range(3)],
                [lo[c, k] for k in range(3)],
                [gathered(x, wide[k][c]) for k in range(3)],
                (FINE_ORDER, RIM_ORDER)[c],
            )
            for c in range(2)
        ],
        axis=1,
    )


def fine_own(hi, lo, x, near):
    return forward(
        [hi[0, k] for k in range(3)],
        [lo[0, k] for k in range(3)],
        [gathered(x, near[k]) for k in range(3)],
        FINE_ORDER,
    )


def first_passes(device, x, sides, rhs, hi, lo, inverse, idx):
    wide, near = fine_tables(device, *idx)
    window = stacked(jnp.concatenate([sides[0], x, sides[1]], axis=1))
    r = rhs - fine_both(hi, lo, window, wide)
    d = inverse * r / CENTER
    r1 = r[:, :64] - fine_own(hi, lo, stacked(d), near)
    d1 = d[:, :64]
    d2 = KEEP[0] * d1 + GAIN[0] * (inverse[:, :64] * r1)
    return x + d1, jnp.concatenate([d2, r1], axis=1)


def last_passes(device, x, own, left, right, hi, lo, inverse, idx):
    wide, near = fine_tables(device, *idx)
    window = stacked(jnp.concatenate([left[:, :64], own[:, :64], right[:, :64]], axis=1))
    rims = rim(jnp.concatenate([left[:, 64:]] * 2, axis=1), jnp.concatenate([right[:, 64:]] * 2, axis=1))
    rim_d = rim(double(left[:, :64]), double(right[:, :64]))
    r = jnp.concatenate([own[:, 64:], rims[:, :64]], axis=1) - fine_both(hi, lo, window, wide)
    d_old = jnp.concatenate([own[:, :64], rim_d[:, :64]], axis=1)
    d = KEEP[1] * d_old + GAIN[1] * (inverse * r)
    residual = r[:, :64] - fine_own(hi, lo, stacked(d), near)
    return x + own[:, :64] + d[:, :64], residual


def indices(payload):
    return payload[:3, 1024:1152].astype(I32)


def fine_start(device, own, left_all, right_all, own_blocks):
    parts = []
    for k in range(3):
        parts.append(tiles(own_blocks[k]))
    for k in range(3):
        parts.append(jnp.concatenate([tiles(left_all[k]), tiles(right_all[k])], axis=0))
    entries = jnp.concatenate([diagonal(parts[0], FINE_ORDER), diagonal(parts[3], RIM_ORDER)], axis=1)
    inverse = jnp.where(entries == 0.0, 0.0, 1.0 / entries)
    pairs = [split(p) for p in parts]
    hi = jnp.stack([p[0] for p in pairs]).reshape(2, 3, 512, 128)
    lo = jnp.stack([p[1] for p in pairs]).reshape(2, 3, 512, 128)
    left, right = left_all[3], right_all[3]
    x = [columns_of(p[:4, :1024]) for p in (left, own, right)]
    b = [columns_of(p[4:, :1024]) for p in (left, own, right)]
    rhs = jnp.concatenate([b[1], rim(b[0], b[2])], axis=1)
    idx = [indices(p) for p in (own, left, right)]
    x1, send = first_passes(device[0, 0], x[1], (x[0], x[2]), rhs, hi, lo, inverse, idx)
    return hi, lo, inverse, rhs, x1, send, jnp.stack(idx)


def lanes_of(values, first=0):
    lane = iota((1, 128), 1)
    v = jnp.zeros((1, 128), I32)
    for n, value in enumerate(values):
        v = jnp.where((lane >> 2) == first + n, value * NRHS + (lane & 3), v)
    return v


def repeated(v, width):
    shift = width
    while shift < 128:
        v = v + pltpu.roll(v, shift, 1)
        shift *= 2
    return v


def payload(x, b, columns):
    lines = []
    for k in range(3):
        values = [None] * R0
        for i in range(R0):
            g = columns[i, k]
            values[FINE_ORDER[i]] = (g >> 4) * 16 + (g & 1) * 8 + ((g & 15) >> 1)
        lines.append(repeated(lanes_of(values), 64))
    v = jnp.concatenate(lines + [jnp.zeros((5, 128), I32)], axis=0).astype(F32)
    return (jnp.concatenate([jnp.concatenate([x, b], axis=0), v, jnp.zeros((8, 2944), F32)], axis=1),)


def restrict(dest, residual, p_hi, p_lo):
    both = jnp.concatenate([residual[:32], residual[32:]], axis=1)
    place = (iota((32, 128), 1) & 63) >> 2
    hi, lo = split(both)
    hi, lo = hi.astype(F32), lo.astype(F32)
    r_hi = jnp.concatenate([jnp.where(place == FINE_ORDER[i], hi, 0.0) for i in range(16)], axis=0).astype(BF16)
    r_lo = jnp.concatenate([jnp.where(place == FINE_ORDER[i], lo, 0.0) for i in range(16)], axis=0).astype(BF16)
    pieces = []
    for e in range(2):
        u = mm(p_hi[e], r_hi, TN) + mm(p_hi[e], r_lo, TN) + mm(p_lo[e], r_hi, TN)
        pieces.append(u[:64, :64] + u[64:, 64:])
    hi, lo = split(jnp.concatenate(pieces, axis=1))
    rows = jnp.broadcast_to(dest[1:2].astype(F32), (16, 128)).astype(BF16)
    x = jnp.concatenate([hi, lo, rows], axis=0)
    out = []
    for q in range(0, XN * YN, 2):
        table = (iota((128, 128), 0) + q * 64 == dest[:1]).astype(F32).astype(BF16)
        g = mm(x, table, NT)
        v, at = g[:64] + g[64:128], g[128:136]
        out.append(jnp.concatenate([jnp.concatenate([v[:32, :64], v[32:, :64]], axis=1), at], axis=0))
        at = jnp.concatenate([at[:, 64:], at[:, :64]], axis=1)
        out.append(jnp.concatenate([jnp.concatenate([v[:32, 64:], v[32:, 64:]], axis=1), at], axis=0))
    return jnp.stack(out)


def fine_down(device, x, own, left, right, hi, lo, inverse, idx, owner, slot, p_hi, p_lo):
    spots, lines = [None] * 32, [None] * 32
    for e in range(2):
        for i in range(R0):
            j, at = owner[i, e], e * R0 + FINE_ORDER[i]
            t = (j >> 3) & (TN_ - 1)
            spots[at] = ((j >> 8) * XN + (t & (XN - 1))) * 16 + (t >> 2) * 2 + slot[i, e]
            lines[at] = (t >> 2) * 8 + (j & 7)
    dest = jnp.concatenate([lanes_of(spots), lanes_of(lines) + 1], axis=0)
    solution, residual = last_passes(
        device[0, 0], x, own, left, right, hi, lo, inverse, [idx[i] for i in range(3)]
    )
    return solution, restrict(dest, residual, p_hi, p_lo)


def fine_middle(device, x, left, right, rhs, hi, lo, inverse, idx):
    sides = (left[:, :64], right[:, :64])
    x1, send = first_passes(
        device[0, 0], x[:, :64], sides, rhs, hi, lo, inverse, [idx[i] for i in range(3)]
    )
    return x1, send


def fine_end(device, x, own, left, right, hi, lo, inverse, idx):
    solution, residual = last_passes(
        device[0, 0], x, own, left, right, hi, lo, inverse, [idx[i] for i in range(3)]
    )
    return rows_of(solution), rows_of(residual)


def prolong_parts(blocks):
    parts = [split(tiles(blocks[:, e, :])) for e in range(2)]
    return jnp.stack([p[0] for p in parts]), jnp.stack([p[1] for p in parts])


def line_windows(place, parts):
    sub = place[0, 1]
    total = jnp.zeros((128, 256), F32)
    for q in range(0, XN * YN, 2):
        v = jnp.concatenate(
            [jnp.concatenate([parts[q + i, :32, :64], parts[q + i, :32, 64:]], axis=0) for i in range(2)], axis=1
        )
        at = jnp.concatenate([parts[q + i, 32:33, :64] for i in range(2)], axis=1).astype(I32)
        table = (iota((256, 128), 0) + 1 == at).astype(F32).astype(BF16)
        total = total + mm(stacked(v), table, NT)
    x = stacked(total[:64] + total[64:])
    lane = iota((1, 128), 1)
    out = []
    for t in range(0, TN_, 2):
        spot = t + (lane >> 6)
        source = (spot + offset(lane, (sub - spot) & 3)) & (TN_ - 1)
        g = mm(x, one_hot(256, (source >> 2) * 32 + (lane & 31)), NN)
        g = g[:64] + g[64:]
        out += [jnp.concatenate([v[:32], v[32:]], axis=1) for v in (g[:, :64], g[:, 64:])]
    return (jnp.stack(out),)


def offset(lane, ahead):
    rel = jnp.where((lane & 32) == 0, ahead - 4, ahead)
    return jnp.where(((lane & 32) == 0) & (ahead == 0) & ((lane & 31) < 16), 4, rel)


def sum_all(parts):
    return (jnp.broadcast_to(jnp.sum(parts, axis=0)[None], (XN * YN, 32, 128)),)


A1_ROWS = 3 * R1 * 32
P1_ROWS = R1 * 32
A2_ROWS = 3 * R2 * 32
D1_AT = A1_ROWS + P1_ROWS
D2_AT = D1_AT + 64
IX_AT = D2_AT + 64
A2_AT = IX_AT + 8
PACK_ROWS = A2_AT + A2_ROWS


def level_pack(blocks, prolong, coarse, columns, coarse_columns):
    lines = [repeated(lanes_of([columns[i, k] for i in range(R1)]), 32) for k in range(3)]
    lines += [repeated(lanes_of([coarse_columns[i, k] for i in range(R2)]), 8) for k in range(3)]
    idx = jnp.concatenate(lines + [jnp.zeros((2, 128), I32)], axis=0).astype(F32)
    a1 = [tiles(blocks[k]) for k in range(3)]
    a2 = [lanes_in(coarse[k].reshape(R2 * 32, 128)) for k in range(3)]
    pad = jnp.zeros((256, 128), F32)
    d1 = 1.0 / diagonal_plain(jnp.concatenate([a1[0], pad], axis=0))[:, :32]
    pad = jnp.zeros((448, 128), F32)
    d2 = 1.0 / diagonal_plain(jnp.concatenate([a2[0], pad], axis=0))[:, :8]
    return (
        jnp.concatenate(
            a1
            + [tiles(prolong)]
            + [jnp.concatenate([d1] * 4, axis=1), jnp.concatenate([d2] * 16, axis=1), idx]
            + a2,
            axis=0,
        ),
    )


def diagonal_plain(m):
    return diagonal(m, PLAIN_ORDER)


STARTS = [0, 0, 0, 128]


def middle_prep(place, p0, m2, p2, crossed, swapped, far):
    slab = place[0, 0]
    even = (slab & 1) == 0
    top = A2_AT
    twin, twin_m2, twin_p2 = (swapped[i * PACK_ROWS : (i + 1) * PACK_ROWS] for i in range(3))
    far_twin = swapped[3 * PACK_ROWS :]
    far_low = jnp.where(even, far, far_twin)
    far_high = jnp.where(even, far_twin, far)
    m3 = jnp.where(even, crossed, twin_m2[:top])
    p3 = jnp.where(even, twin_p2[:top], crossed)
    m1 = jnp.where(even, twin_m2, twin)
    p1 = jnp.where(even, twin, twin_p2)
    packs = [m3, m2, m1, p0, p1, p2, p3]
    lane128 = iota((1, 128), 1)
    quarter = iota((64, 128), 1) >> 5
    tiled = [far_low] + [p[D1_AT : D1_AT + 64] for p in packs] + [far_high]
    d1 = []
    for q in range(3):
        v = jnp.zeros((64, 128), F32)
        for m in range(4):
            if q * 4 + m < 9:
                v = jnp.where(quarter == m, tiled[q * 4 + m], v)
        d1.append(v)
    d1 = jnp.concatenate(d1, axis=1)
    eighth = (iota((64, 128), 1) >> 3) & 7
    d2 = jnp.zeros((64, 128), F32)
    for m in range(7):
        d2 = jnp.where(eighth == m + 1, packs[m][D2_AT : D2_AT + 64], d2)
    d2 = d2[:, :64]
    ix = [p[IX_AT : IX_AT + 8].astype(I32) for p in packs]
    base = (slab - 4) * R1 * NRHS
    tables = []
    for c in range(4):
        for k in range(3):
            one = ix[2 * c - 1][k : k + 1] - base if c > 0 else jnp.full((1, 128), -1, I32)
            two = ix[2 * c][k : k + 1] - base
            at = jnp.where(((lane128 >> 5) & 1) == 0, one, two)
            tables.append(one_hot(256, at - STARTS[c]))
    c_tables = []
    c_base = (slab - 4) * R2 * NRHS
    group = (lane128 >> 3) & 7
    for k in range(3):
        at = jnp.full((1, 128), -1, I32)
        for m in range(1, 6):
            at = jnp.where(group == m + 1, ix[m][3 + k : 4 + k] - c_base, at)
        c_tables.append(one_hot(64, at))
    halves = [split(p[:D1_AT]) for p in packs]
    coarse = [split(p[A2_AT:]) for p in packs[1:6]]
    return (
        jnp.stack([h[0] for h in halves]),
        jnp.stack([h[1] for h in halves]),
        jnp.stack([h[0] for h in coarse]),
        jnp.stack([h[1] for h in coarse]),
        d1,
        d2,
        jnp.stack(tables),
        jnp.stack(c_tables),
    )


def middle(place, parts, b_hi, b_lo, q_hi, q_lo, d1, d2, tables, c_tables, unpack):
    slab, sub = place[0, 0], place[0, 1]
    blocks = (b_hi, b_lo)
    lane128 = iota((1, 128), 1)
    pieces = []
    for x in range(XN):
        spot = slab & (TN_ - 1)
        at = spot + offset(lane128, (x - spot) & 3)
        row = (slab >> 5) + jnp.where(at < 0, -1, jnp.where(at >= TN_, 1, 0))
        row = jnp.broadcast_to(row, (32, 128))
        w = jnp.zeros((32, 128), F32)
        for y in range(YN):
            w = jnp.where(row == y, parts[y * XN + x], w)
        pieces.append(jnp.concatenate([w[:, :64], w[:, 64:]], axis=0))
    g = mm(stacked(jnp.concatenate(pieces, axis=1)), one_hot(256, unpack), NN)
    rhs = g[:64] + g[64:]
    def rows(part, m, start, count):
        return blocks[part][max(m, 0), start : start + count]

    def pair(part, c, start, count):
        return jnp.concatenate(
            [rows(part, 2 * c - 1, start, count), rows(part, 2 * c, start, count)], axis=0
        )

    a_hi = [[pair(0, c, k * 256, 256) for k in range(3)] for c in range(4)]
    a_lo = [[pair(1, c, k * 256, 256) for k in range(3)] for c in range(4)]

    def apply1(v, chunks):
        x = stacked(v)
        return [
            forward(
                a_hi[c], a_lo[c], [gathered(x[:, STARTS[c] : STARTS[c] + 256], tables[3 * c + k]) for k in range(3)], PLAIN_ORDER
            )
            for c in chunks
        ]

    tail = jnp.zeros((64, 128), F32)
    inv = d1[:, :256]
    d = d1 * rhs / CENTER
    y = d[:, :256]
    r = rhs[:, :256] - jnp.concatenate(apply1(d, range(4)), axis=1)
    for t in range(2):
        step = KEEP[t] * d[:, :256] + GAIN[t] * (inv * r)
        d = jnp.concatenate([step, tail], axis=1)
        y = y + step
        r = r - jnp.concatenate(apply1(d, range(4)), axis=1)
    x = stacked(r)
    low = iota((32, 128), 1) < 64
    q_lane = (iota((32, 128), 1) & 63) >> 2
    first = (lane128 & 63) >> 2
    r_hi, r_lo = [], []
    for kk in range(4):
        g = mm(x, one_hot(256, first * 16 + kk * 4 + (lane128 & 3)), NN)
        r_hi.append(jnp.where(low, g[:32], g[32:64]))
        r_lo.append(jnp.where(low, g[64:96], g[96:128]))
    u = jnp.zeros((128, 128), F32)
    for m in range(7):
        keep = [q_lane == 2 * (m + 1) + j // 4 for j in range(R1)]
        b_hi = jnp.concatenate([jnp.where(keep[j], r_hi[j % 4], 0.0) for j in range(R1)], axis=0).astype(BF16)
        b_lo = jnp.concatenate([jnp.where(keep[j], r_lo[j % 4], 0.0) for j in range(R1)], axis=0).astype(BF16)
        p_hi, p_lo = rows(0, m, A1_ROWS, P1_ROWS), rows(1, m, A1_ROWS, P1_ROWS)
        u = u + mm(p_hi, b_hi, TN) + mm(p_hi, b_lo, TN) + mm(p_lo, b_hi, TN)
    r = u[:64, :64] + u[64:, 64:]
    c_hi, c_lo = [], []
    for k in range(3):
        near = [min(max(m - 2, 0), 4) for m in range(8)]
        c_hi.append(jnp.concatenate([q_hi[n, k * 64 : k * 64 + 64] for n in near], axis=0))
        c_lo.append(jnp.concatenate([q_lo[n, k * 64 : k * 64 + 64] for n in near], axis=0))
    d = d2 * r / CENTER
    z = d
    for t in range(3):
        s = stacked(d)
        r = r - forward(c_hi, c_lo, [gathered(s, c_tables[k]) for k in range(3)], PLAIN_ORDER)
        d = KEEP[t] * d + GAIN[t] * (d2 * r)
        z = z + d
    s = stacked(z)
    new = []
    for c in (1, 2):
        at = ((16 * c + ((lane128 & 63) >> 2)) >> 2) * 4 + (lane128 & 3)
        lift = forward(
            [pair(0, c, A1_ROWS, P1_ROWS)], [pair(1, c, A1_ROWS, P1_ROWS)], [gathered(s, one_hot(64, at))], PLAIN_ORDER
        )
        new.append(y[:, c * 64 : c * 64 + 64] + lift)
    y = jnp.concatenate([y[:, :64], new[0], new[1], y[:, 192:256], tail], axis=1)
    side = jnp.zeros((64, 64), F32)

    def at_centre(v):
        return jnp.concatenate([side, v, side, tail], axis=1)

    inv = inv[:, 64:192]
    r = rhs[:, 64:192] - jnp.concatenate(apply1(y, (1, 2)), axis=1)
    d = inv * r / CENTER
    y = y[:, 64:192] + d
    r = r - jnp.concatenate(apply1(at_centre(d), (1, 2)), axis=1)
    d = KEEP[0] * d + GAIN[0] * (inv * r)
    y = y + d
    r = r[:, 64:] - apply1(at_centre(d), (2,))[0]
    own = y[:, 64:] + KEEP[1] * d[:, 64:] + GAIN[1] * (inv[:, 64:] * r)
    pick_rows = (iota((8, 64), 1) == iota((8, 64), 0) + sub * 8).astype(F32).astype(BF16)
    hi, lo = split(own)
    o = mm(pick_rows, hi, NT) + mm(pick_rows, lo, NT)
    o = jnp.concatenate([jnp.concatenate([o[:2], o[4:6]], axis=1), jnp.concatenate([o[2:4], o[6:]], axis=1)], axis=1)
    return (jnp.broadcast_to(o[None], (TN_, 2, 256)),)


def level_cycle(place, parts, p0, m2, p2, crossed, swapped, far, unpack):
    return middle(place, parts, *middle_prep(place, p0, m2, p2, crossed, swapped, far), unpack)


def fine_up(owner_ref, all_ref, x_ref, hi_ref, lo_ref, out_ref, line):
    for n in range(32):
        e, i = n // R0, n % R0
        p, j = e * R0 + FINE_ORDER[i], owner_ref[i, e]
        v = all_ref[((j >> 8) * XN + ((j & 7) >> 1)) * TN_ + ((j >> 3) & (TN_ - 1))]
        v = jnp.concatenate([v[:, :128], v[:, 128:]], axis=0)
        line[p * 4 : p * 4 + 4, :] = jnp.where((j & 1) == 1, pltpu.roll(v, 64, 1), v)
    w = line[:, :64].T
    hi, lo = split(w)
    hi, lo = hi.astype(F32), lo.astype(F32)
    rights = [
        spread(double(hi[:, e * 64 : e * 64 + 64]), double(lo[:, e * 64 : e * 64 + 64])) for e in range(2)
    ]
    x = x_ref[...] + forward([hi_ref[0], hi_ref[1]], [lo_ref[0], lo_ref[1]], rights, FINE_ORDER)
    out_ref[...] = double(x)


def fine_up_call(owner, gathered_rows, x, hi, lo):
    smem, vmem = pl.BlockSpec(memory_space=pltpu.SMEM), pl.BlockSpec(memory_space=pltpu.VMEM)
    return pl.pallas_call(
        fine_up,
        in_specs=[smem, vmem, vmem, vmem, vmem],
        out_specs=vmem,
        out_shape=jax.ShapeDtypeStruct((64, 128), F32),
        scratch_shapes=[pltpu.VMEM((128, 128), F32)],
        compiler_params=pltpu.CompilerParams(vmem_limit_bytes=32 << 20),
        name="fine_up",
    )(owner, gathered_rows, x, hi, lo)


XY = [[(y * TN_ + t) * XN + x for y in range(YN) for x in range(XN)] for t in range(TN_)]
ZC = [[y * TN_ + t for t in range(TN_)] for y in range(YN)]


def across(value):
    return lax.all_to_all(value, ("slab", "sub"), 0, 0, tiled=True, axis_index_groups=XY)


def along(value):
    return lax.all_to_all(value, "slab", 0, 0, tiled=True, axis_index_groups=ZC)


def shifted(value, axis, by):
    n = lax.axis_size(axis)
    return lax.ppermute(value, axis, [(i, i + by) for i in range(n) if 0 <= i + by < n])


def unpack_table(spot):
    lane = jnp.arange(384, dtype=I32)
    rel, row = lane // 32 - 4, (lane % 32) // 4
    x = (spot + rel) % XN
    part = ((rel >= 0) & (rel < 4)).astype(I32)
    idx = x * 64 + part * 32 + lane % 32
    keep = (rel <= 4) & ((rel < 4) | (row < 4)) & ((rel > -4) | (row >= 4))
    return jnp.where(keep, idx, -1).reshape(1, 384)


def body(
    right_side,
    warm_start,
    fine_blocks,
    fine_columns,
    fine_prolong,
    owner_rows,
    send_slots,
    receive_rows,
    middle_blocks,
    middle_columns,
    middle_prolong,
    coarse_blocks,
    coarse_columns,
):
    both = ("slab", "sub")
    slab = lax.axis_index("slab").astype(I32)
    sub = lax.axis_index("sub").astype(I32)
    device = (slab * XN + sub).reshape(1, 1)
    place = jnp.stack([slab, sub]).reshape(1, 2)

    (own,) = kern(payload, [((8, 4096), F32)], [warm_start, right_side, fine_columns], smem=(2,))
    blocks = fine_blocks.transpose(1, 0, 2)
    low, high = (jnp.concatenate([part, own[None]], axis=0) for part in (blocks[:, :8], blocks[:, 8:]))
    middle_columns, low, high = lax.optimization_barrier((middle_columns, low, high))
    left, right = shifted(high, both, 1), shifted(low, both, -1)

    (pack,) = kern(
        level_pack,
        [((PACK_ROWS, 128), F32)],
        [middle_blocks.transpose(1, 0, 2), middle_prolong, coarse_blocks.transpose(1, 0, 2), middle_columns, coarse_columns],
        smem=(3, 4),
    )
    m2, p2 = shifted(pack, "slab", 2), shifted(pack, "slab", -2)
    count = lax.axis_size("slab")

    def crossing(value, by):
        pairs = [(i, i + by if i % 2 == by % 2 else i - by) for i in range(count)]
        return lax.ppermute(value, "slab", [p for p in pairs if 0 <= p[1] < count])

    p_hi, p_lo = kern(prolong_parts, [((2, 512, 128), BF16)] * 2, [fine_prolong])

    sends = ((64, 128), F32)
    hi, lo, inverse, rhs, x1, send, idx = kern(
        fine_start,
        [((2, 3, 512, 128), BF16)] * 2 + [sends, sends, ((64, 64), F32), sends, ((3, 3, 128), I32)],
        [device, own, left, right, blocks],
        smem=(0,),
        own=range(1, 5),
    )
    left, right = shifted(send, both, 1), shifted(send, both, -1)
    left, right, pack = lax.optimization_barrier((left, right, pack))
    crossed = crossing(pack[:A2_AT], 3)
    x3, dense = kern(
        fine_down,
        [((64, 64), F32), ((16, 40, 128), F32)],
        [device, x1, send, left, right, hi, lo, inverse, idx, owner_rows, send_slots, p_hi, p_lo],
        smem=(0, 9, 10),
    )

    dense, m2, p2 = lax.optimization_barrier((dense, m2, p2))
    (part,) = kern(line_windows, [((TN_, 32, 128), F32)], [place, across(dense)], smem=(0,))
    part, m2, p2, crossed, pack = lax.optimization_barrier((part, m2, p2, crossed, pack))
    twin = jnp.concatenate([pack, m2, p2, crossed[D1_AT : D1_AT + 64]], axis=0)
    twin = lax.ppermute(twin, "slab", [(i, i ^ 1) for i in range(count)])
    far = crossing(pack[D1_AT : D1_AT + 64], 4)
    (part,) = kern(sum_all, [((XN * YN, 32, 128), F32)], [along(part)])
    part = across(part)

    (share,) = kern(
        level_cycle,
        [((TN_, 2, 256), F32)],
        [place, part, pack, m2, p2, crossed, twin, far, unpack_table(slab % TN_)],
        smem=(0,),
        own=range(2, 8),
    )
    line = along(share)
    every = across(jnp.broadcast_to(line[None], (XN * YN, TN_, 2, 256)))
    x = fine_up_call(owner_rows, every.reshape(XN * YN * TN_, 2, 256), x3, p_hi, p_lo)

    x1, send = kern(
        fine_middle,
        [((64, 64), F32), sends],
        [device, x, shifted(x, both, 1), shifted(x, both, -1), rhs, hi, lo, inverse, idx],
        smem=(0,),
    )
    return tuple(
        kern(
            fine_end,
            [((NRHS, 1024), F32)] * 2,
            [device, x1, send, shifted(send, both, 1), shifted(send, both, -1), hi, lo, inverse, idx],
            smem=(0,),
        )
    )


def solution(mesh):
    in_specs = (
        P(None, ("slab", "sub")),
        P(None, ("slab", "sub")),
        P(("slab", "sub"), None, None),
        P(("slab", "sub"), None),
        P(("slab", "sub"), None, None),
        P(("slab", "sub"), None),
        P(("slab", "sub"), None),
        P("slab", "sub", None, None),
        P("slab", None, None),
        P("slab", None),
        P("slab", None),
        P("slab", None, None),
        P("slab", None),
    )
    out_specs = (P(None, ("slab", "sub")), P(None, ("slab", "sub")))
    return jax.shard_map(body, mesh=mesh, in_specs=in_specs, out_specs=out_specs, check_vma=False)
```

```python
import jax
import jax.numpy as jnp
from jax import lax
from jax.experimental import pallas as pl
from jax.experimental.pallas import tpu as pltpu
from jax.sharding import PartitionSpec as P

F32 = jnp.float32
BF16 = jnp.bfloat16
I32 = jnp.int32
BS = 64
NRHS = 4
R0 = 16
R1 = 8
R2 = 2
XN = 4
YN = 4
TN_ = 32

CENTER = 0.5 * (2.2 + 0.3)
HALF = 0.5 * (2.2 - 0.3)
SCALED = CENTER / HALF
FACTORS = [1.0 / SCALED]
for _ in range(3):
    FACTORS.append(1.0 / (2.0 * SCALED - FACTORS[-1]))
KEEP = [FACTORS[t + 1] * FACTORS[t] for t in range(3)]
GAIN = [2.0 * FACTORS[t + 1] / HALF for t in range(3)]

NN = ((1,), (0,))
NT = ((1,), (1,))
TN = ((0,), (0,))

FINE_ORDER = [(i % 2) * 8 + i // 2 for i in range(R0)]
RIM_ORDER = FINE_ORDER[8:] + FINE_ORDER[:8]
PLAIN_ORDER = list(range(16))


def kern(body, outs, args, smem=(), own=(), own_outs=False):
    count = len(args)

    def kernel(*refs):
        ins = [r if i in smem else r[...] for i, r in enumerate(refs[:count])]
        for ref, value in zip(refs[count:], body(*ins)):
            ref[...] = value

    vmem = pl.BlockSpec(memory_space=pltpu.VMEM)
    specs = [
        pl.BlockSpec(memory_space=pltpu.SMEM) if i in smem else pl.BlockSpec() if i in own else vmem
        for i in range(count)
    ]
    return pl.pallas_call(
        kernel,
        in_specs=specs,
        out_specs=[pl.BlockSpec() if own_outs else vmem for _ in outs],
        out_shape=[jax.ShapeDtypeStruct(s, d) for s, d in outs],
        compiler_params=pltpu.CompilerParams(vmem_limit_bytes=32 << 20),
        name=body.__name__,
    )(*args)


def mm(a, b, dims):
    return lax.dot_general(a, b, (dims, ((), ())), preferred_element_type=F32)


def iota(shape, dim):
    return lax.broadcasted_iota(I32, shape, dim)


def split(v):
    hi = v.astype(BF16)
    return hi, (v - hi.astype(F32)).astype(BF16)


def stacked(v):
    hi, lo = split(v)
    return jnp.concatenate([hi, lo], axis=0)


def one_hot(size, idx):
    return (iota((size, idx.shape[1]), 0) == idx).astype(F32).astype(BF16)


def lanes_in(x):
    lane = iota(x.shape, 1)
    place = lane & 63
    return jnp.take_along_axis(x, (lane & 64) + 2 * (place & 31) + (place >> 5), axis=1)


def lanes_out(x):
    lane = iota(x.shape, 1)
    b = lane & 63
    return jnp.take_along_axis(x, (lane & 64) + (b & 1) * 32 + (b >> 1), axis=1)


def tiles(raw):
    return lanes_in(raw.reshape(raw.shape[0] * 32, 128))


def double(g):
    return jnp.concatenate([g, g], axis=1)


def spread(hi, lo):
    low = iota(hi.shape, 1) < 64
    zero = jnp.zeros_like(hi)
    top = jnp.concatenate([jnp.where(low, hi, zero), jnp.where(low, lo, zero)], axis=1)
    bottom = jnp.concatenate([jnp.where(low, zero, hi), jnp.where(low, zero, lo)], axis=1)
    return jnp.concatenate([top, bottom], axis=0).astype(BF16)


def gathered(x, table):
    g = mm(x, table, NN)
    return spread(g[:64], g[64:])


def pick(t, order):
    lane = iota((32, 128), 1)
    place = (lane & 63) >> 2
    y = jnp.zeros((32, 128), F32)
    for i in range(16):
        y = y + jnp.where(place == order[i], t[i * 32 : i * 32 + 32], 0.0)
    return jnp.concatenate([y[:, :64], y[:, 64:]], axis=0)


def forward(his, los, rights, order):
    hi = jnp.concatenate(his, axis=1) if len(his) > 1 else his[0]
    lo = jnp.concatenate(los, axis=1) if len(los) > 1 else los[0]
    right = jnp.concatenate(rights, axis=0) if len(rights) > 1 else rights[0]
    a = mm(hi, right, NN)
    return pick(a[:, :128] + a[:, 128:] + mm(lo, right[:, :128], NN), order)


def diagonal(m, order):
    sub = iota(m.shape, 0) & 31
    lane = iota(m.shape, 1)
    kept = jnp.where((lane == sub) | (lane == sub + 96), m, 0.0)
    ones = ((iota((128, 128), 0) >> 6) == (iota((128, 128), 1) >> 6)).astype(F32).astype(BF16)
    hi, lo = split(kept)
    return pick(mm(hi, ones, NN) + mm(lo, ones, NN), order)


def columns_of(rows):
    z = lanes_in(jnp.concatenate([rows[:, m * 128 : m * 128 + 128] for m in range(8)], axis=0))
    t = z.T
    return jnp.concatenate([t[:64], t[64:]], axis=1)


def rows_of(v):
    t = lanes_out(jnp.concatenate([v[:, :32], v[:, 32:]], axis=0).T)
    return jnp.concatenate([t[m * 4 : m * 4 + 4] for m in range(8)], axis=1)


def rim(left, right):
    lane = iota(left.shape, 1)
    return jnp.where((((lane & 63) >> 2) & 7) < 4, right, left)


def fine_tables(device, own, left, right):
    wide, near = [], []
    for k in range(3):
        g = own[k : k + 1]
        r = rim(left[k : k + 1], right[k : k + 1])
        base = (device - 1) * 64
        wide.append([one_hot(192, g - base), one_hot(192, r - base)])
        near.append(one_hot(128, (g & 63) + jnp.where((g >> 6) == device, 0, 64)))
    return wide, near


def fine_both(hi, lo, x, wide):
    return jnp.concatenate(
        [
            forward(
                [hi[c, k] for k in range(3)],
                [lo[c, k] for k in range(3)],
                [gathered(x, wide[k][c]) for k in range(3)],
                (FINE_ORDER, RIM_ORDER)[c],
            )
            for c in range(2)
        ],
        axis=1,
    )


def fine_own(hi, lo, x, near):
    return forward(
        [hi[0, k] for k in range(3)],
        [lo[0, k] for k in range(3)],
        [gathered(x, near[k]) for k in range(3)],
        FINE_ORDER,
    )


def first_passes(device, x, sides, rhs, hi, lo, inverse, idx):
    wide, near = fine_tables(device, *idx)
    window = stacked(jnp.concatenate([sides[0], x, sides[1]], axis=1))
    r = rhs - fine_both(hi, lo, window, wide)
    d = inverse * r / CENTER
    r1 = r[:, :64] - fine_own(hi, lo, stacked(d), near)
    d1 = d[:, :64]
    d2 = KEEP[0] * d1 + GAIN[0] * (inverse[:, :64] * r1)
    return x + d1, jnp.concatenate([d2, r1], axis=1)


def last_passes(device, x, own, left, right, hi, lo, inverse, idx):
    wide, near = fine_tables(device, *idx)
    window = stacked(jnp.concatenate([left[:, :64], own[:, :64], right[:, :64]], axis=1))
    rims = rim(jnp.concatenate([left[:, 64:]] * 2, axis=1), jnp.concatenate([right[:, 64:]] * 2, axis=1))
    rim_d = rim(double(left[:, :64]), double(right[:, :64]))
    r = jnp.concatenate([own[:, 64:], rims[:, :64]], axis=1) - fine_both(hi, lo, window, wide)
    d_old = jnp.concatenate([own[:, :64], rim_d[:, :64]], axis=1)
    d = KEEP[1] * d_old + GAIN[1] * (inverse * r)
    residual = r[:, :64] - fine_own(hi, lo, stacked(d), near)
    return x + own[:, :64] + d[:, :64], residual


def indices(payload):
    return payload[:3, 1024:1152].astype(I32)


def fine_start(device, own, left_all, right_all, own_blocks):
    parts = []
    for k in range(3):
        parts.append(tiles(own_blocks[k]))
    for k in range(3):
        parts.append(jnp.concatenate([tiles(left_all[k]), tiles(right_all[k])], axis=0))
    entries = jnp.concatenate([diagonal(parts[0], FINE_ORDER), diagonal(parts[3], RIM_ORDER)], axis=1)
    inverse = jnp.where(entries == 0.0, 0.0, 1.0 / entries)
    pairs = [split(p) for p in parts]
    hi = jnp.stack([p[0] for p in pairs]).reshape(2, 3, 512, 128)
    lo = jnp.stack([p[1] for p in pairs]).reshape(2, 3, 512, 128)
    left, right = left_all[3], right_all[3]
    x = [columns_of(p[:4, :1024]) for p in (left, own, right)]
    b = [columns_of(p[4:, :1024]) for p in (left, own, right)]
    rhs = jnp.concatenate([b[1], rim(b[0], b[2])], axis=1)
    idx = [indices(p) for p in (own, left, right)]
    x1, send = first_passes(device[0, 0], x[1], (x[0], x[2]), rhs, hi, lo, inverse, idx)
    return hi, lo, inverse, rhs, x1, send, jnp.stack(idx)


def lanes_of(values, first=0):
    lane = iota((1, 128), 1)
    v = jnp.zeros((1, 128), I32)
    for n, value in enumerate(values):
        v = jnp.where((lane >> 2) == first + n, value * NRHS + (lane & 3), v)
    return v


def repeated(v, width):
    shift = width
    while shift < 128:
        v = v + pltpu.roll(v, shift, 1)
        shift *= 2
    return v


def payload(x, b, columns, blocks):
    lines = []
    for k in range(3):
        values = [None] * R0
        for i in range(R0):
            g = columns[i, k]
            values[FINE_ORDER[i]] = (g >> 4) * 16 + (g & 1) * 8 + ((g & 15) >> 1)
        lines.append(repeated(lanes_of(values), 64))
    v = jnp.concatenate(lines + [jnp.zeros((5, 128), I32)], axis=0).astype(F32)
    v = jnp.concatenate([jnp.concatenate([x, b], axis=0), v, jnp.zeros((8, 2944), F32)], axis=1)[None]
    return [v[0]] + [jnp.concatenate([part, v], axis=0) for part in (blocks[:, :8], blocks[:, 8:])]


def restrict(dest, residual, p_hi, p_lo):
    both = jnp.concatenate([residual[:32], residual[32:]], axis=1)
    place = (iota((32, 128), 1) & 63) >> 2
    hi, lo = split(both)
    hi, lo = hi.astype(F32), lo.astype(F32)
    r_hi = jnp.concatenate([jnp.where(place == FINE_ORDER[i], hi, 0.0) for i in range(16)], axis=0).astype(BF16)
    r_lo = jnp.concatenate([jnp.where(place == FINE_ORDER[i], lo, 0.0) for i in range(16)], axis=0).astype(BF16)
    pieces = []
    for e in range(2):
        u = mm(p_hi[e], r_hi, TN) + mm(p_hi[e], r_lo, TN) + mm(p_lo[e], r_hi, TN)
        pieces.append(u[:64, :64] + u[64:, 64:])
    hi, lo = split(jnp.concatenate(pieces, axis=1))
    rows = jnp.broadcast_to(dest[1:2].astype(F32), (16, 128)).astype(BF16)
    x = jnp.concatenate([hi, lo, rows], axis=0)
    out = []
    for q in range(0, XN * YN, 2):
        table = (iota((128, 128), 0) + q * 64 == dest[:1]).astype(F32).astype(BF16)
        g = mm(x, table, NT)
        v, at = g[:64] + g[64:128], g[128:136]
        out.append(jnp.concatenate([jnp.concatenate([v[:32, :64], v[32:, :64]], axis=1), at], axis=0))
        at = jnp.concatenate([at[:, 64:], at[:, :64]], axis=1)
        out.append(jnp.concatenate([jnp.concatenate([v[:32, 64:], v[32:, 64:]], axis=1), at], axis=0))
    return jnp.stack(out)


def fine_down(device, x, own, left, right, hi, lo, inverse, idx, owner, slot, p_hi, p_lo):
    spots, lines = [None] * 32, [None] * 32
    for e in range(2):
        for i in range(R0):
            j, at = owner[i, e], e * R0 + FINE_ORDER[i]
            t = (j >> 3) & (TN_ - 1)
            spots[at] = ((j >> 8) * XN + (t & (XN - 1))) * 16 + (t >> 2) * 2 + slot[i, e]
            lines[at] = (t >> 2) * 8 + (j & 7)
    dest = jnp.concatenate([lanes_of(spots), lanes_of(lines) + 1], axis=0)
    solution, residual = last_passes(
        device[0, 0], x, own, left, right, hi, lo, inverse, [idx[i] for i in range(3)]
    )
    return solution, restrict(dest, residual, p_hi, p_lo)


def fine_middle(device, x, left, right, rhs, hi, lo, inverse, idx):
    sides = (left[:, :64], right[:, :64])
    x1, send = first_passes(
        device[0, 0], x[:, :64], sides, rhs, hi, lo, inverse, [idx[i] for i in range(3)]
    )
    return x1, send


def fine_end(device, x, own, left, right, hi, lo, inverse, idx):
    solution, residual = last_passes(
        device[0, 0], x, own, left, right, hi, lo, inverse, [idx[i] for i in range(3)]
    )
    return rows_of(solution), rows_of(residual)


def prolong_parts(blocks):
    parts = [split(tiles(blocks[:, e, :])) for e in range(2)]
    return jnp.stack([p[0] for p in parts]), jnp.stack([p[1] for p in parts])


def line_windows(place, parts):
    sub = place[0, 1]
    total = jnp.zeros((128, 256), F32)
    for q in range(0, XN * YN, 2):
        v = jnp.concatenate(
            [jnp.concatenate([parts[q + i, :32, :64], parts[q + i, :32, 64:]], axis=0) for i in range(2)], axis=1
        )
        at = jnp.concatenate([parts[q + i, 32:33, :64] for i in range(2)], axis=1).astype(I32)
        table = (iota((256, 128), 0) + 1 == at).astype(F32).astype(BF16)
        total = total + mm(stacked(v), table, NT)
    x = stacked(total[:64] + total[64:])
    lane = iota((1, 128), 1)
    out = []
    for t in range(0, TN_, 2):
        spot = t + (lane >> 6)
        source = (spot + offset(lane, (sub - spot) & 3)) & (TN_ - 1)
        g = mm(x, one_hot(256, (source >> 2) * 32 + (lane & 31)), NN)
        g = g[:64] + g[64:]
        out += [jnp.concatenate([v[:32], v[32:]], axis=1) for v in (g[:, :64], g[:, 64:])]
    return (jnp.stack(out),)


def offset(lane, ahead):
    rel = jnp.where((lane & 32) == 0, ahead - 4, ahead)
    return jnp.where(((lane & 32) == 0) & (ahead == 0) & ((lane & 31) < 16), 4, rel)


def sum_all(parts):
    return (jnp.broadcast_to(jnp.sum(parts, axis=0)[None], (XN * YN, 32, 128)),)


A1_ROWS = 3 * R1 * 32
P1_ROWS = R1 * 32
A2_ROWS = 3 * R2 * 32
D1_AT = A1_ROWS + P1_ROWS
D2_AT = D1_AT + 64
IX_AT = D2_AT + 64
A2_AT = IX_AT + 8
PACK_ROWS = A2_AT + A2_ROWS


def level_pack(blocks, prolong, coarse, columns, coarse_columns):
    lines = [repeated(lanes_of([columns[i, k] for i in range(R1)]), 32) for k in range(3)]
    lines += [repeated(lanes_of([coarse_columns[i, k] for i in range(R2)]), 8) for k in range(3)]
    idx = jnp.concatenate(lines + [jnp.zeros((2, 128), I32)], axis=0).astype(F32)
    a1 = [tiles(blocks[k]) for k in range(3)]
    a2 = [lanes_in(coarse[k].reshape(R2 * 32, 128)) for k in range(3)]
    pad = jnp.zeros((256, 128), F32)
    d1 = 1.0 / diagonal_plain(jnp.concatenate([a1[0], pad], axis=0))[:, :32]
    pad = jnp.zeros((448, 128), F32)
    d2 = 1.0 / diagonal_plain(jnp.concatenate([a2[0], pad], axis=0))[:, :8]
    return (
        jnp.concatenate(
            a1
            + [tiles(prolong)]
            + [jnp.concatenate([d1] * 4, axis=1), jnp.concatenate([d2] * 16, axis=1), idx]
            + a2,
            axis=0,
        ),
    )


def diagonal_plain(m):
    return diagonal(m, PLAIN_ORDER)


STARTS = [0, 0, 0, 128]


def middle_prep(place, p0, m2, p2, crossed, swapped, far):
    slab = place[0, 0]
    even = (slab & 1) == 0
    top = A2_AT
    twin, twin_m2, twin_p2 = (swapped[i * PACK_ROWS : (i + 1) * PACK_ROWS] for i in range(3))
    far_twin = swapped[3 * PACK_ROWS :]
    far_low = jnp.where(even, far, far_twin)
    far_high = jnp.where(even, far_twin, far)
    m3 = jnp.where(even, crossed, twin_m2[:top])
    p3 = jnp.where(even, twin_p2[:top], crossed)
    m1 = jnp.where(even, twin_m2, twin)
    p1 = jnp.where(even, twin, twin_p2)
    packs = [m3, m2, m1, p0, p1, p2, p3]
    lane128 = iota((1, 128), 1)
    quarter = iota((64, 128), 1) >> 5
    tiled = [far_low] + [p[D1_AT : D1_AT + 64] for p in packs] + [far_high]
    d1 = []
    for q in range(3):
        v = jnp.zeros((64, 128), F32)
        for m in range(4):
            if q * 4 + m < 9:
                v = jnp.where(quarter == m, tiled[q * 4 + m], v)
        d1.append(v)
    d1 = jnp.concatenate(d1, axis=1)
    eighth = (iota((64, 128), 1) >> 3) & 7
    d2 = jnp.zeros((64, 128), F32)
    for m in range(7):
        d2 = jnp.where(eighth == m + 1, packs[m][D2_AT : D2_AT + 64], d2)
    d2 = d2[:, :64]
    ix = [p[IX_AT : IX_AT + 8].astype(I32) for p in packs]
    base = (slab - 4) * R1 * NRHS
    tables = []
    for c in range(4):
        for k in range(3):
            one = ix[2 * c - 1][k : k + 1] - base if c > 0 else jnp.full((1, 128), -1, I32)
            two = ix[2 * c][k : k + 1] - base
            at = jnp.where(((lane128 >> 5) & 1) == 0, one, two)
            tables.append(one_hot(256, at - STARTS[c]))
    c_tables = []
    c_base = (slab - 4) * R2 * NRHS
    group = (lane128 >> 3) & 7
    for k in range(3):
        at = jnp.full((1, 128), -1, I32)
        for m in range(1, 6):
            at = jnp.where(group == m + 1, ix[m][3 + k : 4 + k] - c_base, at)
        c_tables.append(one_hot(64, at))
    halves = [split(p[:D1_AT]) for p in packs]
    coarse = [split(p[A2_AT:]) for p in packs[1:6]]
    return (
        jnp.stack([h[0] for h in halves]),
        jnp.stack([h[1] for h in halves]),
        jnp.stack([h[0] for h in coarse]),
        jnp.stack([h[1] for h in coarse]),
        d1,
        d2,
        jnp.stack(tables),
        jnp.stack(c_tables),
    )


def middle(place, parts, b_hi, b_lo, q_hi, q_lo, d1, d2, tables, c_tables, unpack):
    slab, sub = place[0, 0], place[0, 1]
    blocks = (b_hi, b_lo)
    lane128 = iota((1, 128), 1)
    pieces = []
    for x in range(XN):
        spot = slab & (TN_ - 1)
        at = spot + offset(lane128, (x - spot) & 3)
        row = (slab >> 5) + jnp.where(at < 0, -1, jnp.where(at >= TN_, 1, 0))
        row = jnp.broadcast_to(row, (32, 128))
        w = jnp.zeros((32, 128), F32)
        for y in range(YN):
            w = jnp.where(row == y, parts[y * XN + x], w)
        pieces.append(jnp.concatenate([w[:, :64], w[:, 64:]], axis=0))
    g = mm(stacked(jnp.concatenate(pieces, axis=1)), one_hot(256, unpack), NN)
    rhs = g[:64] + g[64:]
    def rows(part, m, start, count):
        return blocks[part][max(m, 0), start : start + count]

    def pair(part, c, start, count):
        return jnp.concatenate(
            [rows(part, 2 * c - 1, start, count), rows(part, 2 * c, start, count)], axis=0
        )

    a_hi = [[pair(0, c, k * 256, 256) for k in range(3)] for c in range(4)]
    a_lo = [[pair(1, c, k * 256, 256) for k in range(3)] for c in range(4)]

    def apply1(v, chunks):
        x = stacked(v)
        return [
            forward(
                a_hi[c], a_lo[c], [gathered(x[:, STARTS[c] : STARTS[c] + 256], tables[3 * c + k]) for k in range(3)], PLAIN_ORDER
            )
            for c in chunks
        ]

    tail = jnp.zeros((64, 128), F32)
    inv = d1[:, :256]
    d = d1 * rhs / CENTER
    y = d[:, :256]
    r = rhs[:, :256] - jnp.concatenate(apply1(d, range(4)), axis=1)
    for t in range(2):
        step = KEEP[t] * d[:, :256] + GAIN[t] * (inv * r)
        d = jnp.concatenate([step, tail], axis=1)
        y = y + step
        r = r - jnp.concatenate(apply1(d, range(4)), axis=1)
    x = stacked(r)
    low = iota((32, 128), 1) < 64
    q_lane = (iota((32, 128), 1) & 63) >> 2
    first = (lane128 & 63) >> 2
    r_hi, r_lo = [], []
    for kk in range(4):
        g = mm(x, one_hot(256, first * 16 + kk * 4 + (lane128 & 3)), NN)
        r_hi.append(jnp.where(low, g[:32], g[32:64]))
        r_lo.append(jnp.where(low, g[64:96], g[96:128]))
    u = jnp.zeros((128, 128), F32)
    for m in range(7):
        keep = [q_lane == 2 * (m + 1) + j // 4 for j in range(R1)]
        b_hi = jnp.concatenate([jnp.where(keep[j], r_hi[j % 4], 0.0) for j in range(R1)], axis=0).astype(BF16)
        b_lo = jnp.concatenate([jnp.where(keep[j], r_lo[j % 4], 0.0) for j in range(R1)], axis=0).astype(BF16)
        p_hi, p_lo = rows(0, m, A1_ROWS, P1_ROWS), rows(1, m, A1_ROWS, P1_ROWS)
        u = u + mm(p_hi, b_hi, TN) + mm(p_hi, b_lo, TN) + mm(p_lo, b_hi, TN)
    r = u[:64, :64] + u[64:, 64:]
    c_hi, c_lo = [], []
    for k in range(3):
        near = [min(max(m - 2, 0), 4) for m in range(8)]
        c_hi.append(jnp.concatenate([q_hi[n, k * 64 : k * 64 + 64] for n in near], axis=0))
        c_lo.append(jnp.concatenate([q_lo[n, k * 64 : k * 64 + 64] for n in near], axis=0))
    d = d2 * r / CENTER
    z = d
    for t in range(3):
        s = stacked(d)
        r = r - forward(c_hi, c_lo, [gathered(s, c_tables[k]) for k in range(3)], PLAIN_ORDER)
        d = KEEP[t] * d + GAIN[t] * (d2 * r)
        z = z + d
    s = stacked(z)
    new = []
    for c in (1, 2):
        at = ((16 * c + ((lane128 & 63) >> 2)) >> 2) * 4 + (lane128 & 3)
        lift = forward(
            [pair(0, c, A1_ROWS, P1_ROWS)], [pair(1, c, A1_ROWS, P1_ROWS)], [gathered(s, one_hot(64, at))], PLAIN_ORDER
        )
        new.append(y[:, c * 64 : c * 64 + 64] + lift)
    y = jnp.concatenate([y[:, :64], new[0], new[1], y[:, 192:256], tail], axis=1)
    side = jnp.zeros((64, 64), F32)

    def at_centre(v):
        return jnp.concatenate([side, v, side, tail], axis=1)

    inv = inv[:, 64:192]
    r = rhs[:, 64:192] - jnp.concatenate(apply1(y, (1, 2)), axis=1)
    d = inv * r / CENTER
    y = y[:, 64:192] + d
    r = r - jnp.concatenate(apply1(at_centre(d), (1, 2)), axis=1)
    d = KEEP[0] * d + GAIN[0] * (inv * r)
    y = y + d
    r = r[:, 64:] - apply1(at_centre(d), (2,))[0]
    own = y[:, 64:] + KEEP[1] * d[:, 64:] + GAIN[1] * (inv[:, 64:] * r)
    pick_rows = (iota((8, 64), 1) == iota((8, 64), 0) + sub * 8).astype(F32).astype(BF16)
    hi, lo = split(own)
    o = mm(pick_rows, hi, NT) + mm(pick_rows, lo, NT)
    o = jnp.concatenate([jnp.concatenate([o[:2], o[4:6]], axis=1), jnp.concatenate([o[2:4], o[6:]], axis=1)], axis=1)
    return (jnp.broadcast_to(o[None], (TN_, 2, 256)),)


def level_cycle(place, parts, p0, m2, p2, crossed, swapped, far, unpack):
    return middle(place, parts, *middle_prep(place, p0, m2, p2, crossed, swapped, far), unpack)


def fine_up(owner_ref, all_ref, x_ref, hi_ref, lo_ref, out_ref, line):
    for n in range(32):
        e, i = n // R0, n % R0
        p, j = e * R0 + FINE_ORDER[i], owner_ref[i, e]
        v = all_ref[((j >> 8) * XN + ((j & 7) >> 1)) * TN_ + ((j >> 3) & (TN_ - 1))]
        v = jnp.concatenate([v[:, :128], v[:, 128:]], axis=0)
        line[p * 4 : p * 4 + 4, :] = jnp.where((j & 1) == 1, pltpu.roll(v, 64, 1), v)
    w = line[:, :64].T
    hi, lo = split(w)
    hi, lo = hi.astype(F32), lo.astype(F32)
    rights = [
        spread(double(hi[:, e * 64 : e * 64 + 64]), double(lo[:, e * 64 : e * 64 + 64])) for e in range(2)
    ]
    x = x_ref[...] + forward([hi_ref[0], hi_ref[1]], [lo_ref[0], lo_ref[1]], rights, FINE_ORDER)
    out_ref[...] = double(x)


def fine_up_call(owner, gathered_rows, x, hi, lo):
    smem, vmem = pl.BlockSpec(memory_space=pltpu.SMEM), pl.BlockSpec(memory_space=pltpu.VMEM)
    return pl.pallas_call(
        fine_up,
        in_specs=[smem, vmem, vmem, vmem, vmem],
        out_specs=vmem,
        out_shape=jax.ShapeDtypeStruct((64, 128), F32),
        scratch_shapes=[pltpu.VMEM((128, 128), F32)],
        compiler_params=pltpu.CompilerParams(vmem_limit_bytes=32 << 20),
        name="fine_up",
    )(owner, gathered_rows, x, hi, lo)


XY = [[(y * TN_ + t) * XN + x for y in range(YN) for x in range(XN)] for t in range(TN_)]
ZC = [[y * TN_ + t for t in range(TN_)] for y in range(YN)]


def across(value):
    return lax.all_to_all(value, ("slab", "sub"), 0, 0, tiled=True, axis_index_groups=XY)


def along(value):
    return lax.all_to_all(value, "slab", 0, 0, tiled=True, axis_index_groups=ZC)


def shifted(value, axis, by):
    n = lax.axis_size(axis)
    return lax.ppermute(value, axis, [(i, i + by) for i in range(n) if 0 <= i + by < n])


def unpack_table(spot):
    lane = jnp.arange(384, dtype=I32)
    rel, row = lane // 32 - 4, (lane % 32) // 4
    x = (spot + rel) % XN
    part = ((rel >= 0) & (rel < 4)).astype(I32)
    idx = x * 64 + part * 32 + lane % 32
    keep = (rel <= 4) & ((rel < 4) | (row < 4)) & ((rel > -4) | (row >= 4))
    return jnp.where(keep, idx, -1).reshape(1, 384)


def body(
    right_side,
    warm_start,
    fine_blocks,
    fine_columns,
    fine_prolong,
    owner_rows,
    send_slots,
    receive_rows,
    middle_blocks,
    middle_columns,
    middle_prolong,
    coarse_blocks,
    coarse_columns,
):
    both = ("slab", "sub")
    slab = lax.axis_index("slab").astype(I32)
    sub = lax.axis_index("sub").astype(I32)
    device = (slab * XN + sub).reshape(1, 1)
    place = jnp.stack([slab, sub]).reshape(1, 2)

    blocks = fine_blocks.transpose(1, 0, 2)
    own, low, high = kern(
        payload, [((8, 4096), F32)] + [((4, 8, 4096), F32)] * 2, [warm_start, right_side, fine_columns, blocks], smem=(2,)
    )
    middle_columns, low, high = lax.optimization_barrier((middle_columns, low, high))
    left, right = shifted(high, both, 1), shifted(low, both, -1)

    (pack,) = kern(
        level_pack,
        [((PACK_ROWS, 128), F32)],
        [middle_blocks.transpose(1, 0, 2), middle_prolong, coarse_blocks.transpose(1, 0, 2), middle_columns, coarse_columns],
        smem=(3, 4),
    )
    m2, p2 = shifted(pack, "slab", 2), shifted(pack, "slab", -2)
    count = lax.axis_size("slab")

    def crossing(value, by):
        pairs = [(i, i + by if i % 2 == by % 2 else i - by) for i in range(count)]
        return lax.ppermute(value, "slab", [p for p in pairs if 0 <= p[1] < count])

    p_hi, p_lo = kern(prolong_parts, [((2, 512, 128), BF16)] * 2, [fine_prolong])

    sends = ((64, 128), F32)
    hi, lo, inverse, rhs, x1, send, idx = kern(
        fine_start,
        [((2, 3, 512, 128), BF16)] * 2 + [sends, sends, ((64, 64), F32), sends, ((3, 3, 128), I32)],
        [device, own, left, right, blocks],
        smem=(0,),
        own=range(1, 5),
    )
    left, right = shifted(send, both, 1), shifted(send, both, -1)
    left, right, pack = lax.optimization_barrier((left, right, pack))
    crossed = crossing(pack[:A2_AT], 3)
    far = crossing(pack[D1_AT : D1_AT + 64], 4)
    x3, dense = kern(
        fine_down,
        [((64, 64), F32), ((16, 40, 128), F32)],
        [device, x1, send, left, right, hi, lo, inverse, idx, owner_rows, send_slots, p_hi, p_lo],
        smem=(0, 9, 10),
    )

    dense, m2, p2 = lax.optimization_barrier((dense, m2, p2))
    (part,) = kern(line_windows, [((TN_, 32, 128), F32)], [place, across(dense)], smem=(0,))
    part, m2, p2, crossed, far, pack = lax.optimization_barrier((part, m2, p2, crossed, far, pack))
    twin = jnp.concatenate([pack, m2, p2, crossed[D1_AT : D1_AT + 64]], axis=0)
    twin = lax.ppermute(twin, "slab", [(i, i ^ 1) for i in range(count)])
    (part,) = kern(sum_all, [((XN * YN, 32, 128), F32)], [along(part)])
    part = across(part)

    (share,) = kern(
        level_cycle,
        [((TN_, 2, 256), F32)],
        [place, part, pack, m2, p2, crossed, twin, far, unpack_table(slab % TN_)],
        smem=(0,),
        own=range(2, 8),
    )
    line = along(share)
    every = across(jnp.broadcast_to(line[None], (XN * YN, TN_, 2, 256)))
    x = fine_up_call(owner_rows, every.reshape(XN * YN * TN_, 2, 256), x3, p_hi, p_lo)

    x1, send = kern(
        fine_middle,
        [((64, 64), F32), sends],
        [device, x, shifted(x, both, 1), shifted(x, both, -1), rhs, hi, lo, inverse, idx],
        smem=(0,),
    )
    return tuple(
        kern(
            fine_end,
            [((NRHS, 1024), F32)] * 2,
            [device, x1, send, shifted(send, both, 1), shifted(send, both, -1), hi, lo, inverse, idx],
            smem=(0,),
        )
    )


def solution(mesh):
    in_specs = (
        P(None, ("slab", "sub")),
        P(None, ("slab", "sub")),
        P(("slab", "sub"), None, None),
        P(("slab", "sub"), None),
        P(("slab", "sub"), None, None),
        P(("slab", "sub"), None),
        P(("slab", "sub"), None),
        P("slab", "sub", None, None),
        P("slab", None, None),
        P("slab", None),
        P("slab", None),
        P("slab", None, None),
        P("slab", None),
    )
    out_specs = (P(None, ("slab", "sub")), P(None, ("slab", "sub")))
    return jax.shard_map(body, mesh=mesh, in_specs=in_specs, out_specs=out_specs, check_vma=False)
```

```python
import jax
import jax.numpy as jnp
from jax import lax
from jax.experimental import pallas as pl
from jax.experimental.pallas import tpu as pltpu
from jax.sharding import PartitionSpec as P

F32 = jnp.float32
BF16 = jnp.bfloat16
I32 = jnp.int32
BS = 64
NRHS = 4
R0 = 16
R1 = 8
R2 = 2
XN = 4
YN = 4
TN_ = 32

CENTER = 0.5 * (2.2 + 0.3)
HALF = 0.5 * (2.2 - 0.3)
SCALED = CENTER / HALF
FACTORS = [1.0 / SCALED]
for _ in range(3):
    FACTORS.append(1.0 / (2.0 * SCALED - FACTORS[-1]))
KEEP = [FACTORS[t + 1] * FACTORS[t] for t in range(3)]
GAIN = [2.0 * FACTORS[t + 1] / HALF for t in range(3)]

NN = ((1,), (0,))
NT = ((1,), (1,))
TN = ((0,), (0,))

FINE_ORDER = [(i % 2) * 8 + i // 2 for i in range(R0)]
RIM_ORDER = FINE_ORDER[8:] + FINE_ORDER[:8]
PLAIN_ORDER = list(range(16))


def kern(body, outs, args, smem=(), own=(), own_outs=False):
    count = len(args)

    def kernel(*refs):
        ins = [r if i in smem else r[...] for i, r in enumerate(refs[:count])]
        for ref, value in zip(refs[count:], body(*ins)):
            ref[...] = value

    vmem = pl.BlockSpec(memory_space=pltpu.VMEM)
    specs = [
        pl.BlockSpec(memory_space=pltpu.SMEM) if i in smem else pl.BlockSpec() if i in own else vmem
        for i in range(count)
    ]
    return pl.pallas_call(
        kernel,
        in_specs=specs,
        out_specs=[pl.BlockSpec() if own_outs else vmem for _ in outs],
        out_shape=[jax.ShapeDtypeStruct(s, d) for s, d in outs],
        compiler_params=pltpu.CompilerParams(vmem_limit_bytes=32 << 20),
        name=body.__name__,
    )(*args)


def mm(a, b, dims):
    return lax.dot_general(a, b, (dims, ((), ())), preferred_element_type=F32)


def iota(shape, dim):
    return lax.broadcasted_iota(I32, shape, dim)


def split(v):
    hi = v.astype(BF16)
    return hi, (v - hi.astype(F32)).astype(BF16)


def stacked(v):
    hi, lo = split(v)
    return jnp.concatenate([hi, lo], axis=0)


def one_hot(size, idx):
    return (iota((size, idx.shape[1]), 0) == idx).astype(F32).astype(BF16)


def lanes_in(x):
    lane = iota(x.shape, 1)
    place = lane & 63
    return jnp.take_along_axis(x, (lane & 64) + 2 * (place & 31) + (place >> 5), axis=1)


def lanes_out(x):
    lane = iota(x.shape, 1)
    b = lane & 63
    return jnp.take_along_axis(x, (lane & 64) + (b & 1) * 32 + (b >> 1), axis=1)


def tiles(raw):
    return lanes_in(raw.reshape(raw.shape[0] * 32, 128))


def double(g):
    return jnp.concatenate([g, g], axis=1)


def spread(hi, lo):
    low = iota(hi.shape, 1) < 64
    zero = jnp.zeros_like(hi)
    top = jnp.concatenate([jnp.where(low, hi, zero), jnp.where(low, lo, zero)], axis=1)
    bottom = jnp.concatenate([jnp.where(low, zero, hi), jnp.where(low, zero, lo)], axis=1)
    return jnp.concatenate([top, bottom], axis=0).astype(BF16)


def gathered(x, table):
    g = mm(x, table, NN)
    return spread(g[:64], g[64:])


def pick(t, order):
    lane = iota((32, 128), 1)
    place = (lane & 63) >> 2
    y = jnp.zeros((32, 128), F32)
    for i in range(16):
        y = y + jnp.where(place == order[i], t[i * 32 : i * 32 + 32], 0.0)
    return jnp.concatenate([y[:, :64], y[:, 64:]], axis=0)


def forward(his, los, rights, order):
    hi = jnp.concatenate(his, axis=1) if len(his) > 1 else his[0]
    lo = jnp.concatenate(los, axis=1) if len(los) > 1 else los[0]
    right = jnp.concatenate(rights, axis=0) if len(rights) > 1 else rights[0]
    a = mm(hi, right, NN)
    return pick(a[:, :128] + a[:, 128:] + mm(lo, right[:, :128], NN), order)


def diagonal(m, order):
    sub = iota(m.shape, 0) & 31
    lane = iota(m.shape, 1)
    kept = jnp.where((lane == sub) | (lane == sub + 96), m, 0.0)
    ones = ((iota((128, 128), 0) >> 6) == (iota((128, 128), 1) >> 6)).astype(F32).astype(BF16)
    hi, lo = split(kept)
    return pick(mm(hi, ones, NN) + mm(lo, ones, NN), order)


def columns_of(rows):
    z = lanes_in(jnp.concatenate([rows[:, m * 128 : m * 128 + 128] for m in range(8)], axis=0))
    t = z.T
    return jnp.concatenate([t[:64], t[64:]], axis=1)


def rows_of(v):
    t = lanes_out(jnp.concatenate([v[:, :32], v[:, 32:]], axis=0).T)
    return jnp.concatenate([t[m * 4 : m * 4 + 4] for m in range(8)], axis=1)


def rim(left, right):
    lane = iota(left.shape, 1)
    return jnp.where((((lane & 63) >> 2) & 7) < 4, right, left)


def fine_tables(device, own, left, right):
    wide, near = [], []
    for k in range(3):
        g = own[k : k + 1]
        r = rim(left[k : k + 1], right[k : k + 1])
        base = (device - 1) * 64
        wide.append([one_hot(192, g - base), one_hot(192, r - base)])
        near.append(one_hot(128, (g & 63) + jnp.where((g >> 6) == device, 0, 64)))
    return wide, near


def fine_both(hi, lo, x, wide):
    return jnp.concatenate(
        [
            forward(
                [hi[c, k] for k in range(3)],
                [lo[c, k] for k in range(3)],
                [gathered(x, wide[k][c]) for k in range(3)],
                (FINE_ORDER, RIM_ORDER)[c],
            )
            for c in range(2)
        ],
        axis=1,
    )


def fine_own(hi, lo, x, near):
    return forward(
        [hi[0, k] for k in range(3)],
        [lo[0, k] for k in range(3)],
        [gathered(x, near[k]) for k in range(3)],
        FINE_ORDER,
    )


def first_passes(device, x, sides, rhs, hi, lo, inverse, idx):
    wide, near = fine_tables(device, *idx)
    window = stacked(jnp.concatenate([sides[0], x, sides[1]], axis=1))
    r = rhs - fine_both(hi, lo, window, wide)
    d = inverse * r / CENTER
    r1 = r[:, :64] - fine_own(hi, lo, stacked(d), near)
    d1 = d[:, :64]
    d2 = KEEP[0] * d1 + GAIN[0] * (inverse[:, :64] * r1)
    return x + d1, jnp.concatenate([d2, r1], axis=1)


def last_passes(device, x, own, left, right, hi, lo, inverse, idx):
    wide, near = fine_tables(device, *idx)
    window = stacked(jnp.concatenate([left[:, :64], own[:, :64], right[:, :64]], axis=1))
    rims = rim(jnp.concatenate([left[:, 64:]] * 2, axis=1), jnp.concatenate([right[:, 64:]] * 2, axis=1))
    rim_d = rim(double(left[:, :64]), double(right[:, :64]))
    r = jnp.concatenate([own[:, 64:], rims[:, :64]], axis=1) - fine_both(hi, lo, window, wide)
    d_old = jnp.concatenate([own[:, :64], rim_d[:, :64]], axis=1)
    d = KEEP[1] * d_old + GAIN[1] * (inverse * r)
    residual = r[:, :64] - fine_own(hi, lo, stacked(d), near)
    return x + own[:, :64] + d[:, :64], residual


def indices(payload):
    return payload[:3, 1024:1152].astype(I32)


def fine_start(device, own, left_all, right_all, own_blocks):
    parts = []
    for k in range(3):
        parts.append(tiles(own_blocks[k]))
    for k in range(3):
        parts.append(jnp.concatenate([tiles(left_all[k]), tiles(right_all[k])], axis=0))
    entries = jnp.concatenate([diagonal(parts[0], FINE_ORDER), diagonal(parts[3], RIM_ORDER)], axis=1)
    inverse = jnp.where(entries == 0.0, 0.0, 1.0 / entries)
    pairs = [split(p) for p in parts]
    hi = jnp.stack([p[0] for p in pairs]).reshape(2, 3, 512, 128)
    lo = jnp.stack([p[1] for p in pairs]).reshape(2, 3, 512, 128)
    left, right = left_all[3], right_all[3]
    x = [columns_of(p[:4, :1024]) for p in (left, own, right)]
    b = [columns_of(p[4:, :1024]) for p in (left, own, right)]
    rhs = jnp.concatenate([b[1], rim(b[0], b[2])], axis=1)
    idx = [indices(p) for p in (own, left, right)]
    x1, send = first_passes(device[0, 0], x[1], (x[0], x[2]), rhs, hi, lo, inverse, idx)
    return hi, lo, inverse, rhs, x1, send, jnp.stack(idx)


def lanes_of(values, first=0):
    lane = iota((1, 128), 1)
    v = jnp.zeros((1, 128), I32)
    for n, value in enumerate(values):
        v = jnp.where((lane >> 2) == first + n, value * NRHS + (lane & 3), v)
    return v


def repeated(v, width):
    shift = width
    while shift < 128:
        v = v + pltpu.roll(v, shift, 1)
        shift *= 2
    return v


def payload(x, b, columns, blocks):
    lines = []
    for k in range(3):
        values = [None] * R0
        for i in range(R0):
            g = columns[i, k]
            values[FINE_ORDER[i]] = (g >> 4) * 16 + (g & 1) * 8 + ((g & 15) >> 1)
        lines.append(repeated(lanes_of(values), 64))
    v = jnp.concatenate(lines + [jnp.zeros((5, 128), I32)], axis=0).astype(F32)
    v = jnp.concatenate([jnp.concatenate([x, b], axis=0), v, jnp.zeros((8, 2944), F32)], axis=1)[None]
    return [v[0]] + [jnp.concatenate([part, v], axis=0) for part in (blocks[:, :8], blocks[:, 8:])]


def restrict(dest, residual, p_hi, p_lo):
    both = jnp.concatenate([residual[:32], residual[32:]], axis=1)
    place = (iota((32, 128), 1) & 63) >> 2
    hi, lo = split(both)
    hi, lo = hi.astype(F32), lo.astype(F32)
    r_hi = jnp.concatenate([jnp.where(place == FINE_ORDER[i], hi, 0.0) for i in range(16)], axis=0).astype(BF16)
    r_lo = jnp.concatenate([jnp.where(place == FINE_ORDER[i], lo, 0.0) for i in range(16)], axis=0).astype(BF16)
    pieces = []
    for e in range(2):
        u = mm(p_hi[e], r_hi, TN) + mm(p_hi[e], r_lo, TN) + mm(p_lo[e], r_hi, TN)
        pieces.append(u[:64, :64] + u[64:, 64:])
    hi, lo = split(jnp.concatenate(pieces, axis=1))
    rows = jnp.broadcast_to(dest[1:2].astype(F32), (16, 128)).astype(BF16)
    x = jnp.concatenate([hi, lo, rows], axis=0)
    out = []
    for q in range(0, XN * YN, 2):
        table = (iota((128, 128), 0) + q * 64 == dest[:1]).astype(F32).astype(BF16)
        g = mm(x, table, NT)
        v, at = g[:64] + g[64:128], g[128:136]
        out.append(jnp.concatenate([jnp.concatenate([v[:32, :64], v[32:, :64]], axis=1), at], axis=0))
        at = jnp.concatenate([at[:, 64:], at[:, :64]], axis=1)
        out.append(jnp.concatenate([jnp.concatenate([v[:32, 64:], v[32:, 64:]], axis=1), at], axis=0))
    return jnp.stack(out)


def fine_down(device, x, own, left, right, hi, lo, inverse, idx, owner, slot, p_hi, p_lo):
    spots, lines = [None] * 32, [None] * 32
    for e in range(2):
        for i in range(R0):
            j, at = owner[i, e], e * R0 + FINE_ORDER[i]
            t = (j >> 3) & (TN_ - 1)
            spots[at] = ((j >> 8) * XN + (t & (XN - 1))) * 16 + (t >> 2) * 2 + slot[i, e]
            lines[at] = (t >> 2) * 8 + (j & 7)
    dest = jnp.concatenate([lanes_of(spots), lanes_of(lines) + 1], axis=0)
    solution, residual = last_passes(
        device[0, 0], x, own, left, right, hi, lo, inverse, [idx[i] for i in range(3)]
    )
    return solution, restrict(dest, residual, p_hi, p_lo)


def fine_middle(device, x, left, right, rhs, hi, lo, inverse, idx):
    sides = (left[:, :64], right[:, :64])
    x1, send = first_passes(
        device[0, 0], x[:, :64], sides, rhs, hi, lo, inverse, [idx[i] for i in range(3)]
    )
    return x1, send


def fine_end(device, x, own, left, right, hi, lo, inverse, idx):
    solution, residual = last_passes(
        device[0, 0], x, own, left, right, hi, lo, inverse, [idx[i] for i in range(3)]
    )
    return rows_of(solution), rows_of(residual)


def prolong_parts(blocks):
    parts = [split(tiles(blocks[:, e, :])) for e in range(2)]
    return jnp.stack([p[0] for p in parts]), jnp.stack([p[1] for p in parts])


def line_windows(place, parts):
    sub = place[0, 1]
    total = jnp.zeros((128, 256), F32)
    for q in range(0, XN * YN, 2):
        v = jnp.concatenate(
            [jnp.concatenate([parts[q + i, :32, :64], parts[q + i, :32, 64:]], axis=0) for i in range(2)], axis=1
        )
        at = jnp.concatenate([parts[q + i, 32:33, :64] for i in range(2)], axis=1).astype(I32)
        table = (iota((256, 128), 0) + 1 == at).astype(F32).astype(BF16)
        total = total + mm(stacked(v), table, NT)
    x = stacked(total[:64] + total[64:])
    lane = iota((1, 128), 1)
    out = []
    for t in range(0, TN_, 2):
        spot = t + (lane >> 6)
        source = (spot + offset(lane, (sub - spot) & 3)) & (TN_ - 1)
        g = mm(x, one_hot(256, (source >> 2) * 32 + (lane & 31)), NN)
        g = g[:64] + g[64:]
        out += [jnp.concatenate([v[:32], v[32:]], axis=1) for v in (g[:, :64], g[:, 64:])]
    return (jnp.stack(out),)


def offset(lane, ahead):
    rel = jnp.where((lane & 32) == 0, ahead - 4, ahead)
    return jnp.where(((lane & 32) == 0) & (ahead == 0) & ((lane & 31) < 16), 4, rel)


def sum_all(parts):
    return (jnp.broadcast_to(jnp.sum(parts, axis=0)[None], (XN * YN, 32, 128)),)


A1_ROWS = 3 * R1 * 32
P1_ROWS = R1 * 32
A2_ROWS = 3 * R2 * 32
D1_AT = A1_ROWS + P1_ROWS
D2_AT = D1_AT + 64
IX_AT = D2_AT + 64
A2_AT = IX_AT + 8
PACK_ROWS = A2_AT + A2_ROWS


def level_pack(blocks, prolong, coarse, columns, coarse_columns):
    lines = [repeated(lanes_of([columns[i, k] for i in range(R1)]), 32) for k in range(3)]
    lines += [repeated(lanes_of([coarse_columns[i, k] for i in range(R2)]), 8) for k in range(3)]
    idx = jnp.concatenate(lines + [jnp.zeros((2, 128), I32)], axis=0).astype(F32)
    a1 = [tiles(blocks[k]) for k in range(3)]
    a2 = [lanes_in(coarse[k].reshape(R2 * 32, 128)) for k in range(3)]
    pad = jnp.zeros((256, 128), F32)
    d1 = 1.0 / diagonal_plain(jnp.concatenate([a1[0], pad], axis=0))[:, :32]
    pad = jnp.zeros((448, 128), F32)
    d2 = 1.0 / diagonal_plain(jnp.concatenate([a2[0], pad], axis=0))[:, :8]
    full = (
        jnp.concatenate(
            a1
            + [tiles(prolong)]
            + [jnp.concatenate([d1] * 4, axis=1), jnp.concatenate([d2] * 16, axis=1), idx]
            + a2,
            axis=0,
        ),
    )[0]
    return full, full[:A2_AT]


def diagonal_plain(m):
    return diagonal(m, PLAIN_ORDER)


STARTS = [0, 0, 0, 128]


def middle_prep(place, p0, m2, p2, crossed, swapped, far):
    slab = place[0, 0]
    even = (slab & 1) == 0
    top = A2_AT
    twin, twin_m2, twin_p2 = (swapped[i * PACK_ROWS : (i + 1) * PACK_ROWS] for i in range(3))
    far_twin = swapped[3 * PACK_ROWS :]
    far_low = jnp.where(even, far, far_twin)
    far_high = jnp.where(even, far_twin, far)
    m3 = jnp.where(even, crossed, twin_m2[:top])
    p3 = jnp.where(even, twin_p2[:top], crossed)
    m1 = jnp.where(even, twin_m2, twin)
    p1 = jnp.where(even, twin, twin_p2)
    packs = [m3, m2, m1, p0, p1, p2, p3]
    lane128 = iota((1, 128), 1)
    quarter = iota((64, 128), 1) >> 5
    tiled = [far_low] + [p[D1_AT : D1_AT + 64] for p in packs] + [far_high]
    d1 = []
    for q in range(3):
        v = jnp.zeros((64, 128), F32)
        for m in range(4):
            if q * 4 + m < 9:
                v = jnp.where(quarter == m, tiled[q * 4 + m], v)
        d1.append(v)
    d1 = jnp.concatenate(d1, axis=1)
    eighth = (iota((64, 128), 1) >> 3) & 7
    d2 = jnp.zeros((64, 128), F32)
    for m in range(7):
        d2 = jnp.where(eighth == m + 1, packs[m][D2_AT : D2_AT + 64], d2)
    d2 = d2[:, :64]
    ix = [p[IX_AT : IX_AT + 8].astype(I32) for p in packs]
    base = (slab - 4) * R1 * NRHS
    tables = []
    for c in range(4):
        for k in range(3):
            one = ix[2 * c - 1][k : k + 1] - base if c > 0 else jnp.full((1, 128), -1, I32)
            two = ix[2 * c][k : k + 1] - base
            at = jnp.where(((lane128 >> 5) & 1) == 0, one, two)
            tables.append(one_hot(256, at - STARTS[c]))
    c_tables = []
    c_base = (slab - 4) * R2 * NRHS
    group = (lane128 >> 3) & 7
    for k in range(3):
        at = jnp.full((1, 128), -1, I32)
        for m in range(1, 6):
            at = jnp.where(group == m + 1, ix[m][3 + k : 4 + k] - c_base, at)
        c_tables.append(one_hot(64, at))
    halves = [split(p[:D1_AT]) for p in packs]
    coarse = [split(p[A2_AT:]) for p in packs[1:6]]
    return (
        jnp.stack([h[0] for h in halves]),
        jnp.stack([h[1] for h in halves]),
        jnp.stack([h[0] for h in coarse]),
        jnp.stack([h[1] for h in coarse]),
        d1,
        d2,
        jnp.stack(tables),
        jnp.stack(c_tables),
    )


def middle(place, parts, b_hi, b_lo, q_hi, q_lo, d1, d2, tables, c_tables, unpack):
    slab, sub = place[0, 0], place[0, 1]
    blocks = (b_hi, b_lo)
    lane128 = iota((1, 128), 1)
    pieces = []
    for x in range(XN):
        spot = slab & (TN_ - 1)
        at = spot + offset(lane128, (x - spot) & 3)
        row = (slab >> 5) + jnp.where(at < 0, -1, jnp.where(at >= TN_, 1, 0))
        row = jnp.broadcast_to(row, (32, 128))
        w = jnp.zeros((32, 128), F32)
        for y in range(YN):
            w = jnp.where(row == y, parts[y * XN + x], w)
        pieces.append(jnp.concatenate([w[:, :64], w[:, 64:]], axis=0))
    g = mm(stacked(jnp.concatenate(pieces, axis=1)), one_hot(256, unpack), NN)
    rhs = g[:64] + g[64:]
    def rows(part, m, start, count):
        return blocks[part][max(m, 0), start : start + count]

    def pair(part, c, start, count):
        return jnp.concatenate(
            [rows(part, 2 * c - 1, start, count), rows(part, 2 * c, start, count)], axis=0
        )

    a_hi = [[pair(0, c, k * 256, 256) for k in range(3)] for c in range(4)]
    a_lo = [[pair(1, c, k * 256, 256) for k in range(3)] for c in range(4)]

    def apply1(v, chunks):
        x = stacked(v)
        return [
            forward(
                a_hi[c], a_lo[c], [gathered(x[:, STARTS[c] : STARTS[c] + 256], tables[3 * c + k]) for k in range(3)], PLAIN_ORDER
            )
            for c in chunks
        ]

    tail = jnp.zeros((64, 128), F32)
    inv = d1[:, :256]
    d = d1 * rhs / CENTER
    y = d[:, :256]
    r = rhs[:, :256] - jnp.concatenate(apply1(d, range(4)), axis=1)
    for t in range(2):
        step = KEEP[t] * d[:, :256] + GAIN[t] * (inv * r)
        d = jnp.concatenate([step, tail], axis=1)
        y = y + step
        r = r - jnp.concatenate(apply1(d, range(4)), axis=1)
    x = stacked(r)
    low = iota((32, 128), 1) < 64
    q_lane = (iota((32, 128), 1) & 63) >> 2
    first = (lane128 & 63) >> 2
    r_hi, r_lo = [], []
    for kk in range(4):
        g = mm(x, one_hot(256, first * 16 + kk * 4 + (lane128 & 3)), NN)
        r_hi.append(jnp.where(low, g[:32], g[32:64]))
        r_lo.append(jnp.where(low, g[64:96], g[96:128]))
    u = jnp.zeros((128, 128), F32)
    for m in range(7):
        keep = [q_lane == 2 * (m + 1) + j // 4 for j in range(R1)]
        b_hi = jnp.concatenate([jnp.where(keep[j], r_hi[j % 4], 0.0) for j in range(R1)], axis=0).astype(BF16)
        b_lo = jnp.concatenate([jnp.where(keep[j], r_lo[j % 4], 0.0) for j in range(R1)], axis=0).astype(BF16)
        p_hi, p_lo = rows(0, m, A1_ROWS, P1_ROWS), rows(1, m, A1_ROWS, P1_ROWS)
        u = u + mm(p_hi, b_hi, TN) + mm(p_hi, b_lo, TN) + mm(p_lo, b_hi, TN)
    r = u[:64, :64] + u[64:, 64:]
    c_hi, c_lo = [], []
    for k in range(3):
        near = [min(max(m - 2, 0), 4) for m in range(8)]
        c_hi.append(jnp.concatenate([q_hi[n, k * 64 : k * 64 + 64] for n in near], axis=0))
        c_lo.append(jnp.concatenate([q_lo[n, k * 64 : k * 64 + 64] for n in near], axis=0))
    d = d2 * r / CENTER
    z = d
    for t in range(3):
        s = stacked(d)
        r = r - forward(c_hi, c_lo, [gathered(s, c_tables[k]) for k in range(3)], PLAIN_ORDER)
        d = KEEP[t] * d + GAIN[t] * (d2 * r)
        z = z + d
    s = stacked(z)
    new = []
    for c in (1, 2):
        at = ((16 * c + ((lane128 & 63) >> 2)) >> 2) * 4 + (lane128 & 3)
        lift = forward(
            [pair(0, c, A1_ROWS, P1_ROWS)], [pair(1, c, A1_ROWS, P1_ROWS)], [gathered(s, one_hot(64, at))], PLAIN_ORDER
        )
        new.append(y[:, c * 64 : c * 64 + 64] + lift)
    y = jnp.concatenate([y[:, :64], new[0], new[1], y[:, 192:256], tail], axis=1)
    side = jnp.zeros((64, 64), F32)

    def at_centre(v):
        return jnp.concatenate([side, v, side, tail], axis=1)

    inv = inv[:, 64:192]
    r = rhs[:, 64:192] - jnp.concatenate(apply1(y, (1, 2)), axis=1)
    d = inv * r / CENTER
    y = y[:, 64:192] + d
    r = r - jnp.concatenate(apply1(at_centre(d), (1, 2)), axis=1)
    d = KEEP[0] * d + GAIN[0] * (inv * r)
    y = y + d
    r = r[:, 64:] - apply1(at_centre(d), (2,))[0]
    own = y[:, 64:] + KEEP[1] * d[:, 64:] + GAIN[1] * (inv[:, 64:] * r)
    pick_rows = (iota((8, 64), 1) == iota((8, 64), 0) + sub * 8).astype(F32).astype(BF16)
    hi, lo = split(own)
    o = mm(pick_rows, hi, NT) + mm(pick_rows, lo, NT)
    o = jnp.concatenate([jnp.concatenate([o[:2], o[4:6]], axis=1), jnp.concatenate([o[2:4], o[6:]], axis=1)], axis=1)
    return (jnp.broadcast_to(o[None], (TN_, 2, 256)),)


def level_cycle(place, parts, p0, m2, p2, crossed, swapped, far, unpack):
    return middle(place, parts, *middle_prep(place, p0, m2, p2, crossed, swapped, far), unpack)


def fine_up(owner_ref, all_ref, x_ref, hi_ref, lo_ref, out_ref, line):
    for n in range(32):
        e, i = n // R0, n % R0
        p, j = e * R0 + FINE_ORDER[i], owner_ref[i, e]
        v = all_ref[((j >> 8) * XN + ((j & 7) >> 1)) * TN_ + ((j >> 3) & (TN_ - 1))]
        v = jnp.concatenate([v[:, :128], v[:, 128:]], axis=0)
        line[p * 4 : p * 4 + 4, :] = jnp.where((j & 1) == 1, pltpu.roll(v, 64, 1), v)
    w = line[:, :64].T
    hi, lo = split(w)
    hi, lo = hi.astype(F32), lo.astype(F32)
    rights = [
        spread(double(hi[:, e * 64 : e * 64 + 64]), double(lo[:, e * 64 : e * 64 + 64])) for e in range(2)
    ]
    x = x_ref[...] + forward([hi_ref[0], hi_ref[1]], [lo_ref[0], lo_ref[1]], rights, FINE_ORDER)
    out_ref[...] = double(x)


def fine_up_call(owner, gathered_rows, x, hi, lo):
    smem, vmem = pl.BlockSpec(memory_space=pltpu.SMEM), pl.BlockSpec(memory_space=pltpu.VMEM)
    return pl.pallas_call(
        fine_up,
        in_specs=[smem, vmem, vmem, vmem, vmem],
        out_specs=vmem,
        out_shape=jax.ShapeDtypeStruct((64, 128), F32),
        scratch_shapes=[pltpu.VMEM((128, 128), F32)],
        compiler_params=pltpu.CompilerParams(vmem_limit_bytes=32 << 20),
        name="fine_up",
    )(owner, gathered_rows, x, hi, lo)


XY = [[(y * TN_ + t) * XN + x for y in range(YN) for x in range(XN)] for t in range(TN_)]
ZC = [[y * TN_ + t for t in range(TN_)] for y in range(YN)]


def across(value):
    return lax.all_to_all(value, ("slab", "sub"), 0, 0, tiled=True, axis_index_groups=XY)


def along(value):
    return lax.all_to_all(value, "slab", 0, 0, tiled=True, axis_index_groups=ZC)


def shifted(value, axis, by):
    n = lax.axis_size(axis)
    return lax.ppermute(value, axis, [(i, i + by) for i in range(n) if 0 <= i + by < n])


def unpack_table(spot):
    lane = jnp.arange(384, dtype=I32)
    rel, row = lane // 32 - 4, (lane % 32) // 4
    x = (spot + rel) % XN
    part = ((rel >= 0) & (rel < 4)).astype(I32)
    idx = x * 64 + part * 32 + lane % 32
    keep = (rel <= 4) & ((rel < 4) | (row < 4)) & ((rel > -4) | (row >= 4))
    return jnp.where(keep, idx, -1).reshape(1, 384)


def body(
    right_side,
    warm_start,
    fine_blocks,
    fine_columns,
    fine_prolong,
    owner_rows,
    send_slots,
    receive_rows,
    middle_blocks,
    middle_columns,
    middle_prolong,
    coarse_blocks,
    coarse_columns,
):
    both = ("slab", "sub")
    slab = lax.axis_index("slab").astype(I32)
    sub = lax.axis_index("sub").astype(I32)
    device = (slab * XN + sub).reshape(1, 1)
    place = jnp.stack([slab, sub]).reshape(1, 2)

    blocks = fine_blocks.transpose(1, 0, 2)
    own, low, high = kern(
        payload, [((8, 4096), F32)] + [((4, 8, 4096), F32)] * 2, [warm_start, right_side, fine_columns, blocks], smem=(2,)
    )
    middle_columns, low, high = lax.optimization_barrier((middle_columns, low, high))
    left, right = shifted(high, both, 1), shifted(low, both, -1)

    pack, short = kern(
        level_pack,
        [((PACK_ROWS, 128), F32), ((A2_AT, 128), F32)],
        [middle_blocks.transpose(1, 0, 2), middle_prolong, coarse_blocks.transpose(1, 0, 2), middle_columns, coarse_columns],
        smem=(3, 4),
    )
    m2, p2 = shifted(pack, "slab", 2), shifted(pack, "slab", -2)
    count = lax.axis_size("slab")

    def crossing(value, by):
        pairs = [(i, i + by if i % 2 == by % 2 else i - by) for i in range(count)]
        return lax.ppermute(value, "slab", [p for p in pairs if 0 <= p[1] < count])

    p_hi, p_lo = kern(prolong_parts, [((2, 512, 128), BF16)] * 2, [fine_prolong])

    sends = ((64, 128), F32)
    hi, lo, inverse, rhs, x1, send, idx = kern(
        fine_start,
        [((2, 3, 512, 128), BF16)] * 2 + [sends, sends, ((64, 64), F32), sends, ((3, 3, 128), I32)],
        [device, own, left, right, blocks],
        smem=(0,),
        own=range(1, 5),
    )
    left, right = shifted(send, both, 1), shifted(send, both, -1)
    left, right, pack, short = lax.optimization_barrier((left, right, pack, short))
    crossed = crossing(short, 3)
    far = crossing(pack[D1_AT : D1_AT + 64], 4)
    x3, dense = kern(
        fine_down,
        [((64, 64), F32), ((16, 40, 128), F32)],
        [device, x1, send, left, right, hi, lo, inverse, idx, owner_rows, send_slots, p_hi, p_lo],
        smem=(0, 9, 10),
    )

    dense, m2, p2 = lax.optimization_barrier((dense, m2, p2))
    (part,) = kern(line_windows, [((TN_, 32, 128), F32)], [place, across(dense)], smem=(0,))
    part, m2, p2, crossed, far, pack = lax.optimization_barrier((part, m2, p2, crossed, far, pack))
    twin = jnp.concatenate([pack, m2, p2, crossed[D1_AT : D1_AT + 64]], axis=0)
    twin = lax.ppermute(twin, "slab", [(i, i ^ 1) for i in range(count)])
    (part,) = kern(sum_all, [((XN * YN, 32, 128), F32)], [along(part)])
    part = across(part)

    (share,) = kern(
        level_cycle,
        [((TN_, 2, 256), F32)],
        [place, part, pack, m2, p2, crossed, twin, far, unpack_table(slab % TN_)],
        smem=(0,),
        own=range(2, 8),
    )
    line = along(share)
    every = across(jnp.broadcast_to(line[None], (XN * YN, TN_, 2, 256)))
    x = fine_up_call(owner_rows, every.reshape(XN * YN * TN_, 2, 256), x3, p_hi, p_lo)

    x1, send = kern(
        fine_middle,
        [((64, 64), F32), sends],
        [device, x, shifted(x, both, 1), shifted(x, both, -1), rhs, hi, lo, inverse, idx],
        smem=(0,),
    )
    return tuple(
        kern(
            fine_end,
            [((NRHS, 1024), F32)] * 2,
            [device, x1, send, shifted(send, both, 1), shifted(send, both, -1), hi, lo, inverse, idx],
            smem=(0,),
        )
    )


def solution(mesh):
    in_specs = (
        P(None, ("slab", "sub")),
        P(None, ("slab", "sub")),
        P(("slab", "sub"), None, None),
        P(("slab", "sub"), None),
        P(("slab", "sub"), None, None),
        P(("slab", "sub"), None),
        P(("slab", "sub"), None),
        P("slab", "sub", None, None),
        P("slab", None, None),
        P("slab", None),
        P("slab", None),
        P("slab", None, None),
        P("slab", None),
    )
    out_specs = (P(None, ("slab", "sub")), P(None, ("slab", "sub")))
    return jax.shard_map(body, mesh=mesh, in_specs=in_specs, out_specs=out_specs, check_vma=False)
```
